512 devices in a mesh: section: 8 (over y_hi, core), dp: 64 (over y_lo, z, x).
Axes of the slice: x: 4, y: 8 (y_hi: 4, y_lo: 2; y = y_hi * 2 + y_lo), z: 8, core: 2. Of those that a mesh axis runs over, the one named last changes fastest.
Arguments:
- token_ids: int32 [8192], P('dp'), may hold values from 0 to 65535
- embed_table: bfloat16 [65536, 8192], P('section', 'dp'), may hold values from -6 to 6
- norm_gain: float32 [8192], replicated, may hold values from 0.1 to 1.9
- cotangent: bfloat16 [8192, 8192], P('dp', 'section'), may hold values from -6 to 6
Outputs:
- grad_table: bfloat16 [65536, 8192], P('section', 'dp')
- input_grad: bfloat16 [8192, 8192], P('dp', 'section')
The draws below stay inside these ranges and needn't reach their ends.
All inputs are finite; a program needn't handle non-finite values.
Results may differ from the reference program's by a relative error of at most 0.0044.
Values may be sent and summed in bfloat16 or wider, within the bound.
No kernel may reach another device: no remote copies, remote signals or barrier semaphores. Data moves between devices by JAX's collectives and lax.ppermute only.
A program may use at most 64 MiB of HBM per device.

```python
import math
import jax
import jax.numpy as jnp
import numpy as np
from jax import lax

D = 8192
VOCAB = 65536
TOKENS = 8192


def with_ends(array, own_key, least, top_value):
    spot = [jax.random.randint(jax.random.fold_in(own_key, axis), (), 0, length) for axis, length in enumerate(array.shape)]
    widest = array.shape.index(max(array.shape))
    beside = spot[:widest] + [(spot[widest] + 1) % array.shape[widest]] + spot[widest + 1:]
    return array.at[tuple(spot)].set(least).at[tuple(beside)].set(top_value)


def shard_levels(key, extent, shards, smallest, top_value):
    gain = 1.0
    for position, blocks in shards:
        heights = jax.random.uniform(jax.random.fold_in(jax.random.fold_in(key, 6), position), (blocks,), jnp.float32, smallest / len(shards), top_value / len(shards))
        gain = gain * jnp.repeat(jnp.exp(heights), extent[position] // blocks).reshape((-1,) + (1,) * (len(extent) - 1 - position))
    return gain


def rank_table(amount, lean):
    portions = [(1 << 20) // math.isqrt(grade ** lean) + 1 for grade in range(1, amount + 1)]
    deviation = 1 + sum(portions) // (1 << 30)
    return np.cumsum(np.array([max(1, weight // deviation) for weight in portions]))


def ranked(rng, extent, count, slope):
    listing = rank_table(count, slope)
    pick = jax.random.randint(jax.random.fold_in(rng, 1), extent, 0, int(listing[count - 1]))
    rank = jnp.searchsorted(jnp.asarray(listing, jnp.int32), pick, side="right")
    return jax.random.permutation(jax.random.fold_in(rng, 2), count)[rank].astype(jnp.int32)


def centred(rng, dims, scale, most, shards=(), dtype=jnp.bfloat16):
    level = shard_levels(rng, dims, shards, -0.22, 0.18) if shards else 1.0
    array = jax.random.normal(rng, dims, jnp.float32) * scale * level
    return jnp.minimum(jnp.maximum(array, -most), most).astype(dtype)


def setup_inputs(seed: int = 0) -> dict:
    arg_keys = jax.random.split(jax.random.key(seed), 5)
    token_ids = with_ends(ranked(arg_keys[0], (TOKENS,), VOCAB, 2), jax.random.fold_in(arg_keys[0], 3), 0, VOCAB - 1).astype(jnp.int32)
    embed_table = centred(arg_keys[1], (VOCAB, D), 1.0, 6.0, ((0, 8), (1, 64)))
    norm_gain = jnp.clip(1.0 + 0.18 * jax.random.normal(arg_keys[2], (D,), jnp.float32), 0.1, 1.9)
    cotangent = centred(arg_keys[3], (TOKENS, D), 1.0, 6.0, ((0, 64), (1, 8)))
    return {"token_ids": token_ids, "embed_table": embed_table, "norm_gain": norm_gain, "cotangent": cotangent}


epsilon = 1e-05

def reference(token_ids, embed_table, norm_gain, cotangent):
    gathered = embed_table[token_ids].astype(jnp.float32)
    square_mean = lax.optimization_barrier(jnp.mean(gathered * gathered, axis=1, keepdims=True))
    inverse = lax.rsqrt(square_mean + epsilon)
    scaled = cotangent.astype(jnp.float32) * norm_gain.astype(jnp.float32)[None, :]
    inner = lax.optimization_barrier(jnp.mean(scaled * gathered, axis=1, keepdims=True))
    input_grad = (inverse * scaled - gathered * inverse * inverse * inverse * inner).astype(jnp.bfloat16)
    step_width = min(D, 1024)
    pieces = []
    for column in range(0, D, step_width):
        values = input_grad[:, column:column + step_width].astype(jnp.float32)
        summed = jnp.zeros((VOCAB, step_width), jnp.float32).at[token_ids].add(values)
        pieces.append(summed.astype(jnp.bfloat16))
    return (jnp.concatenate(pieces, axis=1), input_grad)
```

```python
import functools

import jax
import jax.numpy as jnp
from jax import lax
from jax.experimental import pallas as pl
from jax.experimental.pallas import tpu as pltpu
from jax.sharding import PartitionSpec as P

epsilon = 1e-05
SLOTS = 48
LANES = 128


def whole(shape, space=pltpu.VMEM):
    return pl.BlockSpec(shape, lambda *_: (0,) * len(shape), memory_space=space)


def plan_kernel(section_ref, ids_ref, index_ref, count_ref, *, slots, vocab_section):
    ids = ids_ref[...].astype(jnp.float32)
    ids = jnp.concatenate([ids, ids], axis=0)
    ids = ids.T.astype(jnp.int32)
    local = ids - section_ref[0] * vocab_section
    inside = (local >= 0) & (local < vocab_section)
    before = (
        lax.broadcasted_iota(jnp.int32, (LANES, LANES), 1)
        < lax.broadcasted_iota(jnp.int32, (LANES, LANES), 0)
    )
    ones = jnp.where(inside, 1.0, 0.0)
    rank = jnp.dot(
        jnp.where(before, 1.0, 0.0).astype(jnp.bfloat16),
        ones.astype(jnp.bfloat16),
        preferred_element_type=jnp.float32,
    ).astype(jnp.int32)
    rank = jnp.where(inside, rank, -1)
    for c in range(slots):
        index_ref[pl.ds(c, 1), :] = jnp.sum(jnp.where(rank == c, local, 0), axis=0, keepdims=True)
    count_ref[...] = jnp.broadcast_to(
        jnp.sum(ones, axis=0, keepdims=True).astype(jnp.int32), count_ref.shape
    )


def pick_kernel(index_ref, table_ref, rows_ref, wide_ref, picked_ref, *, slots, groups):
    step = 256

    def widen(i, carry):
        wide_ref[pl.ds(i * step, step), :] = table_ref[pl.ds(i * step, step), :].astype(jnp.float32)
        return carry

    lax.fori_loop(0, table_ref.shape[0] // step, widen, 0)

    def group(g, carry):
        for c in range(slots):
            picked_ref[pl.ds(c, 1), :] = wide_ref[pl.ds(index_ref[c, g], 1), :]
        rows_ref[g] = picked_ref[...].astype(jnp.bfloat16)
        return carry

    lax.fori_loop(0, groups, group, 0)


def slot_of(ids_row, slots, vocab_section):
    wide = jnp.broadcast_to(ids_row // vocab_section, (LANES, LANES))
    tall = wide.astype(jnp.float32).T.astype(jnp.int32)
    first = lax.broadcasted_iota(jnp.int32, (LANES, LANES), 0)
    second = lax.broadcasted_iota(jnp.int32, (LANES, LANES), 1)
    same = wide == tall
    as_row = jnp.sum(jnp.where(same & (first < second), 1, 0), axis=0, keepdims=True)
    as_column = jnp.sum(jnp.where(same & (second < first), 1.0, 0.0), axis=1, keepdims=True)
    row_slot = jnp.where(as_row < slots, wide[:1] * slots + as_row, -1)
    as_column = as_column.astype(jnp.int32)
    column_slot = jnp.where(as_column < slots, tall[:, :1] * slots + as_column, -1)
    return row_slot, column_slot


def deal_kernel(ids_ref, cotangent_ref, dealt_ref, *, slots, sections, vocab_section):
    row_slot, _ = slot_of(ids_ref[...], slots, vocab_section)
    cotangent = cotangent_ref[...]
    for s in range(sections):
        wanted = lax.broadcasted_iota(jnp.int32, (slots, LANES), 0) + s * slots == row_slot
        dealt_ref[s] = jnp.dot(
            jnp.where(wanted, 1.0, 0.0).astype(jnp.bfloat16),
            cotangent,
            preferred_element_type=jnp.float32,
        ).astype(jnp.bfloat16)


def collect_kernel(ids_ref, dealt_ref, own_ref, *, slots, sections, vocab_section):
    _, column_slot = slot_of(ids_ref[...], slots, vocab_section)
    total = jnp.zeros(own_ref.shape, jnp.float32)
    for s in range(sections):
        wanted = lax.broadcasted_iota(jnp.int32, (LANES, slots), 1) + s * slots == column_slot
        total = total + jnp.dot(
            jnp.where(wanted, 1.0, 0.0).astype(jnp.bfloat16),
            dealt_ref[s],
            preferred_element_type=jnp.float32,
        )
    own_ref[...] = total.astype(jnp.bfloat16)


def norm_kernel(rows_ref, cotangent_ref, gain_ref, by_column_ref, by_feature_ref):
    pieces, slots, columns = rows_ref.shape
    per = cotangent_ref.shape[2] // columns
    width = pieces * columns

    def parts(k, j):
        embedded = rows_ref[k * per + j].astype(jnp.float32)
        own = cotangent_ref[k, :, j * columns : (j + 1) * columns].astype(jnp.float32)
        return embedded, own * gain_ref[pl.ds(k * per + j, 1), :]

    def sums(k, carry):
        squares, inners = carry
        for j in range(per):
            embedded, scaled = parts(k, j)
            squares = squares + embedded * embedded
            inners = inners + scaled * embedded
        return squares, inners

    zeros = jnp.zeros((slots, columns), jnp.float32)
    squares, inners = lax.fori_loop(0, pieces // per, sums, (zeros, zeros))
    square_mean = jnp.sum(squares, axis=1, keepdims=True) * (1.0 / width)
    inner = jnp.sum(inners, axis=1, keepdims=True) * (1.0 / width)
    inverse = lax.rsqrt(square_mean + epsilon)
    pull = inverse * inverse * inverse * inner

    def grads(k, carry):
        for j in range(per):
            embedded, scaled = parts(k, j)
            grad = (inverse * scaled - embedded * pull).astype(jnp.bfloat16)
            by_column_ref[k * per + j] = grad
            by_feature_ref[k, :, j * columns : (j + 1) * columns] = grad
        return carry

    lax.fori_loop(0, pieces // per, grads, 0)


def add_kernel(index_ref, count_ref, grads_ref, table_ref, total_ref, wide_ref, *, groups):
    step = 256
    slots = grads_ref.shape[1]

    def clear(i, carry):
        total_ref[pl.ds(i * step, step), :] = jnp.zeros((step, LANES), jnp.float32)
        return carry

    lax.fori_loop(0, total_ref.shape[0] // step, clear, 0)

    def group(g, carry):
        wide_ref[...] = grads_ref[g].astype(jnp.float32)

        def one(c, carry):
            row = pl.ds(index_ref[c, g], 1)
            total_ref[row, :] = total_ref[row, :] + wide_ref[pl.ds(c, 1), :]
            return carry

        lax.fori_loop(0, jnp.minimum(count_ref[0, g], slots), one, 0)
        return carry

    lax.fori_loop(0, groups, group, 0)

    def narrow(i, carry):
        table_ref[pl.ds(i * step, step), :] = total_ref[pl.ds(i * step, step), :].astype(jnp.bfloat16)
        return carry

    lax.fori_loop(0, total_ref.shape[0] // step, narrow, 0)


def call(kernel, operands, spaces, outs, scratch=()):
    return pl.pallas_call(
        kernel,
        in_specs=[whole(o.shape, s) for o, s in zip(operands, spaces)],
        out_specs=[whole(o.shape) for o in outs],
        out_shape=outs,
        scratch_shapes=list(scratch),
    )(*operands)


def passage(slots, section, all_ids, own_ids, embed_table, norm_gain, cotangent):
    vocab_section, columns = embed_table.shape
    groups = all_ids.shape[0]
    tokens, features = cotangent.shape
    sections = lax.axis_size("section")
    V, S = pltpu.VMEM, pltpu.SMEM
    bf16 = functools.partial(jax.ShapeDtypeStruct, dtype=jnp.bfloat16)
    i32 = functools.partial(jax.ShapeDtypeStruct, dtype=jnp.int32)
    (dealt,) = call(
        functools.partial(deal_kernel, slots=slots, sections=sections, vocab_section=vocab_section),
        (own_ids, cotangent), (V, V), [bf16((sections, slots, features))],
    )
    their_cotangent = lax.all_to_all(dealt, "section", 0, 0, tiled=True)
    index, count = call(
        functools.partial(plan_kernel, slots=slots, vocab_section=vocab_section),
        (section, all_ids), (S, V), [i32((slots, LANES)), i32((8, LANES))],
    )
    (rows,) = call(
        functools.partial(pick_kernel, slots=slots, groups=groups),
        (index, embed_table), (S, V), [bf16((groups, slots, columns))],
        [pltpu.VMEM((vocab_section, columns), jnp.float32), pltpu.VMEM((slots, columns), jnp.float32)],
    )
    full_rows = lax.all_to_all(rows, "dp", 0, 0, tiled=True)
    gain = norm_gain.reshape(groups, columns)
    by_column, by_feature = call(
        norm_kernel, (full_rows, their_cotangent, gain), (V, V, V),
        [bf16(full_rows.shape), bf16(their_cotangent.shape)],
    )
    back = lax.all_to_all(by_column, "dp", 0, 0, tiled=True)
    home = lax.all_to_all(by_feature, "section", 0, 0, tiled=True)
    (grad_table,) = call(
        functools.partial(add_kernel, groups=groups),
        (index, count, back), (S, S, V), [bf16((vocab_section, columns))],
        [pltpu.VMEM((vocab_section, columns), jnp.float32), pltpu.VMEM((slots, columns), jnp.float32)],
    )
    (own_grad,) = call(
        functools.partial(collect_kernel, slots=slots, sections=sections, vocab_section=vocab_section),
        (own_ids, home), (V, V), [bf16((tokens, features))],
    )
    return grad_table, own_grad


def on_device(token_ids, embed_table, norm_gain, cotangent):
    vocab_section = embed_table.shape[0]
    groups = lax.axis_size("dp")
    tokens = token_ids.shape[0]
    section = lax.axis_index("section").reshape(1)
    own_ids = token_ids.reshape(1, tokens)
    all_ids = lax.all_to_all(
        jnp.broadcast_to(own_ids[None], (groups, 1, tokens)), "dp", 0, 0, tiled=True
    ).reshape(groups, tokens)
    sections = jnp.arange(lax.axis_size("section"))
    counts = jnp.sum(all_ids[:, :, None] // vocab_section == sections, axis=1)
    fits = jnp.max(counts) <= SLOTS
    return lax.cond(
        fits,
        functools.partial(passage, SLOTS),
        functools.partial(passage, tokens),
        section, all_ids, own_ids, embed_table, norm_gain, cotangent,
    )


def solution(mesh):
    return jax.shard_map(
        on_device,
        mesh=mesh,
        in_specs=(P("dp"), P("section", "dp"), P(), P("dp", "section")),
        out_specs=(P("section", "dp"), P("dp", "section")),
        check_vma=False,
    )
```

```python
import functools

import jax
import jax.numpy as jnp
from jax import lax
from jax.experimental import pallas as pl
from jax.experimental.pallas import tpu as pltpu
from jax.sharding import PartitionSpec as P

epsilon = 1e-05
SLOTS = 48
LANES = 128


def whole(shape, space=pltpu.VMEM):
    return pl.BlockSpec(shape, lambda *_: (0,) * len(shape), memory_space=space)


def plan_kernel(section_ref, ids_ref, index_ref, count_ref, *, slots, vocab_section):
    ids = ids_ref[...].astype(jnp.float32)
    ids = jnp.concatenate([ids, ids], axis=0)
    ids = ids.T.astype(jnp.int32)
    local = ids - section_ref[0] * vocab_section
    inside = (local >= 0) & (local < vocab_section)
    before = (
        lax.broadcasted_iota(jnp.int32, (LANES, LANES), 1)
        < lax.broadcasted_iota(jnp.int32, (LANES, LANES), 0)
    )
    ones = jnp.where(inside, 1.0, 0.0)
    rank = jnp.dot(
        jnp.where(before, 1.0, 0.0).astype(jnp.bfloat16),
        ones.astype(jnp.bfloat16),
        preferred_element_type=jnp.float32,
    ).astype(jnp.int32)
    rank = jnp.where(inside, rank, -1)
    for c in range(slots):
        index_ref[pl.ds(c, 1), :] = jnp.sum(jnp.where(rank == c, local, 0), axis=0, keepdims=True)
    count_ref[...] = jnp.broadcast_to(
        jnp.sum(ones, axis=0, keepdims=True).astype(jnp.int32), count_ref.shape
    )


def pick_kernel(index_ref, table_ref, rows_ref, wide_ref, picked_ref, *, slots, groups):
    step = 256

    def widen(i, carry):
        wide_ref[pl.ds(i * step, step), :] = table_ref[pl.ds(i * step, step), :].astype(jnp.float32)
        return carry

    lax.fori_loop(0, table_ref.shape[0] // step, widen, 0)

    def group(g, carry):
        for c in range(slots):
            picked_ref[pl.ds(c, 1), :] = wide_ref[pl.ds(index_ref[c, g], 1), :]
        rows_ref[g] = picked_ref[...].astype(jnp.bfloat16)
        return carry

    lax.fori_loop(0, groups, group, 0)


def slot_of(ids_row, slots, vocab_section):
    wide = jnp.broadcast_to(ids_row // vocab_section, (LANES, LANES))
    tall = wide.astype(jnp.float32).T.astype(jnp.int32)
    first = lax.broadcasted_iota(jnp.int32, (LANES, LANES), 0)
    second = lax.broadcasted_iota(jnp.int32, (LANES, LANES), 1)
    same = wide == tall
    as_row = jnp.sum(jnp.where(same & (first < second), 1, 0), axis=0, keepdims=True)
    as_column = jnp.sum(jnp.where(same & (second < first), 1.0, 0.0), axis=1, keepdims=True)
    row_slot = jnp.where(as_row < slots, wide[:1] * slots + as_row, -1)
    as_column = as_column.astype(jnp.int32)
    column_slot = jnp.where(as_column < slots, tall[:, :1] * slots + as_column, -1)
    return row_slot, column_slot


def deal_kernel(ids_ref, cotangent_ref, dealt_ref, *, slots, sections, vocab_section):
    row_slot, _ = slot_of(ids_ref[...], slots, vocab_section)
    cotangent = cotangent_ref[...]
    for s in range(sections):
        wanted = lax.broadcasted_iota(jnp.int32, (slots, LANES), 0) + s * slots == row_slot
        dealt_ref[s] = jnp.dot(
            jnp.where(wanted, 1.0, 0.0).astype(jnp.bfloat16),
            cotangent,
            preferred_element_type=jnp.float32,
        ).astype(jnp.bfloat16)


def collect_kernel(ids_ref, dealt_ref, own_ref, *, slots, sections, vocab_section):
    _, column_slot = slot_of(ids_ref[...], slots, vocab_section)
    total = jnp.zeros(own_ref.shape, jnp.float32)
    for s in range(sections):
        wanted = lax.broadcasted_iota(jnp.int32, (LANES, slots), 1) + s * slots == column_slot
        total = total + jnp.dot(
            jnp.where(wanted, 1.0, 0.0).astype(jnp.bfloat16),
            dealt_ref[s],
            preferred_element_type=jnp.float32,
        )
    own_ref[...] = total.astype(jnp.bfloat16)


def own_slots(ids_row, section, slots, vocab_section):
    wide = jnp.broadcast_to(ids_row // vocab_section, (LANES, LANES))
    tall = wide.astype(jnp.float32).T.astype(jnp.int32)
    first = lax.broadcasted_iota(jnp.int32, (LANES, LANES), 0)
    second = lax.broadcasted_iota(jnp.int32, (LANES, LANES), 1)
    as_row = jnp.sum(jnp.where((tall == section) & (first < second), 1, 0), axis=0, keepdims=True)
    as_column = jnp.sum(jnp.where((wide == section) & (second < first), 1.0, 0.0), axis=1, keepdims=True)
    row_slot = jnp.where(wide[:1] == section, as_row, -1)
    column_slot = jnp.where(tall[:, :1] == section, as_column.astype(jnp.int32), -1)
    return row_slot, column_slot


def select_kernel(section_ref, ids_ref, cotangent_ref, own_ref, *, slots, vocab_section):
    row_slot, _ = own_slots(ids_ref[...], section_ref[0], slots, vocab_section)
    wanted = lax.broadcasted_iota(jnp.int32, (slots, LANES), 0) == row_slot
    wanted = jnp.where(wanted, 1.0, 0.0).astype(jnp.bfloat16)
    for s in range(cotangent_ref.shape[0]):
        own_ref[s] = jnp.dot(
            wanted, cotangent_ref[s], preferred_element_type=jnp.float32
        ).astype(jnp.bfloat16)


def norm_kernel(*refs, spread, vocab_section):
    if spread:
        section_ref, ids_ref, *refs = refs
    rows_ref, cotangent_ref, gain_ref, by_column_ref, by_feature_ref, *scratch = refs
    pieces, slots, columns = rows_ref.shape
    per = cotangent_ref.shape[2] // columns
    width = pieces * columns
    if spread:
        _, column_slot = own_slots(ids_ref[...], section_ref[0], slots, vocab_section)
        wanted = lax.broadcasted_iota(jnp.int32, (LANES, slots), 1) == column_slot
        wanted = jnp.where(wanted, 1.0, 0.0).astype(jnp.bfloat16)

    def parts(k, j):
        embedded = rows_ref[k * per + j].astype(jnp.float32)
        own = cotangent_ref[k, :, j * columns : (j + 1) * columns].astype(jnp.float32)
        return embedded, own * gain_ref[pl.ds(k * per + j, 1), :]

    def sums(k, carry):
        squares, inners = carry
        for j in range(per):
            embedded, scaled = parts(k, j)
            squares = squares + embedded * embedded
            inners = inners + scaled * embedded
        return squares, inners

    zeros = jnp.zeros((slots, columns), jnp.float32)
    squares, inners = lax.fori_loop(0, pieces // per, sums, (zeros, zeros))
    square_mean = jnp.sum(squares, axis=1, keepdims=True) * (1.0 / width)
    inner = jnp.sum(inners, axis=1, keepdims=True) * (1.0 / width)
    inverse = lax.rsqrt(square_mean + epsilon)
    pull = inverse * inverse * inverse * inner

    def grads(k, carry):
        for j in range(per):
            embedded, scaled = parts(k, j)
            grad = (inverse * scaled - embedded * pull).astype(jnp.bfloat16)
            by_column_ref[k * per + j] = grad
            if spread:
                scratch[0][:, j * columns : (j + 1) * columns] = grad
            else:
                by_feature_ref[k, :, j * columns : (j + 1) * columns] = grad
        if spread:
            by_feature_ref[k] = jnp.dot(
                wanted, scratch[0][...], preferred_element_type=jnp.float32
            ).astype(jnp.bfloat16)
        return carry

    lax.fori_loop(0, pieces // per, grads, 0)


def add_kernel(index_ref, count_ref, grads_ref, table_ref, total_ref, wide_ref, *, groups):
    step = 256
    slots = grads_ref.shape[1]

    def clear(i, carry):
        total_ref[pl.ds(i * step, step), :] = jnp.zeros((step, LANES), jnp.float32)
        return carry

    lax.fori_loop(0, total_ref.shape[0] // step, clear, 0)

    def group(g, carry):
        wide_ref[...] = grads_ref[g].astype(jnp.float32)

        def one(c, carry):
            row = pl.ds(index_ref[c, g], 1)
            total_ref[row, :] = total_ref[row, :] + wide_ref[pl.ds(c, 1), :]
            return carry

        lax.fori_loop(0, jnp.minimum(count_ref[0, g], slots), one, 0)
        return carry

    lax.fori_loop(0, groups, group, 0)

    def narrow(i, carry):
        table_ref[pl.ds(i * step, step), :] = total_ref[pl.ds(i * step, step), :].astype(jnp.bfloat16)
        return carry

    lax.fori_loop(0, total_ref.shape[0] // step, narrow, 0)


def call(kernel, operands, spaces, outs, scratch=()):
    return pl.pallas_call(
        kernel,
        in_specs=[whole(o.shape, s) for o, s in zip(operands, spaces)],
        out_specs=[whole(o.shape) for o in outs],
        out_shape=outs,
        scratch_shapes=list(scratch),
    )(*operands)


def passage(slots, section, all_ids, own_ids, embed_table, norm_gain, cotangent):
    vocab_section, columns = embed_table.shape
    groups = all_ids.shape[0]
    tokens, features = cotangent.shape
    sections = lax.axis_size("section")
    V, S = pltpu.VMEM, pltpu.SMEM
    bf16 = functools.partial(jax.ShapeDtypeStruct, dtype=jnp.bfloat16)
    i32 = functools.partial(jax.ShapeDtypeStruct, dtype=jnp.int32)
    (dealt,) = call(
        functools.partial(deal_kernel, slots=slots, sections=sections, vocab_section=vocab_section),
        (own_ids, cotangent), (V, V), [bf16((sections, slots, features))],
    )
    their_cotangent = lax.all_to_all(dealt, "section", 0, 0, tiled=True)
    index, count = call(
        functools.partial(plan_kernel, slots=slots, vocab_section=vocab_section),
        (section, all_ids), (S, V), [i32((slots, LANES)), i32((8, LANES))],
    )
    (rows,) = call(
        functools.partial(pick_kernel, slots=slots, groups=groups),
        (index, embed_table), (S, V), [bf16((groups, slots, columns))],
        [pltpu.VMEM((vocab_section, columns), jnp.float32), pltpu.VMEM((slots, columns), jnp.float32)],
    )
    full_rows = lax.all_to_all(rows, "dp", 0, 0, tiled=True)
    gain = norm_gain.reshape(groups, columns)
    by_column, by_feature = call(
        functools.partial(norm_kernel, spread=False, vocab_section=vocab_section),
        (full_rows, their_cotangent, gain), (V, V, V),
        [bf16(full_rows.shape), bf16(their_cotangent.shape)],
    )
    back = lax.all_to_all(by_column, "dp", 0, 0, tiled=True)
    home = lax.all_to_all(by_feature, "section", 0, 0, tiled=True)
    (grad_table,) = call(
        functools.partial(add_kernel, groups=groups),
        (index, count, back), (S, S, V), [bf16((vocab_section, columns))],
        [pltpu.VMEM((vocab_section, columns), jnp.float32), pltpu.VMEM((slots, columns), jnp.float32)],
    )
    (own_grad,) = call(
        functools.partial(collect_kernel, slots=slots, sections=sections, vocab_section=vocab_section),
        (own_ids, home), (V, V), [bf16((tokens, features))],
    )
    return grad_table, own_grad


def on_device(token_ids, embed_table, norm_gain, cotangent):
    vocab_section, columns = embed_table.shape
    groups = lax.axis_size("dp")
    sections = lax.axis_size("section")
    tokens, features = cotangent.shape
    V, S = pltpu.VMEM, pltpu.SMEM
    bf16 = functools.partial(jax.ShapeDtypeStruct, dtype=jnp.bfloat16)
    i32 = functools.partial(jax.ShapeDtypeStruct, dtype=jnp.int32)
    section = lax.axis_index("section").reshape(1)
    own_ids = token_ids.reshape(1, tokens)
    all_cotangent = lax.all_gather(cotangent, "section", axis=0)
    all_ids = lax.all_to_all(
        jnp.broadcast_to(own_ids[None], (groups, 1, tokens)), "dp", 0, 0, tiled=True
    ).reshape(groups, tokens)
    counts = jnp.sum(all_ids[:, :, None] // vocab_section == jnp.arange(sections), axis=1)
    fits = jnp.max(counts) <= SLOTS

    index, count = call(
        functools.partial(plan_kernel, slots=SLOTS, vocab_section=vocab_section),
        (section, all_ids), (S, V), [i32((SLOTS, LANES)), i32((8, LANES))],
    )
    (rows,) = call(
        functools.partial(pick_kernel, slots=SLOTS, groups=groups),
        (index, embed_table), (S, V), [bf16((groups, SLOTS, columns))],
        [pltpu.VMEM((vocab_section, columns), jnp.float32), pltpu.VMEM((SLOTS, columns), jnp.float32)],
    )
    full_rows = lax.all_to_all(rows, "dp", 0, 0, tiled=True)
    (slot_cotangent,) = call(
        functools.partial(select_kernel, slots=SLOTS, vocab_section=vocab_section),
        (section, own_ids, all_cotangent), (S, V, V), [bf16((sections, SLOTS, features))],
    )
    by_column, spread = call(
        functools.partial(norm_kernel, spread=True, vocab_section=vocab_section),
        (section, own_ids, full_rows, slot_cotangent, norm_gain.reshape(groups, columns)),
        (S, V, V, V, V),
        [bf16(full_rows.shape), bf16((sections, tokens, features))],
        [pltpu.VMEM((SLOTS, features), jnp.bfloat16)],
    )
    fast_grad = lax.psum_scatter(spread, "section", scatter_dimension=0, tiled=True)[0]
    back = lax.all_to_all(by_column, "dp", 0, 0, tiled=True)

    def fast(index, count, back, *_):
        (grad_table,) = call(
            functools.partial(add_kernel, groups=groups),
            (index, count, back), (S, S, V), [bf16((vocab_section, columns))],
            [pltpu.VMEM((vocab_section, columns), jnp.float32), pltpu.VMEM((SLOTS, columns), jnp.float32)],
        )
        return grad_table, jnp.zeros((tokens, features), jnp.bfloat16)

    def slow(index, count, back, *operands):
        return passage(tokens, *operands)

    grad_table, slow_grad = lax.cond(
        fits, fast, slow, index, count, back,
        section, all_ids, own_ids, embed_table, norm_gain, cotangent,
    )
    return grad_table, jnp.where(fits, fast_grad, slow_grad)


def solution(mesh):
    return jax.shard_map(
        on_device,
        mesh=mesh,
        in_specs=(P("dp"), P("section", "dp"), P(), P("dp", "section")),
        out_specs=(P("section", "dp"), P("dp", "section")),
        check_vma=False,
    )
```

```python
import functools
import math

import jax
import jax.numpy as jnp
from jax import lax
from jax.experimental import pallas as pl
from jax.experimental.pallas import tpu as pltpu
from jax.sharding import Mesh
from jax.sharding import PartitionSpec as P

epsilon = 1e-05
TOKEN_SLOTS = 48
ROW_SLOTS = 32
CHUNK = 8
REPEATED = 1 << 16
CHIPS = "section_0"
CORES = "section_1"
SECTION = (CHIPS, CORES)
LANES = 128


def whole(shape, space=pltpu.VMEM):
    return pl.BlockSpec(shape, lambda *_: (0,) * len(shape), memory_space=space)


def plan_kernel(section_ref, ids_ref, index_ref, count_ref, *, slots, vocab_section):
    ids = ids_ref[...].astype(jnp.float32)
    ids = jnp.concatenate([ids, ids], axis=0)
    ids = ids.T.astype(jnp.int32)
    local = ids - section_ref[0] * vocab_section
    inside = (local >= 0) & (local < vocab_section)
    before = (
        lax.broadcasted_iota(jnp.int32, (LANES, LANES), 1)
        < lax.broadcasted_iota(jnp.int32, (LANES, LANES), 0)
    )
    ones = jnp.where(inside, 1.0, 0.0)
    rank = jnp.dot(
        jnp.where(before, 1.0, 0.0).astype(jnp.bfloat16),
        ones.astype(jnp.bfloat16),
        preferred_element_type=jnp.float32,
    ).astype(jnp.int32)
    rank = jnp.where(inside, rank, -1)
    for c in range(slots):
        index_ref[pl.ds(c, 1), :] = jnp.sum(jnp.where(rank == c, local, 0), axis=0, keepdims=True)
    count_ref[...] = jnp.broadcast_to(
        jnp.sum(ones, axis=0, keepdims=True).astype(jnp.int32), count_ref.shape
    )


def pick_kernel(index_ref, table_ref, rows_ref, wide_ref, picked_ref, *, slots, groups):
    step = 256

    def widen(i, carry):
        wide_ref[pl.ds(i * step, step), :] = table_ref[pl.ds(i * step, step), :].astype(jnp.float32)
        return carry

    lax.fori_loop(0, table_ref.shape[0] // step, widen, 0)

    def group(g, carry):
        for c in range(slots):
            picked_ref[pl.ds(c, 1), :] = wide_ref[pl.ds(index_ref[c, g], 1), :]
        rows_ref[g] = picked_ref[...].astype(jnp.bfloat16)
        return carry

    lax.fori_loop(0, groups, group, 0)


def slot_of(ids_row, slots, vocab_section):
    wide = jnp.broadcast_to(ids_row // vocab_section, (LANES, LANES))
    tall = wide.astype(jnp.float32).T.astype(jnp.int32)
    first = lax.broadcasted_iota(jnp.int32, (LANES, LANES), 0)
    second = lax.broadcasted_iota(jnp.int32, (LANES, LANES), 1)
    same = wide == tall
    as_row = jnp.sum(jnp.where(same & (first < second), 1, 0), axis=0, keepdims=True)
    as_column = jnp.sum(jnp.where(same & (second < first), 1.0, 0.0), axis=1, keepdims=True)
    row_slot = jnp.where(as_row < slots, wide[:1] * slots + as_row, -1)
    as_column = as_column.astype(jnp.int32)
    column_slot = jnp.where(as_column < slots, tall[:, :1] * slots + as_column, -1)
    return row_slot, column_slot


def deal_kernel(ids_ref, cotangent_ref, dealt_ref, *, slots, sections, vocab_section):
    row_slot, _ = slot_of(ids_ref[...], slots, vocab_section)
    cotangent = cotangent_ref[...]
    for s in range(sections):
        wanted = lax.broadcasted_iota(jnp.int32, (slots, LANES), 0) + s * slots == row_slot
        dealt_ref[s] = jnp.dot(
            jnp.where(wanted, 1.0, 0.0).astype(jnp.bfloat16),
            cotangent,
            preferred_element_type=jnp.float32,
        ).astype(jnp.bfloat16)


def collect_kernel(ids_ref, dealt_ref, own_ref, *, slots, sections, vocab_section):
    _, column_slot = slot_of(ids_ref[...], slots, vocab_section)
    total = jnp.zeros(own_ref.shape, jnp.float32)
    for s in range(sections):
        wanted = lax.broadcasted_iota(jnp.int32, (LANES, slots), 1) + s * slots == column_slot
        total = total + jnp.dot(
            jnp.where(wanted, 1.0, 0.0).astype(jnp.bfloat16),
            dealt_ref[s],
            preferred_element_type=jnp.float32,
        )
    own_ref[...] = total.astype(jnp.bfloat16)


def norm_kernel(rows_ref, cotangent_ref, gain_ref, by_column_ref, by_feature_ref):
    pieces, slots, columns = rows_ref.shape
    per = cotangent_ref.shape[2] // columns
    width = pieces * columns

    def parts(k, j):
        embedded = rows_ref[k * per + j].astype(jnp.float32)
        own = cotangent_ref[k, :, j * columns : (j + 1) * columns].astype(jnp.float32)
        return embedded, own * gain_ref[pl.ds(k * per + j, 1), :]

    def sums(k, carry):
        squares, inners = carry
        for j in range(per):
            embedded, scaled = parts(k, j)
            squares = squares + embedded * embedded
            inners = inners + scaled * embedded
        return squares, inners

    zeros = jnp.zeros((slots, columns), jnp.float32)
    squares, inners = lax.fori_loop(0, pieces // per, sums, (zeros, zeros))
    square_mean = jnp.sum(squares, axis=1, keepdims=True) * (1.0 / width)
    inner = jnp.sum(inners, axis=1, keepdims=True) * (1.0 / width)
    inverse = lax.rsqrt(square_mean + epsilon)
    pull = inverse * inverse * inverse * inner

    def grads(k, carry):
        for j in range(per):
            embedded, scaled = parts(k, j)
            grad = (inverse * scaled - embedded * pull).astype(jnp.bfloat16)
            by_column_ref[k * per + j] = grad
            by_feature_ref[k, :, j * columns : (j + 1) * columns] = grad
        return carry

    lax.fori_loop(0, pieces // per, grads, 0)


def add_kernel(index_ref, count_ref, grads_ref, table_ref, total_ref, wide_ref, *, groups):
    step = 256
    slots = grads_ref.shape[1]

    def clear(i, carry):
        total_ref[pl.ds(i * step, step), :] = jnp.zeros((step, LANES), jnp.float32)
        return carry

    lax.fori_loop(0, total_ref.shape[0] // step, clear, 0)

    def group(g, carry):
        wide_ref[...] = grads_ref[g].astype(jnp.float32)

        def one(c, carry):
            row = pl.ds(index_ref[c, g], 1)
            total_ref[row, :] = total_ref[row, :] + wide_ref[pl.ds(c, 1), :]
            return carry

        lax.fori_loop(0, jnp.minimum(count_ref[0, g], slots), one, 0)
        return carry

    lax.fori_loop(0, groups, group, 0)

    def narrow(i, carry):
        table_ref[pl.ds(i * step, step), :] = total_ref[pl.ds(i * step, step), :].astype(jnp.bfloat16)
        return carry

    lax.fori_loop(0, total_ref.shape[0] // step, narrow, 0)


def call(kernel, operands, spaces, outs, scratch=()):
    held = sum(math.prod(a.shape) * a.dtype.itemsize for a in (*operands, *outs, *scratch))
    return pl.pallas_call(
        kernel,
        in_specs=[whole(o.shape, s) for o, s in zip(operands, spaces)],
        out_specs=[whole(o.shape) for o in outs],
        out_shape=outs,
        scratch_shapes=list(scratch),
        compiler_params=pltpu.CompilerParams(vmem_limit_bytes=2 * held + (6 << 20)),
    )(*operands)


def passage(slots, section, all_ids, own_ids, embed_table, norm_gain, cotangent):
    vocab_section, columns = embed_table.shape
    groups = all_ids.shape[0]
    tokens, features = cotangent.shape
    sections = lax.axis_size(SECTION)
    V, S = pltpu.VMEM, pltpu.SMEM
    bf16 = functools.partial(jax.ShapeDtypeStruct, dtype=jnp.bfloat16)
    i32 = functools.partial(jax.ShapeDtypeStruct, dtype=jnp.int32)
    (dealt,) = call(
        functools.partial(deal_kernel, slots=slots, sections=sections, vocab_section=vocab_section),
        (own_ids, cotangent), (V, V), [bf16((sections, slots, features))],
    )
    their_cotangent = lax.all_to_all(dealt, SECTION, 0, 0, tiled=True)
    index, count = call(
        functools.partial(plan_kernel, slots=slots, vocab_section=vocab_section),
        (section, all_ids), (S, V), [i32((slots, LANES)), i32((8, LANES))],
    )
    (rows,) = call(
        functools.partial(pick_kernel, slots=slots, groups=groups),
        (index, embed_table), (S, V), [bf16((groups, slots, columns))],
        [pltpu.VMEM((vocab_section, columns), jnp.float32), pltpu.VMEM((slots, columns), jnp.float32)],
    )
    full_rows = lax.all_to_all(rows, "dp", 0, 0, tiled=True)
    gain = norm_gain.reshape(groups, columns)
    by_column, by_feature = call(
        norm_kernel, (full_rows, their_cotangent, gain), (V, V, V),
        [bf16(full_rows.shape), bf16(their_cotangent.shape)],
    )
    back = lax.all_to_all(by_column, "dp", 0, 0, tiled=True)
    home = lax.all_to_all(by_feature, SECTION, 0, 0, tiled=True)
    (grad_table,) = call(
        functools.partial(add_kernel, groups=groups),
        (index, count, back), (S, S, V), [bf16((vocab_section, columns))],
        [pltpu.VMEM((vocab_section, columns), jnp.float32), pltpu.VMEM((slots, columns), jnp.float32)],
    )
    (own_grad,) = call(
        functools.partial(collect_kernel, slots=slots, sections=sections, vocab_section=vocab_section),
        (own_ids, home), (V, V), [bf16((tokens, features))],
    )
    return grad_table, own_grad


def row_plan_kernel(section_ref, ids_ref, index_ref, count_ref, *, vocab_section):
    slots = index_ref.shape[0]
    ids = ids_ref[...].astype(jnp.float32)
    ids = jnp.concatenate([ids, ids], axis=0)
    ids = ids.T.astype(jnp.int32)
    local = ids - section_ref[0] * vocab_section
    inside = (local >= 0) & (local < vocab_section) & (ids < REPEATED)
    before = (
        lax.broadcasted_iota(jnp.int32, (LANES, LANES), 1)
        < lax.broadcasted_iota(jnp.int32, (LANES, LANES), 0)
    )
    ones = jnp.where(inside, 1.0, 0.0)
    rank = jnp.dot(
        jnp.where(before, 1.0, 0.0).astype(jnp.bfloat16),
        ones.astype(jnp.bfloat16),
        preferred_element_type=jnp.float32,
    ).astype(jnp.int32)
    rank = jnp.where(inside, rank, -1)
    short = local - vocab_section
    for c in range(slots):
        index_ref[pl.ds(c, 1), :] = vocab_section + jnp.sum(
            jnp.where(rank == c, short, 0), axis=0, keepdims=True
        )
    count = jnp.minimum(jnp.sum(ones, axis=0, keepdims=True).astype(jnp.int32), slots)
    count_ref[...] = jnp.broadcast_to((count + (CHUNK - 1)) // CHUNK, count_ref.shape)


def row_pick_kernel(index_ref, count_ref, table_ref, rows_ref, wide_ref, picked_ref):
    groups, slots, columns = rows_ref.shape
    entries = table_ref.shape[0]
    step = 512
    picked_ref[...] = jnp.zeros(picked_ref.shape, jnp.float32)
    wide_ref[pl.ds(entries, CHUNK), :] = jnp.zeros((CHUNK, columns), jnp.float32)

    def widen(i, carry):
        wide_ref[pl.ds(i * step, step), :] = table_ref[pl.ds(i * step, step), :].astype(jnp.float32)
        return carry

    lax.fori_loop(0, entries // step, widen, 0)

    def group(g, carry):
        def chunk(i, carry):
            for j in range(CHUNK):
                c = i * CHUNK + j
                picked_ref[pl.ds(c, 1), :] = wide_ref[pl.ds(index_ref[c, g], 1), :]
            return carry

        lax.fori_loop(0, count_ref[0, g], chunk, 0)
        rows_ref[g] = picked_ref[...].astype(jnp.bfloat16)
        return carry

    lax.fori_loop(0, groups, group, 0)


def row_add_kernel(index_ref, count_ref, grads_ref, table_ref, total_ref, wide_ref):
    groups, slots, columns = grads_ref.shape
    entries = table_ref.shape[0]
    step = 512

    def clear(i, carry):
        total_ref[pl.ds(i * step, step), :] = jnp.zeros((step, columns), jnp.float32)
        return carry

    lax.fori_loop(0, entries // step, clear, 0)
    total_ref[pl.ds(entries, CHUNK), :] = jnp.zeros((CHUNK, columns), jnp.float32)

    def group(g, carry):
        wide_ref[...] = grads_ref[g].astype(jnp.float32)

        def chunk(i, carry):
            rows = [pl.ds(index_ref[i * CHUNK + j, g], 1) for j in range(CHUNK)]
            sums = [
                total_ref[row, :] + wide_ref[pl.ds(i * CHUNK + j, 1), :]
                for j, row in enumerate(rows)
            ]
            for row, value in zip(rows, sums):
                total_ref[row, :] = value
            return carry

        lax.fori_loop(0, count_ref[0, g], chunk, 0)
        return carry

    lax.fori_loop(0, groups, group, 0)

    def narrow(i, carry):
        table_ref[pl.ds(i * step, step), :] = total_ref[pl.ds(i * step, step), :].astype(jnp.bfloat16)
        return carry

    lax.fori_loop(0, entries // step, narrow, 0)


def both_ways(ids_row):
    wide = jnp.broadcast_to(ids_row, (LANES, LANES))
    tall = wide.astype(jnp.float32).T.astype(jnp.int32)
    down = lax.broadcasted_iota(jnp.int32, (LANES, LANES), 0)
    along = lax.broadcasted_iota(jnp.int32, (LANES, LANES), 1)
    return wide, tall, down < along, along < down


def mark_kernel(ids_ref, marked_ref):
    wide, tall, row_first, _ = both_ways(ids_ref[...])
    repeated = jnp.max(jnp.where((wide == tall) & row_first, REPEATED, 0), axis=0, keepdims=True)
    marked_ref[...] = jnp.broadcast_to((wide[:1] + repeated)[None], marked_ref.shape)


def one_hot(condition):
    return jnp.where(condition, 1.0, 0.0).astype(jnp.bfloat16)


def select_kernel(section_ref, ids_ref, cotangent_ref, own_ref, expand_ref, combine_ref, *, vocab_section):
    token_slots, row_slots = expand_ref.shape
    wide, tall, row_first, column_first = both_ways(ids_ref[...])
    section = section_ref[0]
    wide_in = wide // vocab_section == section
    tall_in = tall // vocab_section == section
    same = wide == tall
    wide_repeat = jnp.max(jnp.where(same & row_first, 1, 0), axis=0, keepdims=True)
    tall_repeat = jnp.max(jnp.where(same & column_first, 1.0, 0.0), axis=1, keepdims=True)
    wide_new = wide_in & (jnp.broadcast_to(wide_repeat, (LANES, LANES)) == 0)
    tall_new = tall_in & (jnp.broadcast_to(tall_repeat, (LANES, LANES)) == 0.0)
    rank = jnp.sum(jnp.where(tall_in & row_first, 1, 0), axis=0, keepdims=True)
    rank = jnp.where(wide_in[:1], rank, -1)
    own = one_hot(lax.broadcasted_iota(jnp.int32, (token_slots, LANES), 0) == rank)
    tall_place = jnp.sum(jnp.where(wide_new & column_first, 1.0, 0.0), axis=1, keepdims=True)
    place = jnp.sum(
        jnp.where(same & tall_new, jnp.broadcast_to(tall_place, (LANES, LANES)), 0.0), axis=0, keepdims=True
    ).astype(jnp.int32)
    place = jnp.where(wide_in[:1], place, -1)
    rows = one_hot(lax.broadcasted_iota(jnp.int32, (row_slots, LANES), 0) == place)
    over_tokens = (((1,), (1,)), ((), ()))
    expand_ref[...] = lax.dot_general(
        own, rows, over_tokens, preferred_element_type=jnp.float32
    ).astype(jnp.bfloat16)
    combine_ref[...] = lax.dot_general(
        rows, own, over_tokens, preferred_element_type=jnp.float32
    ).astype(jnp.bfloat16)
    for s in range(cotangent_ref.shape[0]):
        own_ref[s] = jnp.dot(
            own, cotangent_ref[s], preferred_element_type=jnp.float32
        ).astype(jnp.bfloat16)


def grad_kernel(
    section_ref, rows_ref, cotangent_ref, gain_ref, expand_ref, combine_ref,
    by_column_ref, keep_ref, give_ref, embedded_ref,
):
    pieces, _, columns = rows_ref.shape
    sections, slots, features = cotangent_ref.shape
    per = features // columns
    width = pieces * columns
    expand = expand_ref[...]
    combine = combine_ref[...]

    def sums(k, carry):
        squares, inners = carry
        rows = jnp.concatenate([rows_ref[k * per + j] for j in range(per)], axis=1)
        embedded = jnp.dot(expand, rows, preferred_element_type=jnp.float32)
        embedded_ref[k] = embedded
        scaled = cotangent_ref[k].astype(jnp.float32) * gain_ref[pl.ds(k, 1), :]
        square = embedded * embedded
        inner = scaled * embedded
        for j in range(per):
            squares = squares + square[:, j * columns : (j + 1) * columns]
            inners = inners + inner[:, j * columns : (j + 1) * columns]
        return squares, inners

    zeros = jnp.zeros((slots, columns), jnp.float32)
    squares, inners = lax.fori_loop(0, sections, sums, (zeros, zeros))
    square_mean = jnp.sum(squares, axis=1, keepdims=True) * (1.0 / width)
    inner = jnp.sum(inners, axis=1, keepdims=True) * (1.0 / width)
    inverse = lax.rsqrt(square_mean + epsilon)
    pull = inverse * inverse * inverse * inner
    core = section_ref[0] % 2

    def grads(k, out_ref, place):
        scaled = cotangent_ref[k].astype(jnp.float32) * gain_ref[pl.ds(k, 1), :]
        grad = (inverse * scaled - embedded_ref[k] * pull).astype(jnp.bfloat16)
        out_ref[place] = grad
        added = jnp.dot(combine, grad, preferred_element_type=jnp.float32).astype(jnp.bfloat16)
        for j in range(per):
            by_column_ref[k * per + j] = added[:, j * columns : (j + 1) * columns]

    def chip(h, carry):
        grads(2 * h + core, keep_ref, h)
        grads(2 * h + 1 - core, give_ref, h)
        return carry

    lax.fori_loop(0, sections // 2, chip, 0)


def spread_kernel(section_ref, ids_ref, kept_ref, given_ref, spread_ref, *, vocab_section):
    slots = kept_ref.shape[1]
    wide, tall, _, column_first = both_ways(ids_ref[...])
    wide = wide // vocab_section
    tall = tall // vocab_section
    along = lax.broadcasted_iota(jnp.int32, (LANES, slots), 1)

    def of(section):
        rank = jnp.sum(jnp.where((wide == section) & column_first, 1.0, 0.0), axis=1, keepdims=True)
        rank = jnp.where(tall[:, :1] == section, rank.astype(jnp.int32), -1)
        return one_hot(along == rank)

    section = section_ref[0]
    mine = of(section)
    theirs = of(section + 1 - 2 * (section % 2))
    for h in range(kept_ref.shape[0]):
        spread_ref[h] = (
            jnp.dot(mine, kept_ref[h], preferred_element_type=jnp.float32)
            + jnp.dot(theirs, given_ref[h], preferred_element_type=jnp.float32)
        ).astype(jnp.bfloat16)


def settle_kernel(fits_ref, fast_ref, slow_ref, out_ref, semaphore):
    @pl.when(fits_ref[0] == 0)
    def _():
        copy = pltpu.make_async_copy(slow_ref, out_ref, semaphore)
        copy.start()
        copy.wait()


def on_device(token_ids, embed_table, norm_gain, cotangent):
    vocab_section, columns = embed_table.shape
    groups = lax.axis_size("dp")
    sections = lax.axis_size(SECTION)
    tokens, features = cotangent.shape
    V, S = pltpu.VMEM, pltpu.SMEM
    bf16 = functools.partial(jax.ShapeDtypeStruct, dtype=jnp.bfloat16)
    f32 = pltpu.VMEM
    i32 = functools.partial(jax.ShapeDtypeStruct, dtype=jnp.int32)
    section = lax.axis_index(SECTION).reshape(1)
    own_ids = token_ids.reshape(1, tokens)
    all_cotangent = lax.all_gather(cotangent, SECTION, axis=0)
    (marked,) = call(mark_kernel, (own_ids,), (V,), [i32((groups, 1, tokens))])
    marked = lax.all_to_all(marked, "dp", 0, 0, tiled=True).reshape(groups, tokens)
    all_ids = marked % REPEATED
    in_section = all_ids[:, :, None] // vocab_section == jnp.arange(sections)
    new_in_section = in_section & (marked < REPEATED)[:, :, None]
    fits = (jnp.max(jnp.sum(in_section, axis=1)) <= TOKEN_SLOTS) & (
        jnp.max(jnp.sum(new_in_section, axis=1)) <= ROW_SLOTS
    )

    wide_table = f32((vocab_section + CHUNK, columns), jnp.float32)
    wide_slots = f32((ROW_SLOTS, columns), jnp.float32)
    index, count = call(
        functools.partial(row_plan_kernel, vocab_section=vocab_section),
        (section, marked), (S, V), [i32((ROW_SLOTS, LANES)), i32((8, LANES))],
    )
    (rows,) = call(
        row_pick_kernel, (index, count, embed_table), (S, S, V),
        [bf16((groups, ROW_SLOTS, columns))], [wide_table, wide_slots],
    )
    full_rows = lax.all_to_all(rows, "dp", 0, 0, tiled=True)
    slot_cotangent, expand, combine = call(
        functools.partial(select_kernel, vocab_section=vocab_section),
        (section, own_ids, all_cotangent), (S, V, V),
        [
            bf16((sections, TOKEN_SLOTS, features)),
            bf16((TOKEN_SLOTS, ROW_SLOTS)),
            bf16((ROW_SLOTS, TOKEN_SLOTS)),
        ],
    )
    half = bf16((sections // 2, TOKEN_SLOTS, features))
    by_column, keep, give = call(
        grad_kernel,
        (section, full_rows, slot_cotangent, norm_gain.reshape(sections, features), expand, combine),
        (S, V, V, V, V, V),
        [bf16(full_rows.shape), half, half],
        [f32((sections, TOKEN_SLOTS, features), jnp.float32)],
    )
    given = lax.ppermute(give, CORES, [(0, 1), (1, 0)])
    (spread,) = call(
        functools.partial(spread_kernel, vocab_section=vocab_section),
        (section, own_ids, keep, given), (S, V, V, V), [bf16((sections // 2, tokens, features))],
    )
    by_column, spread = lax.optimization_barrier((by_column, spread))
    fast_grad = lax.psum_scatter(spread, CHIPS, scatter_dimension=0, tiled=True)[0]
    back = lax.all_to_all(by_column, "dp", 0, 0, tiled=True)

    def fast(index, count, back, *_):
        (grad_table,) = call(
            row_add_kernel, (index, count, back), (S, S, V),
            [bf16((vocab_section, columns))], [wide_table, wide_slots],
        )
        return grad_table, jnp.zeros((tokens, features), jnp.bfloat16)

    def slow(index, count, back, *operands):
        return passage(tokens, *operands)

    grad_table, slow_grad = lax.cond(
        fits, fast, slow, index, count, back,
        section, all_ids, own_ids, embed_table, norm_gain, cotangent,
    )
    anywhere = pl.BlockSpec(memory_space=pl.ANY)
    own_grad = pl.pallas_call(
        settle_kernel,
        in_specs=[whole((1,), S), anywhere, anywhere],
        out_specs=anywhere,
        out_shape=bf16((tokens, features)),
        scratch_shapes=[pltpu.SemaphoreType.DMA],
        input_output_aliases={1: 0},
    )(fits.astype(jnp.int32).reshape(1), fast_grad, slow_grad)
    return grad_table, own_grad


def solution(mesh):
    split = Mesh(mesh.devices.reshape(-1, 2, mesh.shape["dp"]), (CHIPS, CORES, "dp"))
    return jax.shard_map(
        on_device,
        mesh=split,
        in_specs=(P("dp"), P(SECTION, "dp"), P(), P("dp", SECTION)),
        out_specs=(P(SECTION, "dp"), P("dp", SECTION)),
        check_vma=False,
    )
```

```python
import functools
import math

import jax
import jax.numpy as jnp
from jax import lax
from jax.experimental import pallas as pl
from jax.experimental.pallas import tpu as pltpu
from jax.sharding import Mesh
from jax.sharding import PartitionSpec as P

epsilon = 1e-05
TOKEN_SLOTS = 48
ROW_SLOTS = 32
CHUNK = 8
REPEATED = 1 << 16
CHIPS = "section_0"
CORES = "section_1"
SECTION = (CHIPS, CORES)
LANES = 128


def whole(shape, space=pltpu.VMEM):
    if space == pltpu.HBM:
        return pl.BlockSpec(memory_space=space)
    return pl.BlockSpec(shape, lambda *_: (0,) * len(shape), memory_space=space)


def plan_kernel(section_ref, ids_ref, index_ref, count_ref, *, slots, vocab_section):
    ids = ids_ref[...].astype(jnp.float32)
    ids = jnp.concatenate([ids, ids], axis=0)
    ids = ids.T.astype(jnp.int32)
    local = ids - section_ref[0] * vocab_section
    inside = (local >= 0) & (local < vocab_section)
    before = (
        lax.broadcasted_iota(jnp.int32, (LANES, LANES), 1)
        < lax.broadcasted_iota(jnp.int32, (LANES, LANES), 0)
    )
    ones = jnp.where(inside, 1.0, 0.0)
    rank = jnp.dot(
        jnp.where(before, 1.0, 0.0).astype(jnp.bfloat16),
        ones.astype(jnp.bfloat16),
        preferred_element_type=jnp.float32,
    ).astype(jnp.int32)
    rank = jnp.where(inside, rank, -1)
    for c in range(slots):
        index_ref[pl.ds(c, 1), :] = jnp.sum(jnp.where(rank == c, local, 0), axis=0, keepdims=True)
    count_ref[...] = jnp.broadcast_to(
        jnp.sum(ones, axis=0, keepdims=True).astype(jnp.int32), count_ref.shape
    )


def pick_kernel(index_ref, table_ref, rows_ref, wide_ref, picked_ref, *, slots, groups):
    step = 256

    def widen(i, carry):
        wide_ref[pl.ds(i * step, step), :] = table_ref[pl.ds(i * step, step), :].astype(jnp.float32)
        return carry

    lax.fori_loop(0, table_ref.shape[0] // step, widen, 0)

    def group(g, carry):
        for c in range(slots):
            picked_ref[pl.ds(c, 1), :] = wide_ref[pl.ds(index_ref[c, g], 1), :]
        rows_ref[g] = picked_ref[...].astype(jnp.bfloat16)
        return carry

    lax.fori_loop(0, groups, group, 0)


def slot_of(ids_row, slots, vocab_section):
    wide = jnp.broadcast_to(ids_row // vocab_section, (LANES, LANES))
    tall = wide.astype(jnp.float32).T.astype(jnp.int32)
    first = lax.broadcasted_iota(jnp.int32, (LANES, LANES), 0)
    second = lax.broadcasted_iota(jnp.int32, (LANES, LANES), 1)
    same = wide == tall
    as_row = jnp.sum(jnp.where(same & (first < second), 1, 0), axis=0, keepdims=True)
    as_column = jnp.sum(jnp.where(same & (second < first), 1.0, 0.0), axis=1, keepdims=True)
    row_slot = jnp.where(as_row < slots, wide[:1] * slots + as_row, -1)
    as_column = as_column.astype(jnp.int32)
    column_slot = jnp.where(as_column < slots, tall[:, :1] * slots + as_column, -1)
    return row_slot, column_slot


def deal_kernel(ids_ref, cotangent_ref, dealt_ref, *, slots, sections, vocab_section):
    row_slot, _ = slot_of(ids_ref[...], slots, vocab_section)
    cotangent = cotangent_ref[...]
    for s in range(sections):
        wanted = lax.broadcasted_iota(jnp.int32, (slots, LANES), 0) + s * slots == row_slot
        dealt_ref[s] = jnp.dot(
            jnp.where(wanted, 1.0, 0.0).astype(jnp.bfloat16),
            cotangent,
            preferred_element_type=jnp.float32,
        ).astype(jnp.bfloat16)


def collect_kernel(ids_ref, dealt_ref, own_ref, *, slots, sections, vocab_section):
    _, column_slot = slot_of(ids_ref[...], slots, vocab_section)
    total = jnp.zeros(own_ref.shape, jnp.float32)
    for s in range(sections):
        wanted = lax.broadcasted_iota(jnp.int32, (LANES, slots), 1) + s * slots == column_slot
        total = total + jnp.dot(
            jnp.where(wanted, 1.0, 0.0).astype(jnp.bfloat16),
            dealt_ref[s],
            preferred_element_type=jnp.float32,
        )
    own_ref[...] = total.astype(jnp.bfloat16)


def norm_kernel(rows_ref, cotangent_ref, gain_ref, by_column_ref, by_feature_ref):
    pieces, slots, columns = rows_ref.shape
    per = cotangent_ref.shape[2] // columns
    width = pieces * columns

    def parts(k, j):
        embedded = rows_ref[k * per + j].astype(jnp.float32)
        own = cotangent_ref[k, :, j * columns : (j + 1) * columns].astype(jnp.float32)
        return embedded, own * gain_ref[pl.ds(k * per + j, 1), :]

    def sums(k, carry):
        squares, inners = carry
        for j in range(per):
            embedded, scaled = parts(k, j)
            squares = squares + embedded * embedded
            inners = inners + scaled * embedded
        return squares, inners

    zeros = jnp.zeros((slots, columns), jnp.float32)
    squares, inners = lax.fori_loop(0, pieces // per, sums, (zeros, zeros))
    square_mean = jnp.sum(squares, axis=1, keepdims=True) * (1.0 / width)
    inner = jnp.sum(inners, axis=1, keepdims=True) * (1.0 / width)
    inverse = lax.rsqrt(square_mean + epsilon)
    pull = inverse * inverse * inverse * inner

    def grads(k, carry):
        for j in range(per):
            embedded, scaled = parts(k, j)
            grad = (inverse * scaled - embedded * pull).astype(jnp.bfloat16)
            by_column_ref[k * per + j] = grad
            by_feature_ref[k, :, j * columns : (j + 1) * columns] = grad
        return carry

    lax.fori_loop(0, pieces // per, grads, 0)


def add_kernel(index_ref, count_ref, grads_ref, table_ref, total_ref, wide_ref, *, groups):
    step = 256
    slots = grads_ref.shape[1]

    def clear(i, carry):
        total_ref[pl.ds(i * step, step), :] = jnp.zeros((step, LANES), jnp.float32)
        return carry

    lax.fori_loop(0, total_ref.shape[0] // step, clear, 0)

    def group(g, carry):
        wide_ref[...] = grads_ref[g].astype(jnp.float32)

        def one(c, carry):
            row = pl.ds(index_ref[c, g], 1)
            total_ref[row, :] = total_ref[row, :] + wide_ref[pl.ds(c, 1), :]
            return carry

        lax.fori_loop(0, jnp.minimum(count_ref[0, g], slots), one, 0)
        return carry

    lax.fori_loop(0, groups, group, 0)

    def narrow(i, carry):
        table_ref[pl.ds(i * step, step), :] = total_ref[pl.ds(i * step, step), :].astype(jnp.bfloat16)
        return carry

    lax.fori_loop(0, total_ref.shape[0] // step, narrow, 0)


def call(kernel, operands, spaces, outs, scratch=(), semaphores=(), room=6):
    held = sum(math.prod(a.shape) * a.dtype.itemsize for a in (*operands, *outs, *scratch))
    return pl.pallas_call(
        kernel,
        in_specs=[whole(o.shape, s) for o, s in zip(operands, spaces)],
        out_specs=[whole(o.shape) for o in outs],
        out_shape=outs,
        scratch_shapes=[*scratch, *semaphores],
        compiler_params=pltpu.CompilerParams(vmem_limit_bytes=2 * held + (room << 20)),
    )(*operands)


def passage(slots, section, all_ids, own_ids, embed_table, norm_gain, cotangent):
    vocab_section, columns = embed_table.shape
    groups = all_ids.shape[0]
    tokens, features = cotangent.shape
    sections = lax.axis_size(SECTION)
    V, S = pltpu.VMEM, pltpu.SMEM
    bf16 = functools.partial(jax.ShapeDtypeStruct, dtype=jnp.bfloat16)
    i32 = functools.partial(jax.ShapeDtypeStruct, dtype=jnp.int32)
    (dealt,) = call(
        functools.partial(deal_kernel, slots=slots, sections=sections, vocab_section=vocab_section),
        (own_ids, cotangent), (V, V), [bf16((sections, slots, features))],
    )
    their_cotangent = lax.all_to_all(dealt, SECTION, 0, 0, tiled=True)
    index, count = call(
        functools.partial(plan_kernel, slots=slots, vocab_section=vocab_section),
        (section, all_ids), (S, V), [i32((slots, LANES)), i32((8, LANES))],
    )
    (rows,) = call(
        functools.partial(pick_kernel, slots=slots, groups=groups),
        (index, embed_table), (S, V), [bf16((groups, slots, columns))],
        [pltpu.VMEM((vocab_section, columns), jnp.float32), pltpu.VMEM((slots, columns), jnp.float32)],
    )
    full_rows = lax.all_to_all(rows, "dp", 0, 0, tiled=True)
    gain = norm_gain.reshape(groups, columns)
    by_column, by_feature = call(
        norm_kernel, (full_rows, their_cotangent, gain), (V, V, V),
        [bf16(full_rows.shape), bf16(their_cotangent.shape)],
    )
    back = lax.all_to_all(by_column, "dp", 0, 0, tiled=True)
    home = lax.all_to_all(by_feature, SECTION, 0, 0, tiled=True)
    (grad_table,) = call(
        functools.partial(add_kernel, groups=groups),
        (index, count, back), (S, S, V), [bf16((vocab_section, columns))],
        [pltpu.VMEM((vocab_section, columns), jnp.float32), pltpu.VMEM((slots, columns), jnp.float32)],
    )
    (own_grad,) = call(
        functools.partial(collect_kernel, slots=slots, sections=sections, vocab_section=vocab_section),
        (own_ids, home), (V, V), [bf16((tokens, features))],
    )
    return grad_table, own_grad


def row_plan(section, ids, plan_ref, vocab_section):
    slots = plan_ref.shape[0] - CHUNK
    ids = ids.astype(jnp.float32)
    ids = jnp.concatenate([ids, ids], axis=0)
    ids = ids.T.astype(jnp.int32)
    local = ids - section * vocab_section
    inside = (local >= 0) & (local < vocab_section) & (ids < REPEATED)
    before = (
        lax.broadcasted_iota(jnp.int32, (LANES, LANES), 1)
        < lax.broadcasted_iota(jnp.int32, (LANES, LANES), 0)
    )
    ones = jnp.where(inside, 1.0, 0.0)
    rank = jnp.dot(
        jnp.where(before, 1.0, 0.0).astype(jnp.bfloat16),
        ones.astype(jnp.bfloat16),
        preferred_element_type=jnp.float32,
    ).astype(jnp.int32)
    rank = jnp.where(inside, rank, -1)
    short = local - vocab_section
    for c in range(slots):
        plan_ref[pl.ds(c, 1), :] = vocab_section + jnp.sum(
            jnp.where(rank == c, short, 0), axis=0, keepdims=True
        )
    count = jnp.minimum(jnp.sum(ones, axis=0, keepdims=True).astype(jnp.int32), slots)
    plan_ref[pl.ds(slots, CHUNK), :] = jnp.broadcast_to((count + (CHUNK - 1)) // CHUNK, (CHUNK, LANES))


def row_pick_kernel(
    section_ref, ids_ref, table_ref, rows_ref, plan_ref,
    held_ref, wide_ref, picked_ref, steps_ref, arrived, planned, *, vocab_section
):
    groups, slots, columns = rows_ref.shape
    entries = table_ref.shape[0]
    pieces = arrived.shape[0]
    piece = entries // pieces
    copies = [
        pltpu.make_async_copy(
            table_ref.at[pl.ds(i * piece, piece)], held_ref.at[pl.ds(i * piece, piece)], arrived.at[i]
        )
        for i in range(pieces)
    ]
    for copy in copies:
        copy.start()
    row_plan(section_ref[0], ids_ref[...], plan_ref, vocab_section)
    plan_copy = pltpu.make_async_copy(plan_ref, steps_ref, planned)
    plan_copy.start()
    picked_ref[...] = jnp.zeros(picked_ref.shape, jnp.float32)
    wide_ref[pl.ds(entries, CHUNK), :] = jnp.zeros((CHUNK, columns), jnp.float32)
    step = 512

    for i, copy in enumerate(copies):
        copy.wait()

        def widen(j, carry):
            at = pl.ds(pl.multiple_of(i * piece + j * step, step), step)
            wide_ref[at, :] = held_ref[at, :].astype(jnp.float32)
            return carry

        lax.fori_loop(0, piece // step, widen, 0)
    plan_copy.wait()

    def group(g, carry):
        def chunk(i, carry):
            for j in range(CHUNK):
                c = i * CHUNK + j
                picked_ref[pl.ds(c, 1), :] = wide_ref[pl.ds(steps_ref[c, g], 1), :]
            return carry

        lax.fori_loop(0, steps_ref[slots, g], chunk, 0)
        rows_ref[g] = picked_ref[...].astype(jnp.bfloat16)
        return carry

    lax.fori_loop(0, groups, group, 0)


def row_add_kernel(plan_ref, grads_ref, table_ref, total_ref, wide_ref):
    groups, slots, columns = grads_ref.shape
    entries = table_ref.shape[0]
    step = 512

    def clear(i, carry):
        total_ref[pl.ds(i * step, step), :] = jnp.zeros((step, columns), jnp.float32)
        return carry

    lax.fori_loop(0, entries // step, clear, 0)
    total_ref[pl.ds(entries, CHUNK), :] = jnp.zeros((CHUNK, columns), jnp.float32)

    def group(g, carry):
        wide_ref[...] = grads_ref[g].astype(jnp.float32)

        def chunk(i, carry):
            rows = [pl.ds(plan_ref[i * CHUNK + j, g], 1) for j in range(CHUNK)]
            sums = [
                total_ref[row, :] + wide_ref[pl.ds(i * CHUNK + j, 1), :]
                for j, row in enumerate(rows)
            ]
            for row, value in zip(rows, sums):
                total_ref[row, :] = value
            return carry

        lax.fori_loop(0, plan_ref[slots, g], chunk, 0)
        return carry

    lax.fori_loop(0, groups, group, 0)

    def narrow(i, carry):
        table_ref[pl.ds(i * step, step), :] = total_ref[pl.ds(i * step, step), :].astype(jnp.bfloat16)
        return carry

    lax.fori_loop(0, entries // step, narrow, 0)


def both_ways(ids_row):
    wide = jnp.broadcast_to(ids_row, (LANES, LANES))
    tall = wide.astype(jnp.float32).T.astype(jnp.int32)
    down = lax.broadcasted_iota(jnp.int32, (LANES, LANES), 0)
    along = lax.broadcasted_iota(jnp.int32, (LANES, LANES), 1)
    return wide, tall, down < along, along < down


def mark_kernel(ids_ref, marked_ref):
    wide, tall, row_first, _ = both_ways(ids_ref[...])
    repeated = jnp.max(jnp.where((wide == tall) & row_first, REPEATED, 0), axis=0, keepdims=True)
    marked_ref[...] = jnp.broadcast_to((wide[:1] + repeated)[None], marked_ref.shape)


def one_hot(condition):
    return jnp.where(condition, 1.0, 0.0).astype(jnp.bfloat16)


def select_kernel(
    section_ref, ids_ref, cotangent_ref, own_ref, expand_ref, combine_ref, held_ref, arrived, *, vocab_section
):
    copies = [
        pltpu.make_async_copy(cotangent_ref.at[s], held_ref.at[s], arrived.at[s])
        for s in range(cotangent_ref.shape[0])
    ]
    for copy in copies:
        copy.start()
    token_slots, row_slots = expand_ref.shape
    wide, tall, row_first, column_first = both_ways(ids_ref[...])
    section = section_ref[0]
    wide_in = wide // vocab_section == section
    tall_in = tall // vocab_section == section
    same = wide == tall
    wide_repeat = jnp.max(jnp.where(same & row_first, 1, 0), axis=0, keepdims=True)
    tall_repeat = jnp.max(jnp.where(same & column_first, 1.0, 0.0), axis=1, keepdims=True)
    wide_new = wide_in & (jnp.broadcast_to(wide_repeat, (LANES, LANES)) == 0)
    tall_new = tall_in & (jnp.broadcast_to(tall_repeat, (LANES, LANES)) == 0.0)
    rank = jnp.sum(jnp.where(tall_in & row_first, 1, 0), axis=0, keepdims=True)
    rank = jnp.where(wide_in[:1], rank, -1)
    own = one_hot(lax.broadcasted_iota(jnp.int32, (token_slots, LANES), 0) == rank)
    tall_place = jnp.sum(jnp.where(wide_new & column_first, 1.0, 0.0), axis=1, keepdims=True)
    place = jnp.sum(
        jnp.where(same & tall_new, jnp.broadcast_to(tall_place, (LANES, LANES)), 0.0), axis=0, keepdims=True
    ).astype(jnp.int32)
    place = jnp.where(wide_in[:1], place, -1)
    rows = one_hot(lax.broadcasted_iota(jnp.int32, (row_slots, LANES), 0) == place)
    over_tokens = (((1,), (1,)), ((), ()))
    expand_ref[...] = lax.dot_general(
        own, rows, over_tokens, preferred_element_type=jnp.float32
    ).astype(jnp.bfloat16)
    combine_ref[...] = lax.dot_general(
        rows, own, over_tokens, preferred_element_type=jnp.float32
    ).astype(jnp.bfloat16)
    for s, copy in enumerate(copies):
        copy.wait()
        own_ref[s] = jnp.dot(
            own, held_ref[s], preferred_element_type=jnp.float32
        ).astype(jnp.bfloat16)


def slot_grad(k, cotangent_ref, gain_ref, embedded_ref, inverse, pull):
    scaled = cotangent_ref[k].astype(jnp.float32) * gain_ref[pl.ds(k, 1), :]
    return (inverse * scaled - embedded_ref[k].astype(jnp.float32) * pull).astype(jnp.bfloat16)


def give_kernel(
    section_ref, rows_ref, cotangent_ref, gain_ref, expand_ref,
    give_ref, inverse_ref, pull_ref, embedded_ref,
):
    pieces, _, columns = rows_ref.shape
    sections, slots, features = cotangent_ref.shape
    per = features // columns
    width = pieces * columns
    expand = expand_ref[...]

    def sums(k, carry):
        squares, inners = carry
        rows = jnp.concatenate([rows_ref[k * per + j] for j in range(per)], axis=1)
        embedded = jnp.dot(expand, rows, preferred_element_type=jnp.float32)
        embedded_ref[k] = embedded.astype(jnp.bfloat16)
        scaled = cotangent_ref[k].astype(jnp.float32) * gain_ref[pl.ds(k, 1), :]
        square = embedded * embedded
        inner = scaled * embedded
        for j in range(per):
            squares = squares + square[:, j * columns : (j + 1) * columns]
            inners = inners + inner[:, j * columns : (j + 1) * columns]
        return squares, inners

    zeros = jnp.zeros((slots, columns), jnp.float32)
    squares, inners = lax.fori_loop(0, sections, sums, (zeros, zeros))
    square_mean = jnp.sum(squares, axis=1, keepdims=True) * (1.0 / width)
    inner = jnp.sum(inners, axis=1, keepdims=True) * (1.0 / width)
    inverse = lax.rsqrt(square_mean + epsilon)
    pull = inverse * inverse * inverse * inner
    inverse_ref[...] = jnp.broadcast_to(inverse, inverse_ref.shape)
    pull_ref[...] = jnp.broadcast_to(pull, pull_ref.shape)
    core = section_ref[0] % 2

    def chip(h, carry):
        give_ref[h] = slot_grad(
            2 * h + 1 - core, cotangent_ref, gain_ref, embedded_ref, inverse, pull
        )
        return carry

    lax.fori_loop(0, sections // 2, chip, 0)


def keep_kernel(
    section_ref, cotangent_ref, gain_ref, embedded_ref, inverse_ref, pull_ref, give_ref, combine_ref,
    by_column_ref, keep_ref,
):
    columns = by_column_ref.shape[2]
    sections, _, features = cotangent_ref.shape
    per = features // columns
    combine = combine_ref[...]
    inverse = inverse_ref[:, :1]
    pull = pull_ref[:, :1]
    core = section_ref[0] % 2

    def add(k, grad):
        added = jnp.dot(combine, grad, preferred_element_type=jnp.float32).astype(jnp.bfloat16)
        for j in range(per):
            by_column_ref[k * per + j] = added[:, j * columns : (j + 1) * columns]

    def chip(h, carry):
        k = 2 * h + core
        grad = slot_grad(k, cotangent_ref, gain_ref, embedded_ref, inverse, pull)
        keep_ref[h] = grad
        add(k, grad)
        add(2 * h + 1 - core, give_ref[h])
        return carry

    lax.fori_loop(0, sections // 2, chip, 0)


def spread_kernel(section_ref, ids_ref, kept_ref, given_ref, spread_ref, *, vocab_section):
    slots = kept_ref.shape[1]
    wide, tall, _, column_first = both_ways(ids_ref[...])
    wide = wide // vocab_section
    tall = tall // vocab_section
    along = lax.broadcasted_iota(jnp.int32, (LANES, slots), 1)

    def of(section):
        rank = jnp.sum(jnp.where((wide == section) & column_first, 1.0, 0.0), axis=1, keepdims=True)
        rank = jnp.where(tall[:, :1] == section, rank.astype(jnp.int32), -1)
        return one_hot(along == rank)

    section = section_ref[0]
    mine = of(section)
    theirs = of(section + 1 - 2 * (section % 2))
    for h in range(kept_ref.shape[0]):
        spread_ref[h] = (
            jnp.dot(mine, kept_ref[h], preferred_element_type=jnp.float32)
            + jnp.dot(theirs, given_ref[h], preferred_element_type=jnp.float32)
        ).astype(jnp.bfloat16)


def settle_kernel(fits_ref, fast_ref, slow_ref, out_ref, semaphore):
    @pl.when(fits_ref[0] == 0)
    def _():
        copy = pltpu.make_async_copy(slow_ref, out_ref, semaphore)
        copy.start()
        copy.wait()


def on_device(token_ids, embed_table, norm_gain, cotangent):
    vocab_section, columns = embed_table.shape
    groups = lax.axis_size("dp")
    sections = lax.axis_size(SECTION)
    tokens, features = cotangent.shape
    V, S = pltpu.VMEM, pltpu.SMEM
    bf16 = functools.partial(jax.ShapeDtypeStruct, dtype=jnp.bfloat16)
    f32 = pltpu.VMEM
    i32 = functools.partial(jax.ShapeDtypeStruct, dtype=jnp.int32)
    section = lax.axis_index(SECTION).reshape(1)
    own_ids = token_ids.reshape(1, tokens)
    all_cotangent = lax.all_gather(cotangent, SECTION, axis=0)
    (marked,) = call(mark_kernel, (own_ids,), (V,), [i32((groups, 1, tokens))])
    marked = lax.all_to_all(marked, "dp", 0, 0, tiled=True).reshape(groups, tokens)
    all_ids = marked % REPEATED
    in_section = all_ids[:, :, None] // vocab_section == jnp.arange(sections)
    new_in_section = in_section & (marked < REPEATED)[:, :, None]
    fits = (jnp.max(jnp.sum(in_section, axis=1)) <= TOKEN_SLOTS) & (
        jnp.max(jnp.sum(new_in_section, axis=1)) <= ROW_SLOTS
    )

    wide_shape = (vocab_section + CHUNK, columns)
    wide_slots = f32((ROW_SLOTS, columns), jnp.float32)
    plan_shape = (ROW_SLOTS + CHUNK, LANES)
    rows, plan = call(
        functools.partial(row_pick_kernel, vocab_section=vocab_section),
        (section, marked, embed_table), (S, V, pltpu.HBM),
        [bf16((groups, ROW_SLOTS, columns)), i32(plan_shape)],
        [f32(embed_table.shape, jnp.bfloat16), f32(wide_shape, jnp.float32), wide_slots],
        [pltpu.SMEM(plan_shape, jnp.int32), pltpu.SemaphoreType.DMA((4,)), pltpu.SemaphoreType.DMA],
    )
    full_rows = lax.all_to_all(rows, "dp", 0, 0, tiled=True)
    own_slots = bf16((sections, TOKEN_SLOTS, features))
    slot_cotangent, expand, combine = call(
        functools.partial(select_kernel, vocab_section=vocab_section),
        (section, own_ids, all_cotangent), (S, V, pltpu.HBM),
        [own_slots, bf16((TOKEN_SLOTS, ROW_SLOTS)), bf16((ROW_SLOTS, TOKEN_SLOTS))],
        [f32((sections, tokens, features), jnp.bfloat16)],
        [pltpu.SemaphoreType.DMA((sections,))], room=42,
    )
    half = bf16((sections // 2, TOKEN_SLOTS, features))
    statistic = jax.ShapeDtypeStruct((TOKEN_SLOTS, LANES), jnp.float32)
    gain = norm_gain.reshape(sections, features)
    give, inverse, pull, embedded = call(
        give_kernel, (section, full_rows, slot_cotangent, gain, expand), (S, V, V, V, V),
        [half, statistic, statistic, own_slots],
    )
    given = lax.ppermute(give, CORES, [(0, 1), (1, 0)])
    by_column, keep = call(
        keep_kernel, (section, slot_cotangent, gain, embedded, inverse, pull, give, combine),
        (S, V, V, V, V, V, V, V), [bf16(full_rows.shape), half],
    )
    (spread,) = call(
        functools.partial(spread_kernel, vocab_section=vocab_section),
        (section, own_ids, keep, given), (S, V, V, V), [bf16((sections // 2, tokens, features))],
    )
    by_column, spread = lax.optimization_barrier((by_column, spread))
    fast_grad = lax.psum_scatter(spread, CHIPS, scatter_dimension=0, tiled=True)[0]
    back = lax.all_to_all(by_column, "dp", 0, 0, tiled=True)

    def fast(plan, back, *_):
        (grad_table,) = call(
            row_add_kernel, (plan, back), (S, V),
            [bf16((vocab_section, columns))], [f32(wide_shape, jnp.float32), wide_slots],
        )
        return grad_table, jnp.zeros((tokens, features), jnp.bfloat16)

    def slow(plan, back, *operands):
        return passage(tokens, *operands)

    grad_table, slow_grad = lax.cond(
        fits, fast, slow, plan, back,
        section, all_ids, own_ids, embed_table, norm_gain, cotangent,
    )
    anywhere = pl.BlockSpec(memory_space=pl.ANY)
    own_grad = pl.pallas_call(
        settle_kernel,
        in_specs=[whole((1,), S), anywhere, anywhere],
        out_specs=anywhere,
        out_shape=bf16((tokens, features)),
        scratch_shapes=[pltpu.SemaphoreType.DMA],
        input_output_aliases={1: 0},
    )(fits.astype(jnp.int32).reshape(1), fast_grad, slow_grad)
    return grad_table, own_grad


def solution(mesh):
    split = Mesh(mesh.devices.reshape(-1, 2, mesh.shape["dp"]), (CHIPS, CORES, "dp"))
    return jax.shard_map(
        on_device,
        mesh=split,
        in_specs=(P("dp"), P(SECTION, "dp"), P(), P("dp", SECTION)),
        out_specs=(P(SECTION, "dp"), P("dp", SECTION)),
        check_vma=False,
    )
```

```python
import functools
import math

import jax
import jax.numpy as jnp
from jax import lax
from jax.experimental import pallas as pl
from jax.experimental.pallas import tpu as pltpu
from jax.sharding import Mesh
from jax.sharding import PartitionSpec as P

epsilon = 1e-05
TOKEN_SLOTS = 48
ROW_SLOTS = 32
CHUNK = 8
REPEATED = 1 << 16
CHIPS = "section_0"
CORES = "section_1"
SECTION = (CHIPS, CORES)
LANES = 128


def whole(shape, space=pltpu.VMEM):
    if space == pltpu.HBM:
        return pl.BlockSpec(memory_space=space)
    return pl.BlockSpec(shape, lambda *_: (0,) * len(shape), memory_space=space)


def plan_kernel(section_ref, ids_ref, index_ref, count_ref, *, slots, vocab_section):
    ids = ids_ref[...].astype(jnp.float32)
    ids = jnp.concatenate([ids, ids], axis=0)
    ids = ids.T.astype(jnp.int32)
    local = ids - section_ref[0] * vocab_section
    inside = (local >= 0) & (local < vocab_section)
    before = (
        lax.broadcasted_iota(jnp.int32, (LANES, LANES), 1)
        < lax.broadcasted_iota(jnp.int32, (LANES, LANES), 0)
    )
    ones = jnp.where(inside, 1.0, 0.0)
    rank = jnp.dot(
        jnp.where(before, 1.0, 0.0).astype(jnp.bfloat16),
        ones.astype(jnp.bfloat16),
        preferred_element_type=jnp.float32,
    ).astype(jnp.int32)
    rank = jnp.where(inside, rank, -1)
    for c in range(slots):
        index_ref[pl.ds(c, 1), :] = jnp.sum(jnp.where(rank == c, local, 0), axis=0, keepdims=True)
    count_ref[...] = jnp.broadcast_to(
        jnp.sum(ones, axis=0, keepdims=True).astype(jnp.int32), count_ref.shape
    )


def pick_kernel(index_ref, table_ref, rows_ref, wide_ref, picked_ref, *, slots, groups):
    step = 256

    def widen(i, carry):
        wide_ref[pl.ds(i * step, step), :] = table_ref[pl.ds(i * step, step), :].astype(jnp.float32)
        return carry

    lax.fori_loop(0, table_ref.shape[0] // step, widen, 0)

    def group(g, carry):
        for c in range(slots):
            picked_ref[pl.ds(c, 1), :] = wide_ref[pl.ds(index_ref[c, g], 1), :]
        rows_ref[g] = picked_ref[...].astype(jnp.bfloat16)
        return carry

    lax.fori_loop(0, groups, group, 0)


def slot_of(ids_row, slots, vocab_section):
    wide = jnp.broadcast_to(ids_row // vocab_section, (LANES, LANES))
    tall = wide.astype(jnp.float32).T.astype(jnp.int32)
    first = lax.broadcasted_iota(jnp.int32, (LANES, LANES), 0)
    second = lax.broadcasted_iota(jnp.int32, (LANES, LANES), 1)
    same = wide == tall
    as_row = jnp.sum(jnp.where(same & (first < second), 1, 0), axis=0, keepdims=True)
    as_column = jnp.sum(jnp.where(same & (second < first), 1.0, 0.0), axis=1, keepdims=True)
    row_slot = jnp.where(as_row < slots, wide[:1] * slots + as_row, -1)
    as_column = as_column.astype(jnp.int32)
    column_slot = jnp.where(as_column < slots, tall[:, :1] * slots + as_column, -1)
    return row_slot, column_slot


def deal_kernel(ids_ref, cotangent_ref, dealt_ref, *, slots, sections, vocab_section):
    row_slot, _ = slot_of(ids_ref[...], slots, vocab_section)
    cotangent = cotangent_ref[...]
    for s in range(sections):
        wanted = lax.broadcasted_iota(jnp.int32, (slots, LANES), 0) + s * slots == row_slot
        dealt_ref[s] = jnp.dot(
            jnp.where(wanted, 1.0, 0.0).astype(jnp.bfloat16),
            cotangent,
            preferred_element_type=jnp.float32,
        ).astype(jnp.bfloat16)


def collect_kernel(ids_ref, dealt_ref, own_ref, *, slots, sections, vocab_section):
    _, column_slot = slot_of(ids_ref[...], slots, vocab_section)
    total = jnp.zeros(own_ref.shape, jnp.float32)
    for s in range(sections):
        wanted = lax.broadcasted_iota(jnp.int32, (LANES, slots), 1) + s * slots == column_slot
        total = total + jnp.dot(
            jnp.where(wanted, 1.0, 0.0).astype(jnp.bfloat16),
            dealt_ref[s],
            preferred_element_type=jnp.float32,
        )
    own_ref[...] = total.astype(jnp.bfloat16)


def norm_kernel(rows_ref, cotangent_ref, gain_ref, by_column_ref, by_feature_ref):
    pieces, slots, columns = rows_ref.shape
    per = cotangent_ref.shape[2] // columns
    width = pieces * columns

    def parts(k, j):
        embedded = rows_ref[k * per + j].astype(jnp.float32)
        own = cotangent_ref[k, :, j * columns : (j + 1) * columns].astype(jnp.float32)
        return embedded, own * gain_ref[pl.ds(k * per + j, 1), :]

    def sums(k, carry):
        squares, inners = carry
        for j in range(per):
            embedded, scaled = parts(k, j)
            squares = squares + embedded * embedded
            inners = inners + scaled * embedded
        return squares, inners

    zeros = jnp.zeros((slots, columns), jnp.float32)
    squares, inners = lax.fori_loop(0, pieces // per, sums, (zeros, zeros))
    square_mean = jnp.sum(squares, axis=1, keepdims=True) * (1.0 / width)
    inner = jnp.sum(inners, axis=1, keepdims=True) * (1.0 / width)
    inverse = lax.rsqrt(square_mean + epsilon)
    pull = inverse * inverse * inverse * inner

    def grads(k, carry):
        for j in range(per):
            embedded, scaled = parts(k, j)
            grad = (inverse * scaled - embedded * pull).astype(jnp.bfloat16)
            by_column_ref[k * per + j] = grad
            by_feature_ref[k, :, j * columns : (j + 1) * columns] = grad
        return carry

    lax.fori_loop(0, pieces // per, grads, 0)


def add_kernel(index_ref, count_ref, grads_ref, table_ref, total_ref, wide_ref, *, groups):
    step = 256
    slots = grads_ref.shape[1]

    def clear(i, carry):
        total_ref[pl.ds(i * step, step), :] = jnp.zeros((step, LANES), jnp.float32)
        return carry

    lax.fori_loop(0, total_ref.shape[0] // step, clear, 0)

    def group(g, carry):
        wide_ref[...] = grads_ref[g].astype(jnp.float32)

        def one(c, carry):
            row = pl.ds(index_ref[c, g], 1)
            total_ref[row, :] = total_ref[row, :] + wide_ref[pl.ds(c, 1), :]
            return carry

        lax.fori_loop(0, jnp.minimum(count_ref[0, g], slots), one, 0)
        return carry

    lax.fori_loop(0, groups, group, 0)

    def narrow(i, carry):
        table_ref[pl.ds(i * step, step), :] = total_ref[pl.ds(i * step, step), :].astype(jnp.bfloat16)
        return carry

    lax.fori_loop(0, total_ref.shape[0] // step, narrow, 0)


def call(kernel, operands, spaces, outs, scratch=(), semaphores=(), room=6):
    held = sum(math.prod(a.shape) * a.dtype.itemsize for a in (*operands, *outs, *scratch))
    return pl.pallas_call(
        kernel,
        in_specs=[whole(o.shape, s) for o, s in zip(operands, spaces)],
        out_specs=[whole(o.shape) for o in outs],
        out_shape=outs,
        scratch_shapes=[*scratch, *semaphores],
        compiler_params=pltpu.CompilerParams(vmem_limit_bytes=2 * held + (room << 20)),
    )(*operands)


def passage(slots, section, all_ids, own_ids, embed_table, norm_gain, cotangent):
    vocab_section, columns = embed_table.shape
    groups = all_ids.shape[0]
    tokens, features = cotangent.shape
    sections = lax.axis_size(SECTION)
    V, S = pltpu.VMEM, pltpu.SMEM
    bf16 = functools.partial(jax.ShapeDtypeStruct, dtype=jnp.bfloat16)
    i32 = functools.partial(jax.ShapeDtypeStruct, dtype=jnp.int32)
    (dealt,) = call(
        functools.partial(deal_kernel, slots=slots, sections=sections, vocab_section=vocab_section),
        (own_ids, cotangent), (V, V), [bf16((sections, slots, features))],
    )
    their_cotangent = lax.all_to_all(dealt, SECTION, 0, 0, tiled=True)
    index, count = call(
        functools.partial(plan_kernel, slots=slots, vocab_section=vocab_section),
        (section, all_ids), (S, V), [i32((slots, LANES)), i32((8, LANES))],
    )
    (rows,) = call(
        functools.partial(pick_kernel, slots=slots, groups=groups),
        (index, embed_table), (S, V), [bf16((groups, slots, columns))],
        [pltpu.VMEM((vocab_section, columns), jnp.float32), pltpu.VMEM((slots, columns), jnp.float32)],
    )
    full_rows = lax.all_to_all(rows, "dp", 0, 0, tiled=True)
    gain = norm_gain.reshape(groups, columns)
    by_column, by_feature = call(
        norm_kernel, (full_rows, their_cotangent, gain), (V, V, V),
        [bf16(full_rows.shape), bf16(their_cotangent.shape)],
    )
    back = lax.all_to_all(by_column, "dp", 0, 0, tiled=True)
    home = lax.all_to_all(by_feature, SECTION, 0, 0, tiled=True)
    (grad_table,) = call(
        functools.partial(add_kernel, groups=groups),
        (index, count, back), (S, S, V), [bf16((vocab_section, columns))],
        [pltpu.VMEM((vocab_section, columns), jnp.float32), pltpu.VMEM((slots, columns), jnp.float32)],
    )
    (own_grad,) = call(
        functools.partial(collect_kernel, slots=slots, sections=sections, vocab_section=vocab_section),
        (own_ids, home), (V, V), [bf16((tokens, features))],
    )
    return grad_table, own_grad


def row_plan(section, ids, plan_ref, vocab_section):
    slots = plan_ref.shape[0] - CHUNK
    ids = ids.astype(jnp.float32)
    ids = jnp.concatenate([ids, ids], axis=0)
    ids = ids.T.astype(jnp.int32)
    local = ids - section * vocab_section
    inside = (local >= 0) & (local < vocab_section) & (ids < REPEATED)
    before = (
        lax.broadcasted_iota(jnp.int32, (LANES, LANES), 1)
        < lax.broadcasted_iota(jnp.int32, (LANES, LANES), 0)
    )
    ones = jnp.where(inside, 1.0, 0.0)
    rank = jnp.dot(
        jnp.where(before, 1.0, 0.0).astype(jnp.bfloat16),
        ones.astype(jnp.bfloat16),
        preferred_element_type=jnp.float32,
    ).astype(jnp.int32)
    rank = jnp.where(inside, rank, -1)
    short = local - vocab_section
    for c in range(slots):
        plan_ref[pl.ds(c, 1), :] = vocab_section + jnp.sum(
            jnp.where(rank == c, short, 0), axis=0, keepdims=True
        )
    count = jnp.minimum(jnp.sum(ones, axis=0, keepdims=True).astype(jnp.int32), slots)
    plan_ref[pl.ds(slots, CHUNK), :] = jnp.broadcast_to((count + (CHUNK - 1)) // CHUNK, (CHUNK, LANES))


def row_pick_kernel(
    section_ref, ids_ref, table_ref, rows_ref, plan_ref,
    held_ref, wide_ref, picked_ref, steps_ref, arrived, planned, *, vocab_section
):
    groups, slots, columns = rows_ref.shape
    entries = table_ref.shape[0]
    pieces = arrived.shape[0]
    piece = entries // pieces
    copies = [
        pltpu.make_async_copy(
            table_ref.at[pl.ds(i * piece, piece)], held_ref.at[pl.ds(i * piece, piece)], arrived.at[i]
        )
        for i in range(pieces)
    ]
    for copy in copies:
        copy.start()
    row_plan(section_ref[0], ids_ref[...], plan_ref, vocab_section)
    plan_copy = pltpu.make_async_copy(plan_ref, steps_ref, planned)
    plan_copy.start()
    picked_ref[...] = jnp.zeros(picked_ref.shape, jnp.float32)
    wide_ref[pl.ds(entries, CHUNK), :] = jnp.zeros((CHUNK, columns), jnp.float32)
    step = 512

    for i, copy in enumerate(copies):
        copy.wait()

        def widen(j, carry):
            at = pl.ds(pl.multiple_of(i * piece + j * step, step), step)
            wide_ref[at, :] = held_ref[at, :].astype(jnp.float32)
            return carry

        lax.fori_loop(0, piece // step, widen, 0)
    plan_copy.wait()

    def group(g, carry):
        def chunk(i, carry):
            for j in range(CHUNK):
                c = i * CHUNK + j
                picked_ref[pl.ds(c, 1), :] = wide_ref[pl.ds(steps_ref[c, g], 1), :]
            return carry

        lax.fori_loop(0, steps_ref[slots, g], chunk, 0)
        rows_ref[g] = picked_ref[...].astype(jnp.bfloat16)
        return carry

    lax.fori_loop(0, groups, group, 0)


def row_add_kernel(plan_ref, grads_ref, table_ref, total_ref, wide_ref):
    groups, slots, columns = grads_ref.shape
    entries = table_ref.shape[0]
    step = 512

    def clear(i, carry):
        total_ref[pl.ds(i * step, step), :] = jnp.zeros((step, columns), jnp.float32)
        return carry

    lax.fori_loop(0, entries // step, clear, 0)
    total_ref[pl.ds(entries, CHUNK), :] = jnp.zeros((CHUNK, columns), jnp.float32)

    def group(g, carry):
        wide_ref[...] = grads_ref[g].astype(jnp.float32)

        def chunk(i, carry):
            rows = [pl.ds(plan_ref[i * CHUNK + j, g], 1) for j in range(CHUNK)]
            sums = [
                total_ref[row, :] + wide_ref[pl.ds(i * CHUNK + j, 1), :]
                for j, row in enumerate(rows)
            ]
            for row, value in zip(rows, sums):
                total_ref[row, :] = value
            return carry

        lax.fori_loop(0, plan_ref[slots, g], chunk, 0)
        return carry

    lax.fori_loop(0, groups, group, 0)

    def narrow(i, carry):
        table_ref[pl.ds(i * step, step), :] = total_ref[pl.ds(i * step, step), :].astype(jnp.bfloat16)
        return carry

    lax.fori_loop(0, entries // step, narrow, 0)


def both_ways(ids_row):
    wide = jnp.broadcast_to(ids_row, (LANES, LANES))
    tall = wide.astype(jnp.float32).T.astype(jnp.int32)
    down = lax.broadcasted_iota(jnp.int32, (LANES, LANES), 0)
    along = lax.broadcasted_iota(jnp.int32, (LANES, LANES), 1)
    return wide, tall, down < along, along < down


def mark_kernel(ids_ref, marked_ref):
    wide, tall, row_first, _ = both_ways(ids_ref[...])
    repeated = jnp.max(jnp.where((wide == tall) & row_first, REPEATED, 0), axis=0, keepdims=True)
    marked_ref[...] = jnp.broadcast_to((wide[:1] + repeated)[None], marked_ref.shape)


def one_hot(condition):
    return jnp.where(condition, 1.0, 0.0).astype(jnp.bfloat16)


def ranks(ids_row, vocab_section):
    wide, tall, row_first, column_first = both_ways(ids_row)
    wide = wide // vocab_section
    tall = tall // vocab_section
    same = wide == tall
    as_row = jnp.sum(jnp.where(same & row_first, 1, 0), axis=0, keepdims=True)
    as_column = jnp.sum(jnp.where(same & column_first, 1.0, 0.0), axis=1, keepdims=True)
    return wide[:1], as_row, tall[:, :1], as_column.astype(jnp.int32)


def hand_kernel(section_ref, ids_ref, cotangent_ref, *refs, vocab_section):
    *hand_refs, expand_ref, combine_ref = refs
    token_slots, row_slots = expand_ref.shape
    section = section_ref[0]
    wide_section, wide_rank, _, _ = ranks(ids_ref[...], vocab_section)
    slot = lax.broadcasted_iota(jnp.int32, (token_slots, LANES), 0)
    cotangent = cotangent_ref[...]
    for k, hand_ref in enumerate(hand_refs):
        for c in range(2):
            to = 2 * ((section // 2) ^ k) + c
            wanted = one_hot((slot == wide_rank) & (wide_section == to))
            hand_ref[c] = jnp.dot(
                wanted, cotangent, preferred_element_type=jnp.float32
            ).astype(jnp.bfloat16)

    wide, tall, row_first, column_first = both_ways(ids_ref[...])
    wide_in = wide // vocab_section == section
    tall_in = tall // vocab_section == section
    same = wide == tall
    wide_repeat = jnp.max(jnp.where(same & row_first, 1, 0), axis=0, keepdims=True)
    tall_repeat = jnp.max(jnp.where(same & column_first, 1.0, 0.0), axis=1, keepdims=True)
    wide_new = wide_in & (jnp.broadcast_to(wide_repeat, (LANES, LANES)) == 0)
    tall_new = tall_in & (jnp.broadcast_to(tall_repeat, (LANES, LANES)) == 0.0)
    own = one_hot((slot == wide_rank) & (wide_section == section))
    tall_place = jnp.sum(jnp.where(wide_new & column_first, 1.0, 0.0), axis=1, keepdims=True)
    place = jnp.sum(
        jnp.where(same & tall_new, jnp.broadcast_to(tall_place, (LANES, LANES)), 0.0), axis=0, keepdims=True
    ).astype(jnp.int32)
    place = jnp.where(wide_in[:1], place, -1)
    rows = one_hot(lax.broadcasted_iota(jnp.int32, (row_slots, LANES), 0) == place)
    over_tokens = (((1,), (1,)), ((), ()))
    expand_ref[...] = lax.dot_general(
        own, rows, over_tokens, preferred_element_type=jnp.float32
    ).astype(jnp.bfloat16)
    combine_ref[...] = lax.dot_general(
        rows, own, over_tokens, preferred_element_type=jnp.float32
    ).astype(jnp.bfloat16)


def part_kernel(section_ref, *refs):
    *hand_refs, give_ref = refs
    for k, hand_ref in enumerate(hand_refs):
        give_ref[k] = hand_ref[1 - section_ref[0] % 2]


def grad_kernel(section_ref, rows_ref, gain_ref, expand_ref, combine_ref, got_ref, *refs, chips):
    own_refs, by_column_ref, out_refs = refs[:chips], refs[chips], refs[chips + 1 : -1]
    embedded_ref = refs[-1]
    pieces, _, columns = rows_ref.shape
    _, slots, features = got_ref.shape
    per = features // columns
    width = pieces * columns
    expand = expand_ref[...]
    combine = combine_ref[...]
    section = section_ref[0]
    core = section % 2
    parts = []
    for k in range(chips):
        chip = (section // 2) ^ k
        parts.append((k, 2 * chip + core, core, own_refs[k].at[core]))
        parts.append((k, 2 * chip + 1 - core, 1 - core, got_ref.at[k]))

    squares = jnp.zeros((slots, columns), jnp.float32)
    inners = jnp.zeros((slots, columns), jnp.float32)
    for i, (_, s, _, cotangent_ref) in enumerate(parts):
        rows = jnp.concatenate([rows_ref[s * per + j] for j in range(per)], axis=1)
        embedded = jnp.dot(expand, rows, preferred_element_type=jnp.float32)
        embedded_ref[i] = embedded.astype(jnp.bfloat16)
        scaled = cotangent_ref[...].astype(jnp.float32) * gain_ref[pl.ds(s, 1), :]
        square = embedded * embedded
        inner = scaled * embedded
        for j in range(per):
            squares = squares + square[:, j * columns : (j + 1) * columns]
            inners = inners + inner[:, j * columns : (j + 1) * columns]
    square_mean = jnp.sum(squares, axis=1, keepdims=True) * (1.0 / width)
    inner = jnp.sum(inners, axis=1, keepdims=True) * (1.0 / width)
    inverse = lax.rsqrt(square_mean + epsilon)
    pull = inverse * inverse * inverse * inner

    for i, (k, s, place, cotangent_ref) in enumerate(parts):
        scaled = cotangent_ref[...].astype(jnp.float32) * gain_ref[pl.ds(s, 1), :]
        grad = (inverse * scaled - embedded_ref[i].astype(jnp.float32) * pull).astype(jnp.bfloat16)
        out_refs[k][place] = grad
        added = jnp.dot(combine, grad, preferred_element_type=jnp.float32).astype(jnp.bfloat16)
        for j in range(per):
            by_column_ref[s * per + j] = added[:, j * columns : (j + 1) * columns]


def gather_kernel(section_ref, ids_ref, got_ref, *refs, vocab_section):
    *home_refs, own_ref = refs
    slots = got_ref.shape[1]
    _, _, tall_section, tall_rank = ranks(ids_ref[...], vocab_section)
    along = lax.broadcasted_iota(jnp.int32, (LANES, slots), 1)
    section = section_ref[0]
    core = section % 2
    total = jnp.zeros(own_ref.shape, jnp.float32)
    for k, home_ref in enumerate(home_refs):
        chip = (section // 2) ^ k
        mine = one_hot((along == tall_rank) & (tall_section == 2 * chip + core))
        theirs = one_hot((along == tall_rank) & (tall_section == 2 * chip + 1 - core))
        total = total + jnp.dot(mine, home_ref[core], preferred_element_type=jnp.float32)
        total = total + jnp.dot(theirs, got_ref[k], preferred_element_type=jnp.float32)
    own_ref[...] = total.astype(jnp.bfloat16)


def settle_kernel(fits_ref, fast_ref, slow_ref, out_ref, semaphore):
    @pl.when(fits_ref[0] == 0)
    def _():
        copy = pltpu.make_async_copy(slow_ref, out_ref, semaphore)
        copy.start()
        copy.wait()


def on_device(token_ids, embed_table, norm_gain, cotangent):
    vocab_section, columns = embed_table.shape
    groups = lax.axis_size("dp")
    sections = lax.axis_size(SECTION)
    tokens, features = cotangent.shape
    V, S = pltpu.VMEM, pltpu.SMEM
    bf16 = functools.partial(jax.ShapeDtypeStruct, dtype=jnp.bfloat16)
    f32 = pltpu.VMEM
    i32 = functools.partial(jax.ShapeDtypeStruct, dtype=jnp.int32)
    section = lax.axis_index(SECTION).reshape(1)
    own_ids = token_ids.reshape(1, tokens)
    (marked,) = call(mark_kernel, (own_ids,), (V,), [i32((groups, 1, tokens))])
    marked = lax.all_to_all(marked, "dp", 0, 0, tiled=True).reshape(groups, tokens)
    all_ids = marked % REPEATED
    in_section = all_ids[:, :, None] // vocab_section == jnp.arange(sections)
    new_in_section = in_section & (marked < REPEATED)[:, :, None]
    fits = (jnp.max(jnp.sum(in_section, axis=1)) <= TOKEN_SLOTS) & (
        jnp.max(jnp.sum(new_in_section, axis=1)) <= ROW_SLOTS
    )

    wide_shape = (vocab_section + CHUNK, columns)
    wide_slots = f32((ROW_SLOTS, columns), jnp.float32)
    *hands, expand, combine = call(
        functools.partial(hand_kernel, vocab_section=vocab_section),
        (section, own_ids, cotangent), (S, V, V),
        [bf16((2, TOKEN_SLOTS, features))] * (sections // 2)
        + [bf16((TOKEN_SLOTS, ROW_SLOTS)), bf16((ROW_SLOTS, TOKEN_SLOTS))],
    )
    hands, marked = lax.optimization_barrier((hands, marked))
    plan_shape = (ROW_SLOTS + CHUNK, LANES)
    rows, plan = call(
        functools.partial(row_pick_kernel, vocab_section=vocab_section),
        (section, marked, embed_table), (S, V, pltpu.HBM),
        [bf16((groups, ROW_SLOTS, columns)), i32(plan_shape)],
        [f32(embed_table.shape, jnp.bfloat16), f32(wide_shape, jnp.float32), wide_slots],
        [pltpu.SMEM(plan_shape, jnp.int32), pltpu.SemaphoreType.DMA((4,)), pltpu.SemaphoreType.DMA],
    )
    full_rows = lax.all_to_all(rows, "dp", 0, 0, tiled=True)
    chips = sections // 2
    both = bf16((2, TOKEN_SLOTS, features))
    one = bf16((chips, TOKEN_SLOTS, features))

    def between_chips(arrays):
        return arrays[:1] + [
            lax.ppermute(a, CHIPS, [(i, i ^ k) for i in range(chips)])
            for k, a in enumerate(arrays[1:], 1)
        ]

    def from_sibling(arrays):
        (give,) = call(part_kernel, (section, *arrays), (S,) + (V,) * chips, [one])
        return lax.ppermute(give, CORES, [(0, 1), (1, 0)])

    handed = between_chips(hands)
    got = from_sibling(handed)
    by_column, *outs = call(
        functools.partial(grad_kernel, chips=chips),
        (section, full_rows, norm_gain.reshape(sections, features), expand, combine, got, *handed),
        (S,) + (V,) * (5 + chips), [bf16(full_rows.shape)] + [both] * chips,
        [f32((sections, TOKEN_SLOTS, features), jnp.bfloat16)],
    )
    home = between_chips(outs)
    back = lax.all_to_all(by_column, "dp", 0, 0, tiled=True)
    home_got = from_sibling(home)
    (fast_grad,) = call(
        functools.partial(gather_kernel, vocab_section=vocab_section),
        (section, own_ids, home_got, *home), (S,) + (V,) * (2 + chips), [bf16((tokens, features))],
    )

    def fast(plan, back, *_):
        (grad_table,) = call(
            row_add_kernel, (plan, back), (S, V),
            [bf16((vocab_section, columns))], [f32(wide_shape, jnp.float32), wide_slots],
        )
        return grad_table, jnp.zeros((tokens, features), jnp.bfloat16)

    def slow(plan, back, *operands):
        return passage(tokens, *operands)

    grad_table, slow_grad = lax.cond(
        fits, fast, slow, plan, back,
        section, all_ids, own_ids, embed_table, norm_gain, cotangent,
    )
    anywhere = pl.BlockSpec(memory_space=pl.ANY)
    own_grad = pl.pallas_call(
        settle_kernel,
        in_specs=[whole((1,), S), anywhere, anywhere],
        out_specs=anywhere,
        out_shape=bf16((tokens, features)),
        scratch_shapes=[pltpu.SemaphoreType.DMA],
        input_output_aliases={1: 0},
    )(fits.astype(jnp.int32).reshape(1), fast_grad, slow_grad)
    return grad_table, own_grad


def solution(mesh):
    split = Mesh(mesh.devices.reshape(-1, 2, mesh.shape["dp"]), (CHIPS, CORES, "dp"))
    return jax.shard_map(
        on_device,
        mesh=split,
        in_specs=(P("dp"), P(SECTION, "dp"), P(), P("dp", SECTION)),
        out_specs=(P(SECTION, "dp"), P("dp", SECTION)),
        check_vma=False,
    )
```

```python
import functools
import math

import jax
import jax.numpy as jnp
from jax import lax
from jax.experimental import pallas as pl
from jax.experimental.pallas import tpu as pltpu
from jax.sharding import Mesh
from jax.sharding import PartitionSpec as P

epsilon = 1e-05
TOKEN_SLOTS = 72
ROW_SLOTS = 32
CHUNK = 8
FRONT_EARLY = 2
BACK_EARLY = 2
REPEATED = 1 << 16
CHIPS = "section_0"
CORES = "section_1"
SECTION = (CHIPS, CORES)
LANES = 128


def whole(shape, space=pltpu.VMEM):
    if space == pltpu.HBM:
        return pl.BlockSpec(memory_space=space)
    return pl.BlockSpec(shape, lambda *_: (0,) * len(shape), memory_space=space)


def plan_kernel(section_ref, ids_ref, index_ref, count_ref, *, slots, vocab_section):
    ids = ids_ref[...].astype(jnp.float32)
    ids = jnp.concatenate([ids, ids], axis=0)
    ids = ids.T.astype(jnp.int32)
    local = ids - section_ref[0] * vocab_section
    inside = (local >= 0) & (local < vocab_section)
    before = (
        lax.broadcasted_iota(jnp.int32, (LANES, LANES), 1)
        < lax.broadcasted_iota(jnp.int32, (LANES, LANES), 0)
    )
    ones = jnp.where(inside, 1.0, 0.0)
    rank = jnp.dot(
        jnp.where(before, 1.0, 0.0).astype(jnp.bfloat16),
        ones.astype(jnp.bfloat16),
        preferred_element_type=jnp.float32,
    ).astype(jnp.int32)
    rank = jnp.where(inside, rank, -1)
    for c in range(slots):
        index_ref[pl.ds(c, 1), :] = jnp.sum(jnp.where(rank == c, local, 0), axis=0, keepdims=True)
    count_ref[...] = jnp.broadcast_to(
        jnp.sum(ones, axis=0, keepdims=True).astype(jnp.int32), count_ref.shape
    )


def pick_kernel(index_ref, table_ref, rows_ref, wide_ref, picked_ref, *, slots, groups):
    step = 256

    def widen(i, carry):
        wide_ref[pl.ds(i * step, step), :] = table_ref[pl.ds(i * step, step), :].astype(jnp.float32)
        return carry

    lax.fori_loop(0, table_ref.shape[0] // step, widen, 0)

    def group(g, carry):
        for c in range(slots):
            picked_ref[pl.ds(c, 1), :] = wide_ref[pl.ds(index_ref[c, g], 1), :]
        rows_ref[g] = picked_ref[...].astype(jnp.bfloat16)
        return carry

    lax.fori_loop(0, groups, group, 0)


def slot_of(ids_row, slots, vocab_section):
    wide = jnp.broadcast_to(ids_row // vocab_section, (LANES, LANES))
    tall = wide.astype(jnp.float32).T.astype(jnp.int32)
    first = lax.broadcasted_iota(jnp.int32, (LANES, LANES), 0)
    second = lax.broadcasted_iota(jnp.int32, (LANES, LANES), 1)
    same = wide == tall
    as_row = jnp.sum(jnp.where(same & (first < second), 1, 0), axis=0, keepdims=True)
    as_column = jnp.sum(jnp.where(same & (second < first), 1.0, 0.0), axis=1, keepdims=True)
    row_slot = jnp.where(as_row < slots, wide[:1] * slots + as_row, -1)
    as_column = as_column.astype(jnp.int32)
    column_slot = jnp.where(as_column < slots, tall[:, :1] * slots + as_column, -1)
    return row_slot, column_slot


def deal_kernel(ids_ref, cotangent_ref, dealt_ref, *, slots, sections, vocab_section):
    row_slot, _ = slot_of(ids_ref[...], slots, vocab_section)
    cotangent = cotangent_ref[...]
    for s in range(sections):
        wanted = lax.broadcasted_iota(jnp.int32, (slots, LANES), 0) + s * slots == row_slot
        dealt_ref[s] = jnp.dot(
            jnp.where(wanted, 1.0, 0.0).astype(jnp.bfloat16),
            cotangent,
            preferred_element_type=jnp.float32,
        ).astype(jnp.bfloat16)


def collect_kernel(ids_ref, dealt_ref, own_ref, *, slots, sections, vocab_section):
    _, column_slot = slot_of(ids_ref[...], slots, vocab_section)
    total = jnp.zeros(own_ref.shape, jnp.float32)
    for s in range(sections):
        wanted = lax.broadcasted_iota(jnp.int32, (LANES, slots), 1) + s * slots == column_slot
        total = total + jnp.dot(
            jnp.where(wanted, 1.0, 0.0).astype(jnp.bfloat16),
            dealt_ref[s],
            preferred_element_type=jnp.float32,
        )
    own_ref[...] = total.astype(jnp.bfloat16)


def norm_kernel(rows_ref, cotangent_ref, gain_ref, by_column_ref, by_feature_ref):
    pieces, slots, columns = rows_ref.shape
    per = cotangent_ref.shape[2] // columns
    width = pieces * columns

    def parts(k, j):
        embedded = rows_ref[k * per + j].astype(jnp.float32)
        own = cotangent_ref[k, :, j * columns : (j + 1) * columns].astype(jnp.float32)
        return embedded, own * gain_ref[pl.ds(k * per + j, 1), :]

    def sums(k, carry):
        squares, inners = carry
        for j in range(per):
            embedded, scaled = parts(k, j)
            squares = squares + embedded * embedded
            inners = inners + scaled * embedded
        return squares, inners

    zeros = jnp.zeros((slots, columns), jnp.float32)
    squares, inners = lax.fori_loop(0, pieces // per, sums, (zeros, zeros))
    square_mean = jnp.sum(squares, axis=1, keepdims=True) * (1.0 / width)
    inner = jnp.sum(inners, axis=1, keepdims=True) * (1.0 / width)
    inverse = lax.rsqrt(square_mean + epsilon)
    pull = inverse * inverse * inverse * inner

    def grads(k, carry):
        for j in range(per):
            embedded, scaled = parts(k, j)
            grad = (inverse * scaled - embedded * pull).astype(jnp.bfloat16)
            by_column_ref[k * per + j] = grad
            by_feature_ref[k, :, j * columns : (j + 1) * columns] = grad
        return carry

    lax.fori_loop(0, pieces // per, grads, 0)


def add_kernel(index_ref, count_ref, grads_ref, table_ref, total_ref, wide_ref, *, groups):
    step = 256
    slots = grads_ref.shape[1]

    def clear(i, carry):
        total_ref[pl.ds(i * step, step), :] = jnp.zeros((step, LANES), jnp.float32)
        return carry

    lax.fori_loop(0, total_ref.shape[0] // step, clear, 0)

    def group(g, carry):
        wide_ref[...] = grads_ref[g].astype(jnp.float32)

        def one(c, carry):
            row = pl.ds(index_ref[c, g], 1)
            total_ref[row, :] = total_ref[row, :] + wide_ref[pl.ds(c, 1), :]
            return carry

        lax.fori_loop(0, jnp.minimum(count_ref[0, g], slots), one, 0)
        return carry

    lax.fori_loop(0, groups, group, 0)

    def narrow(i, carry):
        table_ref[pl.ds(i * step, step), :] = total_ref[pl.ds(i * step, step), :].astype(jnp.bfloat16)
        return carry

    lax.fori_loop(0, total_ref.shape[0] // step, narrow, 0)


def call(kernel, operands, spaces, outs, scratch=(), semaphores=(), room=6):
    held = sum(math.prod(a.shape) * a.dtype.itemsize for a in (*operands, *outs, *scratch))
    return pl.pallas_call(
        kernel,
        in_specs=[whole(o.shape, s) for o, s in zip(operands, spaces)],
        out_specs=[whole(o.shape) for o in outs],
        out_shape=outs,
        scratch_shapes=[*scratch, *semaphores],
        compiler_params=pltpu.CompilerParams(vmem_limit_bytes=2 * held + (room << 20)),
    )(*operands)


def passage(slots, section, all_ids, own_ids, embed_table, norm_gain, cotangent):
    vocab_section, columns = embed_table.shape
    groups = all_ids.shape[0]
    tokens, features = cotangent.shape
    sections = lax.axis_size(SECTION)
    V, S = pltpu.VMEM, pltpu.SMEM
    bf16 = functools.partial(jax.ShapeDtypeStruct, dtype=jnp.bfloat16)
    i32 = functools.partial(jax.ShapeDtypeStruct, dtype=jnp.int32)
    (dealt,) = call(
        functools.partial(deal_kernel, slots=slots, sections=sections, vocab_section=vocab_section),
        (own_ids, cotangent), (V, V), [bf16((sections, slots, features))],
    )
    their_cotangent = lax.all_to_all(dealt, SECTION, 0, 0, tiled=True)
    index, count = call(
        functools.partial(plan_kernel, slots=slots, vocab_section=vocab_section),
        (section, all_ids), (S, V), [i32((slots, LANES)), i32((8, LANES))],
    )
    (rows,) = call(
        functools.partial(pick_kernel, slots=slots, groups=groups),
        (index, embed_table), (S, V), [bf16((groups, slots, columns))],
        [pltpu.VMEM((vocab_section, columns), jnp.float32), pltpu.VMEM((slots, columns), jnp.float32)],
    )
    full_rows = lax.all_to_all(rows, "dp", 0, 0, tiled=True)
    gain = norm_gain.reshape(groups, columns)
    by_column, by_feature = call(
        norm_kernel, (full_rows, their_cotangent, gain), (V, V, V),
        [bf16(full_rows.shape), bf16(their_cotangent.shape)],
    )
    back = lax.all_to_all(by_column, "dp", 0, 0, tiled=True)
    home = lax.all_to_all(by_feature, SECTION, 0, 0, tiled=True)
    (grad_table,) = call(
        functools.partial(add_kernel, groups=groups),
        (index, count, back), (S, S, V), [bf16((vocab_section, columns))],
        [pltpu.VMEM((vocab_section, columns), jnp.float32), pltpu.VMEM((slots, columns), jnp.float32)],
    )
    (own_grad,) = call(
        functools.partial(collect_kernel, slots=slots, sections=sections, vocab_section=vocab_section),
        (own_ids, home), (V, V), [bf16((tokens, features))],
    )
    return grad_table, own_grad


def row_plan(section, ids, plan_ref, vocab_section):
    slots = plan_ref.shape[0] - CHUNK
    ids = ids.astype(jnp.float32)
    ids = jnp.concatenate([ids, ids], axis=0)
    ids = ids.T.astype(jnp.int32)
    local = ids - section * vocab_section
    inside = (local >= 0) & (local < vocab_section) & (ids < REPEATED)
    before = (
        lax.broadcasted_iota(jnp.int32, (LANES, LANES), 1)
        < lax.broadcasted_iota(jnp.int32, (LANES, LANES), 0)
    )
    ones = jnp.where(inside, 1.0, 0.0)
    rank = jnp.dot(
        jnp.where(before, 1.0, 0.0).astype(jnp.bfloat16),
        ones.astype(jnp.bfloat16),
        preferred_element_type=jnp.float32,
    ).astype(jnp.int32)
    rank = jnp.where(inside, rank, -1)
    short = local - vocab_section
    for c in range(slots):
        plan_ref[pl.ds(c, 1), :] = vocab_section + jnp.sum(
            jnp.where(rank == c, short, 0), axis=0, keepdims=True
        )
    count = jnp.minimum(jnp.sum(ones, axis=0, keepdims=True).astype(jnp.int32), slots)
    plan_ref[pl.ds(slots, CHUNK), :] = jnp.broadcast_to((count + (CHUNK - 1)) // CHUNK, (CHUNK, LANES))


def row_pick_kernel(
    section_ref, ids_ref, table_ref, rows_ref, plan_ref,
    held_ref, wide_ref, picked_ref, steps_ref, arrived, planned, *, vocab_section
):
    groups, slots, columns = rows_ref.shape
    entries = table_ref.shape[0]
    pieces = arrived.shape[0]
    piece = entries // pieces
    copies = [
        pltpu.make_async_copy(
            table_ref.at[pl.ds(i * piece, piece)], held_ref.at[pl.ds(i * piece, piece)], arrived.at[i]
        )
        for i in range(pieces)
    ]
    for copy in copies:
        copy.start()
    row_plan(section_ref[0], ids_ref[...], plan_ref, vocab_section)
    plan_copy = pltpu.make_async_copy(plan_ref, steps_ref, planned)
    plan_copy.start()
    picked_ref[...] = jnp.zeros(picked_ref.shape, jnp.float32)
    wide_ref[pl.ds(entries, CHUNK), :] = jnp.zeros((CHUNK, columns), jnp.float32)
    step = 512

    for i, copy in enumerate(copies):
        copy.wait()

        def widen(j, carry):
            at = pl.ds(pl.multiple_of(i * piece + j * step, step), step)
            wide_ref[at, :] = held_ref[at, :].astype(jnp.float32)
            return carry

        lax.fori_loop(0, piece // step, widen, 0)
    plan_copy.wait()

    def group(g, carry):
        def chunk(i, carry):
            for j in range(CHUNK):
                c = i * CHUNK + j
                picked_ref[pl.ds(c, 1), :] = wide_ref[pl.ds(steps_ref[c, g], 1), :]
            return carry

        lax.fori_loop(0, steps_ref[slots, g], chunk, 0)
        rows_ref[g] = picked_ref[...].astype(jnp.bfloat16)
        return carry

    lax.fori_loop(0, groups, group, 0)


def row_add_kernel(plan_ref, grads_ref, table_ref, total_ref, wide_ref):
    groups, slots, columns = grads_ref.shape
    entries = table_ref.shape[0]
    step = 512

    def clear(i, carry):
        total_ref[pl.ds(i * step, step), :] = jnp.zeros((step, columns), jnp.float32)
        return carry

    lax.fori_loop(0, entries // step, clear, 0)
    total_ref[pl.ds(entries, CHUNK), :] = jnp.zeros((CHUNK, columns), jnp.float32)

    def group(g, carry):
        wide_ref[...] = grads_ref[g].astype(jnp.float32)

        def chunk(i, carry):
            rows = [pl.ds(plan_ref[i * CHUNK + j, g], 1) for j in range(CHUNK)]
            sums = [
                total_ref[row, :] + wide_ref[pl.ds(i * CHUNK + j, 1), :]
                for j, row in enumerate(rows)
            ]
            for row, value in zip(rows, sums):
                total_ref[row, :] = value
            return carry

        lax.fori_loop(0, plan_ref[slots, g], chunk, 0)
        return carry

    lax.fori_loop(0, groups, group, 0)

    def narrow(i, carry):
        table_ref[pl.ds(i * step, step), :] = total_ref[pl.ds(i * step, step), :].astype(jnp.bfloat16)
        return carry

    lax.fori_loop(0, entries // step, narrow, 0)


def both_ways(ids_row):
    wide = jnp.broadcast_to(ids_row, (LANES, LANES))
    tall = wide.astype(jnp.float32).T.astype(jnp.int32)
    down = lax.broadcasted_iota(jnp.int32, (LANES, LANES), 0)
    along = lax.broadcasted_iota(jnp.int32, (LANES, LANES), 1)
    return wide, tall, down < along, along < down


def mark_kernel(ids_ref, marked_ref):
    wide, tall, row_first, _ = both_ways(ids_ref[...])
    repeated = jnp.max(jnp.where((wide == tall) & row_first, REPEATED, 0), axis=0, keepdims=True)
    marked_ref[...] = jnp.broadcast_to((wide[:1] + repeated)[None], marked_ref.shape)


def one_hot(condition):
    return jnp.where(condition, 1.0, 0.0).astype(jnp.bfloat16)


def chip_ranks(ids_row, vocab_section):
    wide, tall, row_first, column_first = both_ways(ids_row)
    wide = wide // (2 * vocab_section)
    tall = tall // (2 * vocab_section)
    same = wide == tall
    as_row = jnp.sum(jnp.where(same & row_first, 1, 0), axis=0, keepdims=True)
    as_column = jnp.sum(jnp.where(same & column_first, 1.0, 0.0), axis=1, keepdims=True)
    return wide[:1], as_row, tall[:, :1], as_column.astype(jnp.int32)


def hand_kernel(section_ref, ids_ref, cotangent_ref, *refs, vocab_section):
    *hand_refs, expand_ref, combine_ref = refs
    token_slots, row_slots = expand_ref.shape
    section = section_ref[0]
    wide_chip, wide_rank, _, _ = chip_ranks(ids_ref[...], vocab_section)
    slot = lax.broadcasted_iota(jnp.int32, (token_slots, LANES), 0)
    cotangent = cotangent_ref[...]
    for k, hand_ref in enumerate(hand_refs):
        wanted = one_hot((slot == wide_rank) & (wide_chip == (section // 2) ^ k))
        hand_ref[...] = jnp.dot(
            wanted, cotangent, preferred_element_type=jnp.float32
        ).astype(jnp.bfloat16)

    wide, tall, row_first, column_first = both_ways(ids_ref[...])
    wide_in = wide // vocab_section == section
    tall_in = tall // vocab_section == section
    same = wide == tall
    wide_repeat = jnp.max(jnp.where(same & row_first, 1, 0), axis=0, keepdims=True)
    tall_repeat = jnp.max(jnp.where(same & column_first, 1.0, 0.0), axis=1, keepdims=True)
    wide_new = wide_in & (jnp.broadcast_to(wide_repeat, (LANES, LANES)) == 0)
    tall_new = tall_in & (jnp.broadcast_to(tall_repeat, (LANES, LANES)) == 0.0)
    own = one_hot((slot == wide_rank) & wide_in[:1])
    tall_place = jnp.sum(jnp.where(wide_new & column_first, 1.0, 0.0), axis=1, keepdims=True)
    place = jnp.sum(
        jnp.where(same & tall_new, jnp.broadcast_to(tall_place, (LANES, LANES)), 0.0), axis=0, keepdims=True
    ).astype(jnp.int32)
    place = jnp.where(wide_in[:1], place, -1)
    rows = one_hot(lax.broadcasted_iota(jnp.int32, (row_slots, LANES), 0) == place)
    over_tokens = (((1,), (1,)), ((), ()))
    expand_ref[...] = lax.dot_general(
        own, rows, over_tokens, preferred_element_type=jnp.float32
    ).astype(jnp.bfloat16)
    combine_ref[...] = lax.dot_general(
        rows, own, over_tokens, preferred_element_type=jnp.float32
    ).astype(jnp.bfloat16)


def stack_kernel(*refs):
    *part_refs, stack_ref = refs
    for k, part_ref in enumerate(part_refs):
        stack_ref[k] = part_ref[...]


def grad_kernel(section_ref, rows_ref, gain_ref, expand_ref, got_ref, *refs):
    *hand_refs, keep_ref, give_ref, embedded_ref = refs
    pieces, _, columns = rows_ref.shape
    chips, slots, features = got_ref.shape
    per = features // columns
    width = pieces * columns
    expand = expand_ref[...]
    section = section_ref[0]
    core = section % 2
    parts = []
    for k in range(chips):
        chip = (section // 2) ^ k
        parts.append((2 * chip + core, hand_refs[k], keep_ref.at[k]))
        parts.append((2 * chip + 1 - core, got_ref.at[k], give_ref.at[k]))

    squares = jnp.zeros((slots, columns), jnp.float32)
    inners = jnp.zeros((slots, columns), jnp.float32)
    for i, (s, cotangent_ref, _) in enumerate(parts):
        rows = jnp.concatenate([rows_ref[s * per + j] for j in range(per)], axis=1)
        embedded = jnp.dot(expand, rows, preferred_element_type=jnp.float32)
        embedded_ref[i] = embedded.astype(jnp.bfloat16)
        scaled = cotangent_ref[...].astype(jnp.float32) * gain_ref[pl.ds(s, 1), :]
        square = embedded * embedded
        inner = scaled * embedded
        for j in range(per):
            squares = squares + square[:, j * columns : (j + 1) * columns]
            inners = inners + inner[:, j * columns : (j + 1) * columns]
    square_mean = jnp.sum(squares, axis=1, keepdims=True) * (1.0 / width)
    inner = jnp.sum(inners, axis=1, keepdims=True) * (1.0 / width)
    own = jnp.sum(expand.astype(jnp.float32), axis=1, keepdims=True)
    inverse = jnp.where(own > 0.0, lax.rsqrt(square_mean + epsilon), 0.0)
    pull = inverse * inverse * inverse * inner

    for i, (s, cotangent_ref, out_ref) in enumerate(parts):
        scaled = cotangent_ref[...].astype(jnp.float32) * gain_ref[pl.ds(s, 1), :]
        out_ref[...] = (inverse * scaled - embedded_ref[i].astype(jnp.float32) * pull).astype(jnp.bfloat16)


def combine_kernel(section_ref, combine_ref, keep_ref, give_ref, by_column_ref):
    columns = by_column_ref.shape[2]
    chips, _, features = keep_ref.shape
    per = features // columns
    combine = combine_ref[...]
    section = section_ref[0]
    core = section % 2
    for k in range(chips):
        chip = (section // 2) ^ k
        for s, grad_ref in ((2 * chip + core, keep_ref), (2 * chip + 1 - core, give_ref)):
            added = jnp.dot(combine, grad_ref[k], preferred_element_type=jnp.float32).astype(jnp.bfloat16)
            for j in range(per):
                by_column_ref[s * per + j] = added[:, j * columns : (j + 1) * columns]


def merge_kernel(keep_ref, got_ref, *out_refs):
    for k, out_ref in enumerate(out_refs):
        out_ref[...] = (keep_ref[k].astype(jnp.float32) + got_ref[k].astype(jnp.float32)).astype(jnp.bfloat16)


def gather_kernel(section_ref, ids_ref, *refs, vocab_section):
    *home_refs, own_ref = refs
    slots = home_refs[0].shape[0]
    _, _, tall_chip, tall_rank = chip_ranks(ids_ref[...], vocab_section)
    along = lax.broadcasted_iota(jnp.int32, (LANES, slots), 1)
    total = jnp.zeros(own_ref.shape, jnp.float32)
    for k, home_ref in enumerate(home_refs):
        wanted = one_hot((along == tall_rank) & (tall_chip == (section_ref[0] // 2) ^ k))
        total = total + jnp.dot(wanted, home_ref[...], preferred_element_type=jnp.float32)
    own_ref[...] = total.astype(jnp.bfloat16)


def settle_kernel(fits_ref, fast_ref, slow_ref, out_ref, semaphore):
    @pl.when(fits_ref[0] == 0)
    def _():
        copy = pltpu.make_async_copy(slow_ref, out_ref, semaphore)
        copy.start()
        copy.wait()


def on_device(token_ids, embed_table, norm_gain, cotangent):
    vocab_section, columns = embed_table.shape
    groups = lax.axis_size("dp")
    sections = lax.axis_size(SECTION)
    tokens, features = cotangent.shape
    V, S = pltpu.VMEM, pltpu.SMEM
    bf16 = functools.partial(jax.ShapeDtypeStruct, dtype=jnp.bfloat16)
    f32 = pltpu.VMEM
    i32 = functools.partial(jax.ShapeDtypeStruct, dtype=jnp.int32)
    section = lax.axis_index(SECTION).reshape(1)
    own_ids = token_ids.reshape(1, tokens)
    (marked,) = call(mark_kernel, (own_ids,), (V,), [i32((groups, 1, tokens))])
    marked = lax.all_to_all(marked, "dp", 0, 0, tiled=True)
    chips = sections // 2
    part = bf16((TOKEN_SLOTS, features))
    parts = bf16((chips, TOKEN_SLOTS, features))

    def to_chip(k, array):
        return lax.ppermute(array, CHIPS, [(i, i ^ k) for i in range(chips)])

    def to_sibling(array):
        return lax.ppermute(array, CORES, [(0, 1), (1, 0)])

    *hands, expand, combine = call(
        functools.partial(hand_kernel, vocab_section=vocab_section),
        (section, own_ids, cotangent), (S, V, V),
        [part] * chips + [bf16((TOKEN_SLOTS, ROW_SLOTS)), bf16((ROW_SLOTS, TOKEN_SLOTS))],
    )
    handed = hands[:1] + [to_chip(k, hands[k]) for k in range(1, chips)]
    marked, handed[:FRONT_EARLY] = lax.optimization_barrier((marked, handed[:FRONT_EARLY]))
    marked = marked.reshape(groups, tokens)
    all_ids = marked % REPEATED
    in_chip = all_ids[:, :, None] // (2 * vocab_section) == jnp.arange(chips)
    in_section = all_ids[:, :, None] // vocab_section == jnp.arange(sections)
    new_in_section = in_section & (marked < REPEATED)[:, :, None]
    fits = (jnp.max(jnp.sum(in_chip, axis=1)) <= TOKEN_SLOTS) & (
        jnp.max(jnp.sum(new_in_section, axis=1)) <= ROW_SLOTS
    )

    wide_shape = (vocab_section + CHUNK, columns)
    wide_slots = f32((ROW_SLOTS, columns), jnp.float32)
    plan_shape = (ROW_SLOTS + CHUNK, LANES)
    rows, plan = call(
        functools.partial(row_pick_kernel, vocab_section=vocab_section),
        (section, marked, embed_table), (S, V, pltpu.HBM),
        [bf16((groups, ROW_SLOTS, columns)), i32(plan_shape)],
        [f32(embed_table.shape, jnp.bfloat16), f32(wide_shape, jnp.float32), wide_slots],
        [pltpu.SMEM(plan_shape, jnp.int32), pltpu.SemaphoreType.DMA((4,)), pltpu.SemaphoreType.DMA],
    )
    full_rows = lax.all_to_all(rows, "dp", 0, 0, tiled=True)
    (stack,) = call(stack_kernel, tuple(handed), (V,) * chips, [parts])
    got = to_sibling(stack)
    keep, give = call(
        grad_kernel,
        (section, full_rows, norm_gain.reshape(sections, features), expand, got, *handed),
        (S,) + (V,) * (4 + chips), [parts, parts],
        [f32((sections, TOKEN_SLOTS, features), jnp.bfloat16)],
    )
    (by_column,) = call(
        combine_kernel, (section, combine, keep, give), (S, V, V, V), [bf16(full_rows.shape)]
    )
    outs = call(merge_kernel, (keep, to_sibling(give)), (V, V), [part] * chips)
    home = [outs[0]] + [to_chip(k, outs[k]) for k in range(1, chips)]
    by_column, home[:BACK_EARLY] = lax.optimization_barrier((by_column, home[:BACK_EARLY]))
    back = lax.all_to_all(by_column, "dp", 0, 0, tiled=True)
    (fast_grad,) = call(
        functools.partial(gather_kernel, vocab_section=vocab_section),
        (section, own_ids, *home), (S,) + (V,) * (1 + chips), [bf16((tokens, features))],
    )

    def fast(plan, back, *_):
        (grad_table,) = call(
            row_add_kernel, (plan, back), (S, V),
            [bf16((vocab_section, columns))], [f32(wide_shape, jnp.float32), wide_slots],
        )
        return grad_table, jnp.zeros((tokens, features), jnp.bfloat16)

    def slow(plan, back, *operands):
        return passage(tokens, *operands)

    grad_table, slow_grad = lax.cond(
        fits, fast, slow, plan, back,
        section, all_ids, own_ids, embed_table, norm_gain, cotangent,
    )
    anywhere = pl.BlockSpec(memory_space=pl.ANY)
    own_grad = pl.pallas_call(
        settle_kernel,
        in_specs=[whole((1,), S), anywhere, anywhere],
        out_specs=anywhere,
        out_shape=bf16((tokens, features)),
        scratch_shapes=[pltpu.SemaphoreType.DMA],
        input_output_aliases={1: 0},
    )(fits.astype(jnp.int32).reshape(1), fast_grad, slow_grad)
    return grad_table, own_grad


def solution(mesh):
    split = Mesh(mesh.devices.reshape(-1, 2, mesh.shape["dp"]), (CHIPS, CORES, "dp"))
    return jax.shard_map(
        on_device,
        mesh=split,
        in_specs=(P("dp"), P(SECTION, "dp"), P(), P("dp", SECTION)),
        out_specs=(P(SECTION, "dp"), P("dp", SECTION)),
        check_vma=False,
    )
```

```python
import functools
import math

import jax
import jax.numpy as jnp
from jax import lax
from jax.experimental import pallas as pl
from jax.experimental.pallas import tpu as pltpu
from jax.sharding import Mesh
from jax.sharding import PartitionSpec as P

epsilon = 1e-05
TOKEN_SLOTS = 72
ROW_SLOTS = 32
CHUNK = 8
FAR_FIRST = (2, 1, 3)
EARLY = 2
REPEATED = 1 << 16
CHIPS = "section_0"
CORES = "section_1"
SECTION = (CHIPS, CORES)
LANES = 128


def whole(shape, space=pltpu.VMEM):
    if space == pltpu.HBM:
        return pl.BlockSpec(memory_space=space)
    return pl.BlockSpec(shape, lambda *_: (0,) * len(shape), memory_space=space)


def plan_kernel(section_ref, ids_ref, index_ref, count_ref, *, slots, vocab_section):
    ids = ids_ref[...].astype(jnp.float32)
    ids = jnp.concatenate([ids, ids], axis=0)
    ids = ids.T.astype(jnp.int32)
    local = ids - section_ref[0] * vocab_section
    inside = (local >= 0) & (local < vocab_section)
    before = (
        lax.broadcasted_iota(jnp.int32, (LANES, LANES), 1)
        < lax.broadcasted_iota(jnp.int32, (LANES, LANES), 0)
    )
    ones = jnp.where(inside, 1.0, 0.0)
    rank = jnp.dot(
        jnp.where(before, 1.0, 0.0).astype(jnp.bfloat16),
        ones.astype(jnp.bfloat16),
        preferred_element_type=jnp.float32,
    ).astype(jnp.int32)
    rank = jnp.where(inside, rank, -1)
    for c in range(slots):
        index_ref[pl.ds(c, 1), :] = jnp.sum(jnp.where(rank == c, local, 0), axis=0, keepdims=True)
    count_ref[...] = jnp.broadcast_to(
        jnp.sum(ones, axis=0, keepdims=True).astype(jnp.int32), count_ref.shape
    )


def pick_kernel(index_ref, table_ref, rows_ref, wide_ref, picked_ref, *, slots, groups):
    step = 256

    def widen(i, carry):
        wide_ref[pl.ds(i * step, step), :] = table_ref[pl.ds(i * step, step), :].astype(jnp.float32)
        return carry

    lax.fori_loop(0, table_ref.shape[0] // step, widen, 0)

    def group(g, carry):
        for c in range(slots):
            picked_ref[pl.ds(c, 1), :] = wide_ref[pl.ds(index_ref[c, g], 1), :]
        rows_ref[g] = picked_ref[...].astype(jnp.bfloat16)
        return carry

    lax.fori_loop(0, groups, group, 0)


def slot_of(ids_row, slots, vocab_section):
    wide = jnp.broadcast_to(ids_row // vocab_section, (LANES, LANES))
    tall = wide.astype(jnp.float32).T.astype(jnp.int32)
    first = lax.broadcasted_iota(jnp.int32, (LANES, LANES), 0)
    second = lax.broadcasted_iota(jnp.int32, (LANES, LANES), 1)
    same = wide == tall
    as_row = jnp.sum(jnp.where(same & (first < second), 1, 0), axis=0, keepdims=True)
    as_column = jnp.sum(jnp.where(same & (second < first), 1.0, 0.0), axis=1, keepdims=True)
    row_slot = jnp.where(as_row < slots, wide[:1] * slots + as_row, -1)
    as_column = as_column.astype(jnp.int32)
    column_slot = jnp.where(as_column < slots, tall[:, :1] * slots + as_column, -1)
    return row_slot, column_slot


def deal_kernel(ids_ref, cotangent_ref, dealt_ref, *, slots, sections, vocab_section):
    row_slot, _ = slot_of(ids_ref[...], slots, vocab_section)
    cotangent = cotangent_ref[...]
    for s in range(sections):
        wanted = lax.broadcasted_iota(jnp.int32, (slots, LANES), 0) + s * slots == row_slot
        dealt_ref[s] = jnp.dot(
            jnp.where(wanted, 1.0, 0.0).astype(jnp.bfloat16),
            cotangent,
            preferred_element_type=jnp.float32,
        ).astype(jnp.bfloat16)


def collect_kernel(ids_ref, dealt_ref, own_ref, *, slots, sections, vocab_section):
    _, column_slot = slot_of(ids_ref[...], slots, vocab_section)
    total = jnp.zeros(own_ref.shape, jnp.float32)
    for s in range(sections):
        wanted = lax.broadcasted_iota(jnp.int32, (LANES, slots), 1) + s * slots == column_slot
        total = total + jnp.dot(
            jnp.where(wanted, 1.0, 0.0).astype(jnp.bfloat16),
            dealt_ref[s],
            preferred_element_type=jnp.float32,
        )
    own_ref[...] = total.astype(jnp.bfloat16)


def norm_kernel(rows_ref, cotangent_ref, gain_ref, by_column_ref, by_feature_ref):
    pieces, slots, columns = rows_ref.shape
    per = cotangent_ref.shape[2] // columns
    width = pieces * columns

    def parts(k, j):
        embedded = rows_ref[k * per + j].astype(jnp.float32)
        own = cotangent_ref[k, :, j * columns : (j + 1) * columns].astype(jnp.float32)
        return embedded, own * gain_ref[pl.ds(k * per + j, 1), :]

    def sums(k, carry):
        squares, inners = carry
        for j in range(per):
            embedded, scaled = parts(k, j)
            squares = squares + embedded * embedded
            inners = inners + scaled * embedded
        return squares, inners

    zeros = jnp.zeros((slots, columns), jnp.float32)
    squares, inners = lax.fori_loop(0, pieces // per, sums, (zeros, zeros))
    square_mean = jnp.sum(squares, axis=1, keepdims=True) * (1.0 / width)
    inner = jnp.sum(inners, axis=1, keepdims=True) * (1.0 / width)
    inverse = lax.rsqrt(square_mean + epsilon)
    pull = inverse * inverse * inverse * inner

    def grads(k, carry):
        for j in range(per):
            embedded, scaled = parts(k, j)
            grad = (inverse * scaled - embedded * pull).astype(jnp.bfloat16)
            by_column_ref[k * per + j] = grad
            by_feature_ref[k, :, j * columns : (j + 1) * columns] = grad
        return carry

    lax.fori_loop(0, pieces // per, grads, 0)


def add_kernel(index_ref, count_ref, grads_ref, table_ref, total_ref, wide_ref, *, groups):
    step = 256
    slots = grads_ref.shape[1]

    def clear(i, carry):
        total_ref[pl.ds(i * step, step), :] = jnp.zeros((step, LANES), jnp.float32)
        return carry

    lax.fori_loop(0, total_ref.shape[0] // step, clear, 0)

    def group(g, carry):
        wide_ref[...] = grads_ref[g].astype(jnp.float32)

        def one(c, carry):
            row = pl.ds(index_ref[c, g], 1)
            total_ref[row, :] = total_ref[row, :] + wide_ref[pl.ds(c, 1), :]
            return carry

        lax.fori_loop(0, jnp.minimum(count_ref[0, g], slots), one, 0)
        return carry

    lax.fori_loop(0, groups, group, 0)

    def narrow(i, carry):
        table_ref[pl.ds(i * step, step), :] = total_ref[pl.ds(i * step, step), :].astype(jnp.bfloat16)
        return carry

    lax.fori_loop(0, total_ref.shape[0] // step, narrow, 0)


def call(kernel, operands, spaces, outs, scratch=(), semaphores=(), room=6):
    held = sum(math.prod(a.shape) * a.dtype.itemsize for a in (*operands, *outs, *scratch))
    return pl.pallas_call(
        kernel,
        in_specs=[whole(o.shape, s) for o, s in zip(operands, spaces)],
        out_specs=[whole(o.shape) for o in outs],
        out_shape=outs,
        scratch_shapes=[*scratch, *semaphores],
        compiler_params=pltpu.CompilerParams(vmem_limit_bytes=2 * held + (room << 20)),
    )(*operands)


def passage(slots, section, all_ids, own_ids, embed_table, norm_gain, cotangent):
    vocab_section, columns = embed_table.shape
    groups = all_ids.shape[0]
    tokens, features = cotangent.shape
    sections = lax.axis_size(SECTION)
    V, S = pltpu.VMEM, pltpu.SMEM
    bf16 = functools.partial(jax.ShapeDtypeStruct, dtype=jnp.bfloat16)
    i32 = functools.partial(jax.ShapeDtypeStruct, dtype=jnp.int32)
    (dealt,) = call(
        functools.partial(deal_kernel, slots=slots, sections=sections, vocab_section=vocab_section),
        (own_ids, cotangent), (V, V), [bf16((sections, slots, features))],
    )
    their_cotangent = lax.all_to_all(dealt, SECTION, 0, 0, tiled=True)
    index, count = call(
        functools.partial(plan_kernel, slots=slots, vocab_section=vocab_section),
        (section, all_ids), (S, V), [i32((slots, LANES)), i32((8, LANES))],
    )
    (rows,) = call(
        functools.partial(pick_kernel, slots=slots, groups=groups),
        (index, embed_table), (S, V), [bf16((groups, slots, columns))],
        [pltpu.VMEM((vocab_section, columns), jnp.float32), pltpu.VMEM((slots, columns), jnp.float32)],
    )
    full_rows = lax.all_to_all(rows, "dp", 0, 0, tiled=True)
    gain = norm_gain.reshape(groups, columns)
    by_column, by_feature = call(
        norm_kernel, (full_rows, their_cotangent, gain), (V, V, V),
        [bf16(full_rows.shape), bf16(their_cotangent.shape)],
    )
    back = lax.all_to_all(by_column, "dp", 0, 0, tiled=True)
    home = lax.all_to_all(by_feature, SECTION, 0, 0, tiled=True)
    (grad_table,) = call(
        functools.partial(add_kernel, groups=groups),
        (index, count, back), (S, S, V), [bf16((vocab_section, columns))],
        [pltpu.VMEM((vocab_section, columns), jnp.float32), pltpu.VMEM((slots, columns), jnp.float32)],
    )
    (own_grad,) = call(
        functools.partial(collect_kernel, slots=slots, sections=sections, vocab_section=vocab_section),
        (own_ids, home), (V, V), [bf16((tokens, features))],
    )
    return grad_table, own_grad


def row_plan(section, ids, plan_ref, vocab_section):
    slots = plan_ref.shape[0] - CHUNK
    ids = ids.astype(jnp.float32)
    ids = jnp.concatenate([ids, ids], axis=0)
    ids = ids.T.astype(jnp.int32)
    local = ids - section * vocab_section
    inside = (local >= 0) & (local < vocab_section) & (ids < REPEATED)
    before = (
        lax.broadcasted_iota(jnp.int32, (LANES, LANES), 1)
        < lax.broadcasted_iota(jnp.int32, (LANES, LANES), 0)
    )
    ones = jnp.where(inside, 1.0, 0.0)
    rank = jnp.dot(
        jnp.where(before, 1.0, 0.0).astype(jnp.bfloat16),
        ones.astype(jnp.bfloat16),
        preferred_element_type=jnp.float32,
    ).astype(jnp.int32)
    rank = jnp.where(inside, rank, -1)
    short = local - vocab_section
    for c in range(slots):
        plan_ref[pl.ds(c, 1), :] = vocab_section + jnp.sum(
            jnp.where(rank == c, short, 0), axis=0, keepdims=True
        )
    count = jnp.minimum(jnp.sum(ones, axis=0, keepdims=True).astype(jnp.int32), slots)
    plan_ref[pl.ds(slots, CHUNK), :] = jnp.broadcast_to((count + (CHUNK - 1)) // CHUNK, (CHUNK, LANES))


def row_pick_kernel(
    section_ref, ids_ref, table_ref, rows_ref, plan_ref,
    held_ref, wide_ref, picked_ref, steps_ref, arrived, planned, *, vocab_section
):
    groups, slots, columns = rows_ref.shape
    entries = table_ref.shape[0]
    pieces = arrived.shape[0]
    piece = entries // pieces
    copies = [
        pltpu.make_async_copy(
            table_ref.at[pl.ds(i * piece, piece)], held_ref.at[pl.ds(i * piece, piece)], arrived.at[i]
        )
        for i in range(pieces)
    ]
    for copy in copies:
        copy.start()
    row_plan(section_ref[0], ids_ref[...], plan_ref, vocab_section)
    plan_copy = pltpu.make_async_copy(plan_ref, steps_ref, planned)
    plan_copy.start()
    picked_ref[...] = jnp.zeros(picked_ref.shape, jnp.float32)
    wide_ref[pl.ds(entries, CHUNK), :] = jnp.zeros((CHUNK, columns), jnp.float32)
    step = 512

    for i, copy in enumerate(copies):
        copy.wait()

        def widen(j, carry):
            at = pl.ds(pl.multiple_of(i * piece + j * step, step), step)
            wide_ref[at, :] = held_ref[at, :].astype(jnp.float32)
            return carry

        lax.fori_loop(0, piece // step, widen, 0)
    plan_copy.wait()

    def group(g, carry):
        def chunk(i, carry):
            for j in range(CHUNK):
                c = i * CHUNK + j
                picked_ref[pl.ds(c, 1), :] = wide_ref[pl.ds(steps_ref[c, g], 1), :]
            return carry

        lax.fori_loop(0, steps_ref[slots, g], chunk, 0)
        rows_ref[g] = picked_ref[...].astype(jnp.bfloat16)
        return carry

    lax.fori_loop(0, groups, group, 0)


def row_add_kernel(plan_ref, grads_ref, table_ref, total_ref, wide_ref):
    groups, slots, columns = grads_ref.shape
    entries = table_ref.shape[0]
    step = 512

    def clear(i, carry):
        total_ref[pl.ds(i * step, step), :] = jnp.zeros((step, columns), jnp.float32)
        return carry

    lax.fori_loop(0, entries // step, clear, 0)
    total_ref[pl.ds(entries, CHUNK), :] = jnp.zeros((CHUNK, columns), jnp.float32)

    def group(g, carry):
        wide_ref[...] = grads_ref[g].astype(jnp.float32)

        def chunk(i, carry):
            rows = [pl.ds(plan_ref[i * CHUNK + j, g], 1) for j in range(CHUNK)]
            sums = [
                total_ref[row, :] + wide_ref[pl.ds(i * CHUNK + j, 1), :]
                for j, row in enumerate(rows)
            ]
            for row, value in zip(rows, sums):
                total_ref[row, :] = value
            return carry

        lax.fori_loop(0, plan_ref[slots, g], chunk, 0)
        return carry

    lax.fori_loop(0, groups, group, 0)

    def narrow(i, carry):
        table_ref[pl.ds(i * step, step), :] = total_ref[pl.ds(i * step, step), :].astype(jnp.bfloat16)
        return carry

    lax.fori_loop(0, entries // step, narrow, 0)


def both_ways(ids_row):
    wide = jnp.broadcast_to(ids_row, (LANES, LANES))
    tall = wide.astype(jnp.float32).T.astype(jnp.int32)
    down = lax.broadcasted_iota(jnp.int32, (LANES, LANES), 0)
    along = lax.broadcasted_iota(jnp.int32, (LANES, LANES), 1)
    return wide, tall, down < along, along < down


def mark_kernel(ids_ref, marked_ref):
    wide, tall, row_first, _ = both_ways(ids_ref[...])
    repeated = jnp.max(jnp.where((wide == tall) & row_first, REPEATED, 0), axis=0, keepdims=True)
    marked_ref[...] = jnp.broadcast_to((wide[:1] + repeated)[None], marked_ref.shape)


def one_hot(condition):
    return jnp.where(condition, 1.0, 0.0).astype(jnp.bfloat16)


def chip_ranks(ids_row, vocab_section):
    wide, tall, row_first, column_first = both_ways(ids_row)
    wide = wide // (2 * vocab_section)
    tall = tall // (2 * vocab_section)
    same = wide == tall
    as_row = jnp.sum(jnp.where(same & row_first, 1, 0), axis=0, keepdims=True)
    as_column = jnp.sum(jnp.where(same & column_first, 1.0, 0.0), axis=1, keepdims=True)
    return wide[:1], as_row, tall[:, :1], as_column.astype(jnp.int32)


def hand_kernel(section_ref, ids_ref, cotangent_ref, *refs, vocab_section):
    *hand_refs, expand_ref, combine_ref = refs
    token_slots, row_slots = expand_ref.shape
    section = section_ref[0]
    wide_chip, wide_rank, _, _ = chip_ranks(ids_ref[...], vocab_section)
    slot = lax.broadcasted_iota(jnp.int32, (token_slots, LANES), 0)
    cotangent = cotangent_ref[...]
    for k, hand_ref in enumerate(hand_refs):
        wanted = one_hot((slot == wide_rank) & (wide_chip == (section // 2) ^ k))
        hand_ref[...] = jnp.dot(
            wanted, cotangent, preferred_element_type=jnp.float32
        ).astype(jnp.bfloat16)

    wide, tall, row_first, column_first = both_ways(ids_ref[...])
    wide_in = wide // vocab_section == section
    tall_in = tall // vocab_section == section
    same = wide == tall
    wide_repeat = jnp.max(jnp.where(same & row_first, 1, 0), axis=0, keepdims=True)
    tall_repeat = jnp.max(jnp.where(same & column_first, 1.0, 0.0), axis=1, keepdims=True)
    wide_new = wide_in & (jnp.broadcast_to(wide_repeat, (LANES, LANES)) == 0)
    tall_new = tall_in & (jnp.broadcast_to(tall_repeat, (LANES, LANES)) == 0.0)
    own = one_hot((slot == wide_rank) & wide_in[:1])
    tall_place = jnp.sum(jnp.where(wide_new & column_first, 1.0, 0.0), axis=1, keepdims=True)
    place = jnp.sum(
        jnp.where(same & tall_new, jnp.broadcast_to(tall_place, (LANES, LANES)), 0.0), axis=0, keepdims=True
    ).astype(jnp.int32)
    place = jnp.where(wide_in[:1], place, -1)
    rows = one_hot(lax.broadcasted_iota(jnp.int32, (row_slots, LANES), 0) == place)
    over_tokens = (((1,), (1,)), ((), ()))
    expand_ref[...] = lax.dot_general(
        own, rows, over_tokens, preferred_element_type=jnp.float32
    ).astype(jnp.bfloat16)
    combine_ref[...] = lax.dot_general(
        rows, own, over_tokens, preferred_element_type=jnp.float32
    ).astype(jnp.bfloat16)


def stack_kernel(*refs):
    *part_refs, stack_ref = refs
    for k, part_ref in enumerate(part_refs):
        stack_ref[k] = part_ref[...]


def grad_kernel(section_ref, rows_ref, gain_ref, expand_ref, got_ref, *refs):
    *hand_refs, keep_ref, give_ref, embedded_ref = refs
    pieces, _, columns = rows_ref.shape
    chips, slots, features = got_ref.shape
    per = features // columns
    width = pieces * columns
    expand = expand_ref[...]
    section = section_ref[0]
    core = section % 2
    parts = []
    for k in range(chips):
        chip = (section // 2) ^ k
        parts.append((2 * chip + core, hand_refs[k], keep_ref.at[k]))
        parts.append((2 * chip + 1 - core, got_ref.at[k], give_ref.at[k]))

    squares = jnp.zeros((slots, columns), jnp.float32)
    inners = jnp.zeros((slots, columns), jnp.float32)
    for i, (s, cotangent_ref, _) in enumerate(parts):
        rows = jnp.concatenate([rows_ref[s * per + j] for j in range(per)], axis=1)
        embedded = jnp.dot(expand, rows, preferred_element_type=jnp.float32)
        embedded_ref[i] = embedded.astype(jnp.bfloat16)
        scaled = cotangent_ref[...].astype(jnp.float32) * gain_ref[pl.ds(s, 1), :]
        square = embedded * embedded
        inner = scaled * embedded
        for j in range(per):
            squares = squares + square[:, j * columns : (j + 1) * columns]
            inners = inners + inner[:, j * columns : (j + 1) * columns]
    square_mean = jnp.sum(squares, axis=1, keepdims=True) * (1.0 / width)
    inner = jnp.sum(inners, axis=1, keepdims=True) * (1.0 / width)
    own = jnp.sum(expand.astype(jnp.float32), axis=1, keepdims=True)
    inverse = jnp.where(own > 0.0, lax.rsqrt(square_mean + epsilon), 0.0)
    pull = inverse * inverse * inverse * inner

    for i, (s, cotangent_ref, out_ref) in enumerate(parts):
        scaled = cotangent_ref[...].astype(jnp.float32) * gain_ref[pl.ds(s, 1), :]
        out_ref[...] = (inverse * scaled - embedded_ref[i].astype(jnp.float32) * pull).astype(jnp.bfloat16)


def combine_kernel(section_ref, combine_ref, keep_ref, give_ref, by_column_ref):
    columns = by_column_ref.shape[2]
    chips, _, features = keep_ref.shape
    per = features // columns
    combine = combine_ref[...]
    section = section_ref[0]
    core = section % 2
    for k in range(chips):
        chip = (section // 2) ^ k
        for s, grad_ref in ((2 * chip + core, keep_ref), (2 * chip + 1 - core, give_ref)):
            added = jnp.dot(combine, grad_ref[k], preferred_element_type=jnp.float32).astype(jnp.bfloat16)
            for j in range(per):
                by_column_ref[s * per + j] = added[:, j * columns : (j + 1) * columns]


def merge_kernel(keep_ref, got_ref, *out_refs):
    for k, out_ref in enumerate(out_refs):
        out_ref[...] = (keep_ref[k].astype(jnp.float32) + got_ref[k].astype(jnp.float32)).astype(jnp.bfloat16)


def gather_kernel(section_ref, ids_ref, *refs, vocab_section):
    *home_refs, own_ref = refs
    slots = home_refs[0].shape[0]
    _, _, tall_chip, tall_rank = chip_ranks(ids_ref[...], vocab_section)
    along = lax.broadcasted_iota(jnp.int32, (LANES, slots), 1)
    total = jnp.zeros(own_ref.shape, jnp.float32)
    for k, home_ref in enumerate(home_refs):
        wanted = one_hot((along == tall_rank) & (tall_chip == (section_ref[0] // 2) ^ k))
        total = total + jnp.dot(wanted, home_ref[...], preferred_element_type=jnp.float32)
    own_ref[...] = total.astype(jnp.bfloat16)


def settle_kernel(fits_ref, fast_ref, slow_ref, out_ref, semaphore):
    @pl.when(fits_ref[0] == 0)
    def _():
        copy = pltpu.make_async_copy(slow_ref, out_ref, semaphore)
        copy.start()
        copy.wait()


def in_order(own, travelled):
    return [own[0]] + [travelled[FAR_FIRST.index(k)] for k in range(1, len(own))]


def on_device(token_ids, embed_table, norm_gain, cotangent):
    vocab_section, columns = embed_table.shape
    groups = lax.axis_size("dp")
    sections = lax.axis_size(SECTION)
    tokens, features = cotangent.shape
    V, S = pltpu.VMEM, pltpu.SMEM
    bf16 = functools.partial(jax.ShapeDtypeStruct, dtype=jnp.bfloat16)
    f32 = pltpu.VMEM
    i32 = functools.partial(jax.ShapeDtypeStruct, dtype=jnp.int32)
    section = lax.axis_index(SECTION).reshape(1)
    own_ids = token_ids.reshape(1, tokens)
    (marked,) = call(mark_kernel, (own_ids,), (V,), [i32((groups, 1, tokens))])
    marked = lax.all_to_all(marked, "dp", 0, 0, tiled=True)
    chips = sections // 2
    part = bf16((TOKEN_SLOTS, features))
    parts = bf16((chips, TOKEN_SLOTS, features))

    def to_chip(k, array):
        return lax.ppermute(array, CHIPS, [(i, i ^ k) for i in range(chips)])

    def to_sibling(array):
        return lax.ppermute(array, CORES, [(0, 1), (1, 0)])

    *hands, expand, combine = call(
        functools.partial(hand_kernel, vocab_section=vocab_section),
        (section, own_ids, cotangent), (S, V, V),
        [part] * chips + [bf16((TOKEN_SLOTS, ROW_SLOTS)), bf16((ROW_SLOTS, TOKEN_SLOTS))],
    )
    handed = [to_chip(k, hands[k]) for k in FAR_FIRST]
    marked, handed[:EARLY] = lax.optimization_barrier((marked, handed[:EARLY]))
    handed = in_order(hands, handed)
    marked = marked.reshape(groups, tokens)
    all_ids = marked % REPEATED
    in_chip = all_ids[:, :, None] // (2 * vocab_section) == jnp.arange(chips)
    in_section = all_ids[:, :, None] // vocab_section == jnp.arange(sections)
    new_in_section = in_section & (marked < REPEATED)[:, :, None]
    fits = (jnp.max(jnp.sum(in_chip, axis=1)) <= TOKEN_SLOTS) & (
        jnp.max(jnp.sum(new_in_section, axis=1)) <= ROW_SLOTS
    )

    wide_shape = (vocab_section + CHUNK, columns)
    wide_slots = f32((ROW_SLOTS, columns), jnp.float32)
    plan_shape = (ROW_SLOTS + CHUNK, LANES)
    rows, plan = call(
        functools.partial(row_pick_kernel, vocab_section=vocab_section),
        (section, marked, embed_table), (S, V, pltpu.HBM),
        [bf16((groups, ROW_SLOTS, columns)), i32(plan_shape)],
        [f32(embed_table.shape, jnp.bfloat16), f32(wide_shape, jnp.float32), wide_slots],
        [pltpu.SMEM(plan_shape, jnp.int32), pltpu.SemaphoreType.DMA((4,)), pltpu.SemaphoreType.DMA],
    )
    full_rows = lax.all_to_all(rows, "dp", 0, 0, tiled=True)
    fits, full_rows = lax.optimization_barrier((fits, full_rows))
    (stack,) = call(stack_kernel, tuple(handed), (V,) * chips, [parts])
    got = to_sibling(stack)
    keep, give = call(
        grad_kernel,
        (section, full_rows, norm_gain.reshape(sections, features), expand, got, *handed),
        (S,) + (V,) * (4 + chips), [parts, parts],
        [f32((sections, TOKEN_SLOTS, features), jnp.bfloat16)],
    )
    (by_column,) = call(
        combine_kernel, (section, combine, keep, give), (S, V, V, V), [bf16(full_rows.shape)]
    )
    outs = call(merge_kernel, (keep, to_sibling(give)), (V, V), [part] * chips)
    by_column, outs = lax.optimization_barrier((by_column, list(outs)))
    home = [to_chip(k, outs[k]) for k in FAR_FIRST]
    back = lax.all_to_all(by_column, "dp", 0, 0, tiled=True)

    def fast(plan, back, *_):
        (grad_table,) = call(
            row_add_kernel, (plan, back), (S, V),
            [bf16((vocab_section, columns))], [f32(wide_shape, jnp.float32), wide_slots],
        )
        return grad_table, jnp.zeros((tokens, features), jnp.bfloat16)

    def slow(plan, back, *operands):
        return passage(tokens, *operands)

    grad_table, slow_grad = lax.cond(
        fits, fast, slow, plan, back,
        section, all_ids, own_ids, embed_table, norm_gain, cotangent,
    )
    grad_table, slow_grad, home = lax.optimization_barrier((grad_table, slow_grad, home))
    (fast_grad,) = call(
        functools.partial(gather_kernel, vocab_section=vocab_section),
        (section, own_ids, *in_order(outs, home)), (S,) + (V,) * (1 + chips), [bf16((tokens, features))],
    )
    anywhere = pl.BlockSpec(memory_space=pl.ANY)
    own_grad = pl.pallas_call(
        settle_kernel,
        in_specs=[whole((1,), S), anywhere, anywhere],
        out_specs=anywhere,
        out_shape=bf16((tokens, features)),
        scratch_shapes=[pltpu.SemaphoreType.DMA],
        input_output_aliases={1: 0},
    )(fits.astype(jnp.int32).reshape(1), fast_grad, slow_grad)
    return grad_table, own_grad


def solution(mesh):
    split = Mesh(mesh.devices.reshape(-1, 2, mesh.shape["dp"]), (CHIPS, CORES, "dp"))
    return jax.shard_map(
        on_device,
        mesh=split,
        in_specs=(P("dp"), P(SECTION, "dp"), P(), P("dp", SECTION)),
        out_specs=(P(SECTION, "dp"), P("dp", SECTION)),
        check_vma=False,
    )
```

```python
import functools
import math

import jax
import jax.numpy as jnp
from jax import lax
from jax.experimental import pallas as pl
from jax.experimental.pallas import tpu as pltpu
from jax.sharding import Mesh
from jax.sharding import PartitionSpec as P

epsilon = 1e-05
TOKEN_SLOTS = 72
ROW_SLOTS = 32
CHUNK = 8
FAR_FIRST = (2, 1, 3)
EARLY = 1
REPEATED = 1 << 16
CHIPS = "section_0"
CORES = "section_1"
SECTION = (CHIPS, CORES)
LANES = 128


def whole(shape, space=pltpu.VMEM):
    if space == pltpu.HBM:
        return pl.BlockSpec(memory_space=space)
    return pl.BlockSpec(shape, lambda *_: (0,) * len(shape), memory_space=space)


def plan_kernel(section_ref, ids_ref, index_ref, count_ref, *, slots, vocab_section):
    ids = ids_ref[...].astype(jnp.float32)
    ids = jnp.concatenate([ids, ids], axis=0)
    ids = ids.T.astype(jnp.int32)
    local = ids - section_ref[0] * vocab_section
    inside = (local >= 0) & (local < vocab_section)
    before = (
        lax.broadcasted_iota(jnp.int32, (LANES, LANES), 1)
        < lax.broadcasted_iota(jnp.int32, (LANES, LANES), 0)
    )
    ones = jnp.where(inside, 1.0, 0.0)
    rank = jnp.dot(
        jnp.where(before, 1.0, 0.0).astype(jnp.bfloat16),
        ones.astype(jnp.bfloat16),
        preferred_element_type=jnp.float32,
    ).astype(jnp.int32)
    rank = jnp.where(inside, rank, -1)
    for c in range(slots):
        index_ref[pl.ds(c, 1), :] = jnp.sum(jnp.where(rank == c, local, 0), axis=0, keepdims=True)
    count_ref[...] = jnp.broadcast_to(
        jnp.sum(ones, axis=0, keepdims=True).astype(jnp.int32), count_ref.shape
    )


def pick_kernel(index_ref, table_ref, rows_ref, wide_ref, picked_ref, *, slots, groups):
    step = 256

    def widen(i, carry):
        wide_ref[pl.ds(i * step, step), :] = table_ref[pl.ds(i * step, step), :].astype(jnp.float32)
        return carry

    lax.fori_loop(0, table_ref.shape[0] // step, widen, 0)

    def group(g, carry):
        for c in range(slots):
            picked_ref[pl.ds(c, 1), :] = wide_ref[pl.ds(index_ref[c, g], 1), :]
        rows_ref[g] = picked_ref[...].astype(jnp.bfloat16)
        return carry

    lax.fori_loop(0, groups, group, 0)


def slot_of(ids_row, slots, vocab_section):
    wide = jnp.broadcast_to(ids_row // vocab_section, (LANES, LANES))
    tall = wide.astype(jnp.float32).T.astype(jnp.int32)
    first = lax.broadcasted_iota(jnp.int32, (LANES, LANES), 0)
    second = lax.broadcasted_iota(jnp.int32, (LANES, LANES), 1)
    same = wide == tall
    as_row = jnp.sum(jnp.where(same & (first < second), 1, 0), axis=0, keepdims=True)
    as_column = jnp.sum(jnp.where(same & (second < first), 1.0, 0.0), axis=1, keepdims=True)
    row_slot = jnp.where(as_row < slots, wide[:1] * slots + as_row, -1)
    as_column = as_column.astype(jnp.int32)
    column_slot = jnp.where(as_column < slots, tall[:, :1] * slots + as_column, -1)
    return row_slot, column_slot


def deal_kernel(ids_ref, cotangent_ref, dealt_ref, *, slots, sections, vocab_section):
    row_slot, _ = slot_of(ids_ref[...], slots, vocab_section)
    cotangent = cotangent_ref[...]
    for s in range(sections):
        wanted = lax.broadcasted_iota(jnp.int32, (slots, LANES), 0) + s * slots == row_slot
        dealt_ref[s] = jnp.dot(
            jnp.where(wanted, 1.0, 0.0).astype(jnp.bfloat16),
            cotangent,
            preferred_element_type=jnp.float32,
        ).astype(jnp.bfloat16)


def collect_kernel(ids_ref, dealt_ref, own_ref, *, slots, sections, vocab_section):
    _, column_slot = slot_of(ids_ref[...], slots, vocab_section)
    total = jnp.zeros(own_ref.shape, jnp.float32)
    for s in range(sections):
        wanted = lax.broadcasted_iota(jnp.int32, (LANES, slots), 1) + s * slots == column_slot
        total = total + jnp.dot(
            jnp.where(wanted, 1.0, 0.0).astype(jnp.bfloat16),
            dealt_ref[s],
            preferred_element_type=jnp.float32,
        )
    own_ref[...] = total.astype(jnp.bfloat16)


def norm_kernel(rows_ref, cotangent_ref, gain_ref, by_column_ref, by_feature_ref):
    pieces, slots, columns = rows_ref.shape
    per = cotangent_ref.shape[2] // columns
    width = pieces * columns

    def parts(k, j):
        embedded = rows_ref[k * per + j].astype(jnp.float32)
        own = cotangent_ref[k, :, j * columns : (j + 1) * columns].astype(jnp.float32)
        return embedded, own * gain_ref[pl.ds(k * per + j, 1), :]

    def sums(k, carry):
        squares, inners = carry
        for j in range(per):
            embedded, scaled = parts(k, j)
            squares = squares + embedded * embedded
            inners = inners + scaled * embedded
        return squares, inners

    zeros = jnp.zeros((slots, columns), jnp.float32)
    squares, inners = lax.fori_loop(0, pieces // per, sums, (zeros, zeros))
    square_mean = jnp.sum(squares, axis=1, keepdims=True) * (1.0 / width)
    inner = jnp.sum(inners, axis=1, keepdims=True) * (1.0 / width)
    inverse = lax.rsqrt(square_mean + epsilon)
    pull = inverse * inverse * inverse * inner

    def grads(k, carry):
        for j in range(per):
            embedded, scaled = parts(k, j)
            grad = (inverse * scaled - embedded * pull).astype(jnp.bfloat16)
            by_column_ref[k * per + j] = grad
            by_feature_ref[k, :, j * columns : (j + 1) * columns] = grad
        return carry

    lax.fori_loop(0, pieces // per, grads, 0)


def add_kernel(index_ref, count_ref, grads_ref, table_ref, total_ref, wide_ref, *, groups):
    step = 256
    slots = grads_ref.shape[1]

    def clear(i, carry):
        total_ref[pl.ds(i * step, step), :] = jnp.zeros((step, LANES), jnp.float32)
        return carry

    lax.fori_loop(0, total_ref.shape[0] // step, clear, 0)

    def group(g, carry):
        wide_ref[...] = grads_ref[g].astype(jnp.float32)

        def one(c, carry):
            row = pl.ds(index_ref[c, g], 1)
            total_ref[row, :] = total_ref[row, :] + wide_ref[pl.ds(c, 1), :]
            return carry

        lax.fori_loop(0, jnp.minimum(count_ref[0, g], slots), one, 0)
        return carry

    lax.fori_loop(0, groups, group, 0)

    def narrow(i, carry):
        table_ref[pl.ds(i * step, step), :] = total_ref[pl.ds(i * step, step), :].astype(jnp.bfloat16)
        return carry

    lax.fori_loop(0, total_ref.shape[0] // step, narrow, 0)


def call(kernel, operands, spaces, outs, scratch=(), semaphores=(), room=6):
    held = sum(math.prod(a.shape) * a.dtype.itemsize for a in (*operands, *outs, *scratch))
    return pl.pallas_call(
        kernel,
        in_specs=[whole(o.shape, s) for o, s in zip(operands, spaces)],
        out_specs=[whole(o.shape) for o in outs],
        out_shape=outs,
        scratch_shapes=[*scratch, *semaphores],
        compiler_params=pltpu.CompilerParams(vmem_limit_bytes=2 * held + (room << 20)),
    )(*operands)


def passage(slots, section, all_ids, own_ids, embed_table, norm_gain, cotangent):
    vocab_section, columns = embed_table.shape
    groups = all_ids.shape[0]
    tokens, features = cotangent.shape
    sections = lax.axis_size(SECTION)
    V, S = pltpu.VMEM, pltpu.SMEM
    bf16 = functools.partial(jax.ShapeDtypeStruct, dtype=jnp.bfloat16)
    i32 = functools.partial(jax.ShapeDtypeStruct, dtype=jnp.int32)
    (dealt,) = call(
        functools.partial(deal_kernel, slots=slots, sections=sections, vocab_section=vocab_section),
        (own_ids, cotangent), (V, V), [bf16((sections, slots, features))],
    )
    their_cotangent = lax.all_to_all(dealt, SECTION, 0, 0, tiled=True)
    index, count = call(
        functools.partial(plan_kernel, slots=slots, vocab_section=vocab_section),
        (section, all_ids), (S, V), [i32((slots, LANES)), i32((8, LANES))],
    )
    (rows,) = call(
        functools.partial(pick_kernel, slots=slots, groups=groups),
        (index, embed_table), (S, V), [bf16((groups, slots, columns))],
        [pltpu.VMEM((vocab_section, columns), jnp.float32), pltpu.VMEM((slots, columns), jnp.float32)],
    )
    full_rows = lax.all_to_all(rows, "dp", 0, 0, tiled=True)
    gain = norm_gain.reshape(groups, columns)
    by_column, by_feature = call(
        norm_kernel, (full_rows, their_cotangent, gain), (V, V, V),
        [bf16(full_rows.shape), bf16(their_cotangent.shape)],
    )
    back = lax.all_to_all(by_column, "dp", 0, 0, tiled=True)
    home = lax.all_to_all(by_feature, SECTION, 0, 0, tiled=True)
    (grad_table,) = call(
        functools.partial(add_kernel, groups=groups),
        (index, count, back), (S, S, V), [bf16((vocab_section, columns))],
        [pltpu.VMEM((vocab_section, columns), jnp.float32), pltpu.VMEM((slots, columns), jnp.float32)],
    )
    (own_grad,) = call(
        functools.partial(collect_kernel, slots=slots, sections=sections, vocab_section=vocab_section),
        (own_ids, home), (V, V), [bf16((tokens, features))],
    )
    return grad_table, own_grad


def row_plan(section, ids, plan_ref, over_ref, vocab_section):
    slots = plan_ref.shape[0] - CHUNK
    sections = 1 + (REPEATED - 1) // vocab_section
    ids = ids.astype(jnp.float32)
    ids = jnp.concatenate([ids, ids], axis=0)
    ids = ids.T.astype(jnp.int32)
    home = (ids % REPEATED) // vocab_section
    over = jnp.full((1, LANES), -1, jnp.int32)
    for s in range(sections):
        new = jnp.where((home == s) & (ids < REPEATED), 1, 0)
        over = jnp.maximum(over, jnp.sum(new, axis=0, keepdims=True) - slots)
    for s in range(0, sections, 2):
        here = jnp.where(home // 2 == s // 2, 1, 0)
        over = jnp.maximum(over, jnp.sum(here, axis=0, keepdims=True) - TOKEN_SLOTS)
    over_ref[...] = jnp.broadcast_to(over, over_ref.shape)
    local = ids - section * vocab_section
    inside = (local >= 0) & (local < vocab_section) & (ids < REPEATED)
    before = (
        lax.broadcasted_iota(jnp.int32, (LANES, LANES), 1)
        < lax.broadcasted_iota(jnp.int32, (LANES, LANES), 0)
    )
    ones = jnp.where(inside, 1.0, 0.0)
    rank = jnp.dot(
        jnp.where(before, 1.0, 0.0).astype(jnp.bfloat16),
        ones.astype(jnp.bfloat16),
        preferred_element_type=jnp.float32,
    ).astype(jnp.int32)
    rank = jnp.where(inside, rank, -1)
    short = local - vocab_section
    for c in range(slots):
        plan_ref[pl.ds(c, 1), :] = vocab_section + jnp.sum(
            jnp.where(rank == c, short, 0), axis=0, keepdims=True
        )
    count = jnp.minimum(jnp.sum(ones, axis=0, keepdims=True).astype(jnp.int32), slots)
    plan_ref[pl.ds(slots, CHUNK), :] = jnp.broadcast_to((count + (CHUNK - 1)) // CHUNK, (CHUNK, LANES))


def row_pick_kernel(
    section_ref, ids_ref, table_ref, rows_ref, plan_ref, over_ref,
    held_ref, wide_ref, picked_ref, steps_ref, arrived, planned, *, vocab_section
):
    groups, slots, columns = rows_ref.shape
    entries = table_ref.shape[0]
    pieces = arrived.shape[0]
    piece = entries // pieces
    copies = [
        pltpu.make_async_copy(
            table_ref.at[pl.ds(i * piece, piece)], held_ref.at[pl.ds(i * piece, piece)], arrived.at[i]
        )
        for i in range(pieces)
    ]
    for copy in copies:
        copy.start()
    row_plan(section_ref[0], ids_ref[...], plan_ref, over_ref, vocab_section)
    plan_copy = pltpu.make_async_copy(plan_ref, steps_ref, planned)
    plan_copy.start()
    picked_ref[...] = jnp.zeros(picked_ref.shape, jnp.float32)
    wide_ref[pl.ds(entries, CHUNK), :] = jnp.zeros((CHUNK, columns), jnp.float32)
    step = 512

    for i, copy in enumerate(copies):
        copy.wait()

        def widen(j, carry):
            at = pl.ds(pl.multiple_of(i * piece + j * step, step), step)
            wide_ref[at, :] = held_ref[at, :].astype(jnp.float32)
            return carry

        lax.fori_loop(0, piece // step, widen, 0)
    plan_copy.wait()

    def group(g, carry):
        def chunk(i, carry):
            for j in range(CHUNK):
                c = i * CHUNK + j
                picked_ref[pl.ds(c, 1), :] = wide_ref[pl.ds(steps_ref[c, g], 1), :]
            return carry

        lax.fori_loop(0, steps_ref[slots, g], chunk, 0)
        rows_ref[g] = picked_ref[...].astype(jnp.bfloat16)
        return carry

    lax.fori_loop(0, groups, group, 0)


def row_add_kernel(plan_ref, grads_ref, table_ref, total_ref, wide_ref):
    groups, slots, columns = grads_ref.shape
    entries = table_ref.shape[0]
    step = 512

    def clear(i, carry):
        total_ref[pl.ds(i * step, step), :] = jnp.zeros((step, columns), jnp.float32)
        return carry

    lax.fori_loop(0, entries // step, clear, 0)
    total_ref[pl.ds(entries, CHUNK), :] = jnp.zeros((CHUNK, columns), jnp.float32)

    def group(g, carry):
        wide_ref[...] = grads_ref[g].astype(jnp.float32)

        def chunk(i, carry):
            rows = [pl.ds(plan_ref[i * CHUNK + j, g], 1) for j in range(CHUNK)]
            sums = [
                total_ref[row, :] + wide_ref[pl.ds(i * CHUNK + j, 1), :]
                for j, row in enumerate(rows)
            ]
            for row, value in zip(rows, sums):
                total_ref[row, :] = value
            return carry

        lax.fori_loop(0, plan_ref[slots, g], chunk, 0)
        return carry

    lax.fori_loop(0, groups, group, 0)

    def narrow(i, carry):
        table_ref[pl.ds(i * step, step), :] = total_ref[pl.ds(i * step, step), :].astype(jnp.bfloat16)
        return carry

    lax.fori_loop(0, entries // step, narrow, 0)


def both_ways(ids_row):
    wide = jnp.broadcast_to(ids_row, (LANES, LANES))
    tall = wide.astype(jnp.float32).T.astype(jnp.int32)
    down = lax.broadcasted_iota(jnp.int32, (LANES, LANES), 0)
    along = lax.broadcasted_iota(jnp.int32, (LANES, LANES), 1)
    return wide, tall, down < along, along < down


def mark_kernel(ids_ref, marked_ref):
    wide, tall, row_first, _ = both_ways(ids_ref[...])
    repeated = jnp.max(jnp.where((wide == tall) & row_first, REPEATED, 0), axis=0, keepdims=True)
    marked_ref[...] = jnp.broadcast_to((wide[:1] + repeated)[None], marked_ref.shape)


def one_hot(condition):
    return jnp.where(condition, 1.0, 0.0).astype(jnp.bfloat16)


def chip_ranks(ids_row, vocab_section):
    wide, tall, row_first, column_first = both_ways(ids_row)
    wide = wide // (2 * vocab_section)
    tall = tall // (2 * vocab_section)
    same = wide == tall
    as_row = jnp.sum(jnp.where(same & row_first, 1, 0), axis=0, keepdims=True)
    as_column = jnp.sum(jnp.where(same & column_first, 1.0, 0.0), axis=1, keepdims=True)
    return wide[:1], as_row, tall[:, :1], as_column.astype(jnp.int32)


def hand_kernel(section_ref, ids_ref, cotangent_ref, *refs, vocab_section):
    *hand_refs, expand_ref, combine_ref = refs
    token_slots, row_slots = expand_ref.shape
    section = section_ref[0]
    wide_chip, wide_rank, _, _ = chip_ranks(ids_ref[...], vocab_section)
    slot = lax.broadcasted_iota(jnp.int32, (token_slots, LANES), 0)
    cotangent = cotangent_ref[...]
    for k, hand_ref in enumerate(hand_refs):
        wanted = one_hot((slot == wide_rank) & (wide_chip == (section // 2) ^ k))
        hand_ref[...] = jnp.dot(
            wanted, cotangent, preferred_element_type=jnp.float32
        ).astype(jnp.bfloat16)

    wide, tall, row_first, column_first = both_ways(ids_ref[...])
    wide_in = wide // vocab_section == section
    tall_in = tall // vocab_section == section
    same = wide == tall
    wide_repeat = jnp.max(jnp.where(same & row_first, 1, 0), axis=0, keepdims=True)
    tall_repeat = jnp.max(jnp.where(same & column_first, 1.0, 0.0), axis=1, keepdims=True)
    wide_new = wide_in & (jnp.broadcast_to(wide_repeat, (LANES, LANES)) == 0)
    tall_new = tall_in & (jnp.broadcast_to(tall_repeat, (LANES, LANES)) == 0.0)
    own = one_hot((slot == wide_rank) & wide_in[:1])
    tall_place = jnp.sum(jnp.where(wide_new & column_first, 1.0, 0.0), axis=1, keepdims=True)
    place = jnp.sum(
        jnp.where(same & tall_new, jnp.broadcast_to(tall_place, (LANES, LANES)), 0.0), axis=0, keepdims=True
    ).astype(jnp.int32)
    place = jnp.where(wide_in[:1], place, -1)
    rows = one_hot(lax.broadcasted_iota(jnp.int32, (row_slots, LANES), 0) == place)
    over_tokens = (((1,), (1,)), ((), ()))
    expand_ref[...] = lax.dot_general(
        own, rows, over_tokens, preferred_element_type=jnp.float32
    ).astype(jnp.bfloat16)
    combine_ref[...] = lax.dot_general(
        rows, own, over_tokens, preferred_element_type=jnp.float32
    ).astype(jnp.bfloat16)


def stack_kernel(*refs):
    *part_refs, stack_ref = refs
    for k, part_ref in enumerate(part_refs):
        stack_ref[k] = part_ref[...]


def grad_kernel(section_ref, rows_ref, gain_ref, expand_ref, got_ref, *refs):
    *hand_refs, keep_ref, give_ref, embedded_ref = refs
    pieces, _, columns = rows_ref.shape
    chips, slots, features = got_ref.shape
    per = features // columns
    width = pieces * columns
    expand = expand_ref[...]
    section = section_ref[0]
    core = section % 2
    parts = []
    for k in range(chips):
        chip = (section // 2) ^ k
        parts.append((2 * chip + core, hand_refs[k], keep_ref.at[k]))
        parts.append((2 * chip + 1 - core, got_ref.at[k], give_ref.at[k]))

    squares = jnp.zeros((slots, columns), jnp.float32)
    inners = jnp.zeros((slots, columns), jnp.float32)
    for i, (s, cotangent_ref, _) in enumerate(parts):
        rows = jnp.concatenate([rows_ref[s * per + j] for j in range(per)], axis=1)
        embedded = jnp.dot(expand, rows, preferred_element_type=jnp.float32)
        embedded_ref[i] = embedded.astype(jnp.bfloat16)
        scaled = cotangent_ref[...].astype(jnp.float32) * gain_ref[pl.ds(s, 1), :]
        square = embedded * embedded
        inner = scaled * embedded
        for j in range(per):
            squares = squares + square[:, j * columns : (j + 1) * columns]
            inners = inners + inner[:, j * columns : (j + 1) * columns]
    square_mean = jnp.sum(squares, axis=1, keepdims=True) * (1.0 / width)
    inner = jnp.sum(inners, axis=1, keepdims=True) * (1.0 / width)
    own = jnp.sum(expand.astype(jnp.float32), axis=1, keepdims=True)
    inverse = jnp.where(own > 0.0, lax.rsqrt(square_mean + epsilon), 0.0)
    pull = inverse * inverse * inverse * inner

    for i, (s, cotangent_ref, out_ref) in enumerate(parts):
        scaled = cotangent_ref[...].astype(jnp.float32) * gain_ref[pl.ds(s, 1), :]
        out_ref[...] = (inverse * scaled - embedded_ref[i].astype(jnp.float32) * pull).astype(jnp.bfloat16)


def combine_kernel(section_ref, combine_ref, keep_ref, give_ref, by_column_ref):
    columns = by_column_ref.shape[2]
    chips, _, features = keep_ref.shape
    per = features // columns
    combine = combine_ref[...]
    section = section_ref[0]
    core = section % 2
    for k in range(chips):
        chip = (section // 2) ^ k
        for s, grad_ref in ((2 * chip + core, keep_ref), (2 * chip + 1 - core, give_ref)):
            added = jnp.dot(combine, grad_ref[k], preferred_element_type=jnp.float32).astype(jnp.bfloat16)
            for j in range(per):
                by_column_ref[s * per + j] = added[:, j * columns : (j + 1) * columns]


def merge_kernel(keep_ref, got_ref, *out_refs):
    for k, out_ref in enumerate(out_refs):
        out_ref[...] = (keep_ref[k].astype(jnp.float32) + got_ref[k].astype(jnp.float32)).astype(jnp.bfloat16)


def gather_kernel(section_ref, ids_ref, *refs, vocab_section):
    *home_refs, own_ref = refs
    slots = home_refs[0].shape[0]
    _, _, tall_chip, tall_rank = chip_ranks(ids_ref[...], vocab_section)
    along = lax.broadcasted_iota(jnp.int32, (LANES, slots), 1)
    total = jnp.zeros(own_ref.shape, jnp.float32)
    for k, home_ref in enumerate(home_refs):
        wanted = one_hot((along == tall_rank) & (tall_chip == (section_ref[0] // 2) ^ k))
        total = total + jnp.dot(wanted, home_ref[...], preferred_element_type=jnp.float32)
    own_ref[...] = total.astype(jnp.bfloat16)


def settle_kernel(fits_ref, fast_ref, slow_ref, out_ref, semaphore):
    @pl.when(fits_ref[0] == 0)
    def _():
        copy = pltpu.make_async_copy(slow_ref, out_ref, semaphore)
        copy.start()
        copy.wait()


def in_order(own, travelled):
    return [own[0]] + [travelled[FAR_FIRST.index(k)] for k in range(1, len(own))]


def on_device(token_ids, embed_table, norm_gain, cotangent):
    vocab_section, columns = embed_table.shape
    groups = lax.axis_size("dp")
    sections = lax.axis_size(SECTION)
    tokens, features = cotangent.shape
    V, S = pltpu.VMEM, pltpu.SMEM
    bf16 = functools.partial(jax.ShapeDtypeStruct, dtype=jnp.bfloat16)
    f32 = pltpu.VMEM
    i32 = functools.partial(jax.ShapeDtypeStruct, dtype=jnp.int32)
    section = lax.axis_index(SECTION).reshape(1)
    own_ids = token_ids.reshape(1, tokens)
    (marked,) = call(mark_kernel, (own_ids,), (V,), [i32((groups, 1, tokens))])
    marked = lax.all_to_all(marked, "dp", 0, 0, tiled=True)
    chips = sections // 2
    part = bf16((TOKEN_SLOTS, features))
    parts = bf16((chips, TOKEN_SLOTS, features))

    def to_chip(k, array):
        return lax.ppermute(array, CHIPS, [(i, i ^ k) for i in range(chips)])

    def to_sibling(array):
        return lax.ppermute(array, CORES, [(0, 1), (1, 0)])

    *hands, expand, combine = call(
        functools.partial(hand_kernel, vocab_section=vocab_section),
        (section, own_ids, cotangent), (S, V, V),
        [part] * chips + [bf16((TOKEN_SLOTS, ROW_SLOTS)), bf16((ROW_SLOTS, TOKEN_SLOTS))],
    )
    handed = [to_chip(k, hands[k]) for k in FAR_FIRST]
    marked, handed[:EARLY] = lax.optimization_barrier((marked, handed[:EARLY]))
    handed = in_order(hands, handed)
    marked = marked.reshape(groups, tokens)
    wide_shape = (vocab_section + CHUNK, columns)
    wide_slots = f32((ROW_SLOTS, columns), jnp.float32)
    plan_shape = (ROW_SLOTS + CHUNK, LANES)
    rows, plan, over = call(
        functools.partial(row_pick_kernel, vocab_section=vocab_section),
        (section, marked, embed_table), (S, V, pltpu.HBM),
        [bf16((groups, ROW_SLOTS, columns)), i32(plan_shape), i32((8, LANES))],
        [f32(embed_table.shape, jnp.bfloat16), f32(wide_shape, jnp.float32), wide_slots],
        [pltpu.SMEM(plan_shape, jnp.int32), pltpu.SemaphoreType.DMA((4,)), pltpu.SemaphoreType.DMA],
    )
    full_rows = lax.all_to_all(rows, "dp", 0, 0, tiled=True)
    (stack,) = call(stack_kernel, tuple(handed), (V,) * chips, [parts])
    got = to_sibling(stack)
    keep, give = call(
        grad_kernel,
        (section, full_rows, norm_gain.reshape(sections, features), expand, got, *handed),
        (S,) + (V,) * (4 + chips), [parts, parts],
        [f32((sections, TOKEN_SLOTS, features), jnp.bfloat16)],
    )
    (by_column,) = call(
        combine_kernel, (section, combine, keep, give), (S, V, V, V), [bf16(full_rows.shape)]
    )
    outs = call(merge_kernel, (keep, to_sibling(give)), (V, V), [part] * chips)
    by_column, outs = lax.optimization_barrier((by_column, list(outs)))
    home = [to_chip(k, outs[k]) for k in FAR_FIRST]
    back = lax.all_to_all(by_column, "dp", 0, 0, tiled=True)

    def fast(plan, back, *_):
        (grad_table,) = call(
            row_add_kernel, (plan, back), (S, V),
            [bf16((vocab_section, columns))], [f32(wide_shape, jnp.float32), wide_slots],
        )
        return grad_table, jnp.zeros((tokens, features), jnp.bfloat16)

    def slow(plan, back, section, marked, *operands):
        return passage(tokens, section, marked % REPEATED, *operands)

    fits = jnp.max(over[:1]) <= 0

    grad_table, slow_grad = lax.cond(
        fits, fast, slow, plan, back,
        section, marked, own_ids, embed_table, norm_gain, cotangent,
    )
    grad_table, slow_grad, home = lax.optimization_barrier((grad_table, slow_grad, home))
    (fast_grad,) = call(
        functools.partial(gather_kernel, vocab_section=vocab_section),
        (section, own_ids, *in_order(outs, home)), (S,) + (V,) * (1 + chips), [bf16((tokens, features))],
    )
    anywhere = pl.BlockSpec(memory_space=pl.ANY)
    own_grad = pl.pallas_call(
        settle_kernel,
        in_specs=[whole((1,), S), anywhere, anywhere],
        out_specs=anywhere,
        out_shape=bf16((tokens, features)),
        scratch_shapes=[pltpu.SemaphoreType.DMA],
        input_output_aliases={1: 0},
    )(fits.astype(jnp.int32).reshape(1), fast_grad, slow_grad)
    return grad_table, own_grad


def solution(mesh):
    split = Mesh(mesh.devices.reshape(-1, 2, mesh.shape["dp"]), (CHIPS, CORES, "dp"))
    return jax.shard_map(
        on_device,
        mesh=split,
        in_specs=(P("dp"), P(SECTION, "dp"), P(), P("dp", SECTION)),
        out_specs=(P(SECTION, "dp"), P("dp", SECTION)),
        check_vma=False,
    )
```

```python
import functools
import math

import jax
import jax.numpy as jnp
from jax import lax
from jax.experimental import pallas as pl
from jax.experimental.pallas import tpu as pltpu
from jax.sharding import Mesh
from jax.sharding import PartitionSpec as P

epsilon = 1e-05
TOKEN_SLOTS = 72
ROW_SLOTS = 32
CHUNK = 8
ALWAYS = 2
FAR_FIRST = (2, 1, 3)
EARLY = 1
REPEATED = 1 << 16
CHIPS = "section_0"
CORES = "section_1"
SECTION = (CHIPS, CORES)
LANES = 128


def whole(shape, space=pltpu.VMEM):
    if space == pltpu.HBM:
        return pl.BlockSpec(memory_space=space)
    return pl.BlockSpec(shape, lambda *_: (0,) * len(shape), memory_space=space)


def plan_kernel(section_ref, ids_ref, index_ref, count_ref, *, slots, vocab_section):
    ids = ids_ref[...].astype(jnp.float32)
    ids = jnp.concatenate([ids, ids], axis=0)
    ids = ids.T.astype(jnp.int32)
    local = ids - section_ref[0] * vocab_section
    inside = (local >= 0) & (local < vocab_section)
    before = (
        lax.broadcasted_iota(jnp.int32, (LANES, LANES), 1)
        < lax.broadcasted_iota(jnp.int32, (LANES, LANES), 0)
    )
    ones = jnp.where(inside, 1.0, 0.0)
    rank = jnp.dot(
        jnp.where(before, 1.0, 0.0).astype(jnp.bfloat16),
        ones.astype(jnp.bfloat16),
        preferred_element_type=jnp.float32,
    ).astype(jnp.int32)
    rank = jnp.where(inside, rank, -1)
    for c in range(slots):
        index_ref[pl.ds(c, 1), :] = jnp.sum(jnp.where(rank == c, local, 0), axis=0, keepdims=True)
    count_ref[...] = jnp.broadcast_to(
        jnp.sum(ones, axis=0, keepdims=True).astype(jnp.int32), count_ref.shape
    )


def pick_kernel(index_ref, table_ref, rows_ref, wide_ref, picked_ref, *, slots, groups):
    step = 256

    def widen(i, carry):
        wide_ref[pl.ds(i * step, step), :] = table_ref[pl.ds(i * step, step), :].astype(jnp.float32)
        return carry

    lax.fori_loop(0, table_ref.shape[0] // step, widen, 0)

    def group(g, carry):
        for c in range(slots):
            picked_ref[pl.ds(c, 1), :] = wide_ref[pl.ds(index_ref[c, g], 1), :]
        rows_ref[g] = picked_ref[...].astype(jnp.bfloat16)
        return carry

    lax.fori_loop(0, groups, group, 0)


def slot_of(ids_row, slots, vocab_section):
    wide = jnp.broadcast_to(ids_row // vocab_section, (LANES, LANES))
    tall = wide.astype(jnp.float32).T.astype(jnp.int32)
    first = lax.broadcasted_iota(jnp.int32, (LANES, LANES), 0)
    second = lax.broadcasted_iota(jnp.int32, (LANES, LANES), 1)
    same = wide == tall
    as_row = jnp.sum(jnp.where(same & (first < second), 1, 0), axis=0, keepdims=True)
    as_column = jnp.sum(jnp.where(same & (second < first), 1.0, 0.0), axis=1, keepdims=True)
    row_slot = jnp.where(as_row < slots, wide[:1] * slots + as_row, -1)
    as_column = as_column.astype(jnp.int32)
    column_slot = jnp.where(as_column < slots, tall[:, :1] * slots + as_column, -1)
    return row_slot, column_slot


def deal_kernel(ids_ref, cotangent_ref, dealt_ref, *, slots, sections, vocab_section):
    row_slot, _ = slot_of(ids_ref[...], slots, vocab_section)
    cotangent = cotangent_ref[...]
    for s in range(sections):
        wanted = lax.broadcasted_iota(jnp.int32, (slots, LANES), 0) + s * slots == row_slot
        dealt_ref[s] = jnp.dot(
            jnp.where(wanted, 1.0, 0.0).astype(jnp.bfloat16),
            cotangent,
            preferred_element_type=jnp.float32,
        ).astype(jnp.bfloat16)


def collect_kernel(ids_ref, dealt_ref, own_ref, *, slots, sections, vocab_section):
    _, column_slot = slot_of(ids_ref[...], slots, vocab_section)
    total = jnp.zeros(own_ref.shape, jnp.float32)
    for s in range(sections):
        wanted = lax.broadcasted_iota(jnp.int32, (LANES, slots), 1) + s * slots == column_slot
        total = total + jnp.dot(
            jnp.where(wanted, 1.0, 0.0).astype(jnp.bfloat16),
            dealt_ref[s],
            preferred_element_type=jnp.float32,
        )
    own_ref[...] = total.astype(jnp.bfloat16)


def norm_kernel(rows_ref, cotangent_ref, gain_ref, by_column_ref, by_feature_ref):
    pieces, slots, columns = rows_ref.shape
    per = cotangent_ref.shape[2] // columns
    width = pieces * columns

    def parts(k, j):
        embedded = rows_ref[k * per + j].astype(jnp.float32)
        own = cotangent_ref[k, :, j * columns : (j + 1) * columns].astype(jnp.float32)
        return embedded, own * gain_ref[pl.ds(k * per + j, 1), :]

    def sums(k, carry):
        squares, inners = carry
        for j in range(per):
            embedded, scaled = parts(k, j)
            squares = squares + embedded * embedded
            inners = inners + scaled * embedded
        return squares, inners

    zeros = jnp.zeros((slots, columns), jnp.float32)
    squares, inners = lax.fori_loop(0, pieces // per, sums, (zeros, zeros))
    square_mean = jnp.sum(squares, axis=1, keepdims=True) * (1.0 / width)
    inner = jnp.sum(inners, axis=1, keepdims=True) * (1.0 / width)
    inverse = lax.rsqrt(square_mean + epsilon)
    pull = inverse * inverse * inverse * inner

    def grads(k, carry):
        for j in range(per):
            embedded, scaled = parts(k, j)
            grad = (inverse * scaled - embedded * pull).astype(jnp.bfloat16)
            by_column_ref[k * per + j] = grad
            by_feature_ref[k, :, j * columns : (j + 1) * columns] = grad
        return carry

    lax.fori_loop(0, pieces // per, grads, 0)


def add_kernel(index_ref, count_ref, grads_ref, table_ref, total_ref, wide_ref, *, groups):
    step = 256
    slots = grads_ref.shape[1]

    def clear(i, carry):
        total_ref[pl.ds(i * step, step), :] = jnp.zeros((step, LANES), jnp.float32)
        return carry

    lax.fori_loop(0, total_ref.shape[0] // step, clear, 0)

    def group(g, carry):
        wide_ref[...] = grads_ref[g].astype(jnp.float32)

        def one(c, carry):
            row = pl.ds(index_ref[c, g], 1)
            total_ref[row, :] = total_ref[row, :] + wide_ref[pl.ds(c, 1), :]
            return carry

        lax.fori_loop(0, jnp.minimum(count_ref[0, g], slots), one, 0)
        return carry

    lax.fori_loop(0, groups, group, 0)

    def narrow(i, carry):
        table_ref[pl.ds(i * step, step), :] = total_ref[pl.ds(i * step, step), :].astype(jnp.bfloat16)
        return carry

    lax.fori_loop(0, total_ref.shape[0] // step, narrow, 0)


def call(kernel, operands, spaces, outs, scratch=(), semaphores=(), room=6):
    held = sum(math.prod(a.shape) * a.dtype.itemsize for a in (*operands, *outs, *scratch))
    return pl.pallas_call(
        kernel,
        in_specs=[whole(o.shape, s) for o, s in zip(operands, spaces)],
        out_specs=[whole(o.shape) for o in outs],
        out_shape=outs,
        scratch_shapes=[*scratch, *semaphores],
        compiler_params=pltpu.CompilerParams(vmem_limit_bytes=2 * held + (room << 20)),
    )(*operands)


def passage(slots, section, all_ids, own_ids, embed_table, norm_gain, cotangent):
    vocab_section, columns = embed_table.shape
    groups = all_ids.shape[0]
    tokens, features = cotangent.shape
    sections = lax.axis_size(SECTION)
    V, S = pltpu.VMEM, pltpu.SMEM
    bf16 = functools.partial(jax.ShapeDtypeStruct, dtype=jnp.bfloat16)
    i32 = functools.partial(jax.ShapeDtypeStruct, dtype=jnp.int32)
    (dealt,) = call(
        functools.partial(deal_kernel, slots=slots, sections=sections, vocab_section=vocab_section),
        (own_ids, cotangent), (V, V), [bf16((sections, slots, features))],
    )
    their_cotangent = lax.all_to_all(dealt, SECTION, 0, 0, tiled=True)
    index, count = call(
        functools.partial(plan_kernel, slots=slots, vocab_section=vocab_section),
        (section, all_ids), (S, V), [i32((slots, LANES)), i32((8, LANES))],
    )
    (rows,) = call(
        functools.partial(pick_kernel, slots=slots, groups=groups),
        (index, embed_table), (S, V), [bf16((groups, slots, columns))],
        [pltpu.VMEM((vocab_section, columns), jnp.float32), pltpu.VMEM((slots, columns), jnp.float32)],
    )
    full_rows = lax.all_to_all(rows, "dp", 0, 0, tiled=True)
    gain = norm_gain.reshape(groups, columns)
    by_column, by_feature = call(
        norm_kernel, (full_rows, their_cotangent, gain), (V, V, V),
        [bf16(full_rows.shape), bf16(their_cotangent.shape)],
    )
    back = lax.all_to_all(by_column, "dp", 0, 0, tiled=True)
    home = lax.all_to_all(by_feature, SECTION, 0, 0, tiled=True)
    (grad_table,) = call(
        functools.partial(add_kernel, groups=groups),
        (index, count, back), (S, S, V), [bf16((vocab_section, columns))],
        [pltpu.VMEM((vocab_section, columns), jnp.float32), pltpu.VMEM((slots, columns), jnp.float32)],
    )
    (own_grad,) = call(
        functools.partial(collect_kernel, slots=slots, sections=sections, vocab_section=vocab_section),
        (own_ids, home), (V, V), [bf16((tokens, features))],
    )
    return grad_table, own_grad


def row_plan(section, ids, plan_ref, over_ref, vocab_section):
    slots = plan_ref.shape[0] - CHUNK
    sections = 1 + (REPEATED - 1) // vocab_section
    ids = ids.astype(jnp.float32)
    ids = jnp.concatenate([ids, ids], axis=0)
    ids = ids.T.astype(jnp.int32)
    home = (ids % REPEATED) // vocab_section
    over = jnp.full((1, LANES), -1, jnp.int32)
    for s in range(sections):
        new = jnp.where((home == s) & (ids < REPEATED), 1, 0)
        over = jnp.maximum(over, jnp.sum(new, axis=0, keepdims=True) - slots)
    for s in range(0, sections, 2):
        here = jnp.where(home // 2 == s // 2, 1, 0)
        over = jnp.maximum(over, jnp.sum(here, axis=0, keepdims=True) - TOKEN_SLOTS)
    over_ref[...] = jnp.broadcast_to(over, over_ref.shape)
    local = ids - section * vocab_section
    inside = (local >= 0) & (local < vocab_section) & (ids < REPEATED)
    before = (
        lax.broadcasted_iota(jnp.int32, (LANES, LANES), 1)
        < lax.broadcasted_iota(jnp.int32, (LANES, LANES), 0)
    )
    ones = jnp.where(inside, 1.0, 0.0)
    rank = jnp.dot(
        jnp.where(before, 1.0, 0.0).astype(jnp.bfloat16),
        ones.astype(jnp.bfloat16),
        preferred_element_type=jnp.float32,
    ).astype(jnp.int32)
    rank = jnp.where(inside, rank, -1)
    short = local - vocab_section
    for c in range(slots):
        plan_ref[pl.ds(c, 1), :] = vocab_section + jnp.sum(
            jnp.where(rank == c, short, 0), axis=0, keepdims=True
        )
    count = jnp.minimum(jnp.sum(ones, axis=0, keepdims=True).astype(jnp.int32), slots)
    plan_ref[pl.ds(slots, CHUNK), :] = jnp.broadcast_to((count + (CHUNK - 1)) // CHUNK, (CHUNK, LANES))


def row_pick_kernel(
    section_ref, ids_ref, table_ref, rows_ref, plan_ref, over_ref,
    held_ref, wide_ref, picked_ref, steps_ref, arrived, planned, *, vocab_section
):
    groups, slots, columns = rows_ref.shape
    entries = table_ref.shape[0]
    pieces = arrived.shape[0]
    piece = entries // pieces
    copies = [
        pltpu.make_async_copy(
            table_ref.at[pl.ds(i * piece, piece)], held_ref.at[pl.ds(i * piece, piece)], arrived.at[i]
        )
        for i in range(pieces)
    ]
    for copy in copies:
        copy.start()
    row_plan(section_ref[0], ids_ref[...], plan_ref, over_ref, vocab_section)
    plan_copy = pltpu.make_async_copy(plan_ref, steps_ref, planned)
    plan_copy.start()
    picked_ref[...] = jnp.zeros(picked_ref.shape, jnp.float32)
    wide_ref[pl.ds(entries, CHUNK), :] = jnp.zeros((CHUNK, columns), jnp.float32)
    step = 512

    for i, copy in enumerate(copies):
        copy.wait()

        def widen(j, carry):
            at = pl.ds(pl.multiple_of(i * piece + j * step, step), step)
            wide_ref[at, :] = held_ref[at, :].astype(jnp.float32)
            return carry

        lax.fori_loop(0, piece // step, widen, 0)
    plan_copy.wait()

    def group(g, carry):
        def copy_row(c):
            picked_ref[pl.ds(c, 1), :] = wide_ref[pl.ds(steps_ref[c, g], 1), :]

        def chunk(i, carry):
            for j in range(CHUNK):
                copy_row(i * CHUNK + j)
            return carry

        for c in range(ALWAYS * CHUNK):
            copy_row(c)
        lax.fori_loop(ALWAYS, steps_ref[slots, g], chunk, 0)
        rows_ref[g] = picked_ref[...].astype(jnp.bfloat16)
        return carry

    lax.fori_loop(0, groups, group, 0)


def row_add_kernel(plan_ref, grads_ref, table_ref, total_ref, wide_ref):
    groups, slots, columns = grads_ref.shape
    entries = table_ref.shape[0]
    step = 512

    def clear(i, carry):
        total_ref[pl.ds(i * step, step), :] = jnp.zeros((step, columns), jnp.float32)
        return carry

    lax.fori_loop(0, entries // step, clear, 0)
    total_ref[pl.ds(entries, CHUNK), :] = jnp.zeros((CHUNK, columns), jnp.float32)

    def group(g, carry):
        wide_ref[...] = grads_ref[g].astype(jnp.float32)

        def add_rows(slots_here):
            rows = [pl.ds(plan_ref[c, g], 1) for c in slots_here]
            sums = [total_ref[row, :] + wide_ref[pl.ds(c, 1), :] for c, row in zip(slots_here, rows)]
            for row, value in zip(rows, sums):
                total_ref[row, :] = value

        def chunk(i, carry):
            add_rows([i * CHUNK + j for j in range(CHUNK)])
            return carry

        add_rows(list(range(ALWAYS * CHUNK)))
        lax.fori_loop(ALWAYS, plan_ref[slots, g], chunk, 0)
        return carry

    lax.fori_loop(0, groups, group, 0)

    def narrow(i, carry):
        table_ref[pl.ds(i * step, step), :] = total_ref[pl.ds(i * step, step), :].astype(jnp.bfloat16)
        return carry

    lax.fori_loop(0, entries // step, narrow, 0)


def both_ways(ids_row):
    wide = jnp.broadcast_to(ids_row, (LANES, LANES))
    tall = wide.astype(jnp.float32).T.astype(jnp.int32)
    down = lax.broadcasted_iota(jnp.int32, (LANES, LANES), 0)
    along = lax.broadcasted_iota(jnp.int32, (LANES, LANES), 1)
    return wide, tall, down < along, along < down


def mark_kernel(ids_ref, marked_ref):
    wide, tall, row_first, _ = both_ways(ids_ref[...])
    repeated = jnp.max(jnp.where((wide == tall) & row_first, REPEATED, 0), axis=0, keepdims=True)
    marked_ref[...] = jnp.broadcast_to((wide[:1] + repeated)[None], marked_ref.shape)


def one_hot(condition):
    return jnp.where(condition, 1.0, 0.0).astype(jnp.bfloat16)


def chip_ranks(ids_row, vocab_section):
    wide, tall, row_first, column_first = both_ways(ids_row)
    wide = wide // (2 * vocab_section)
    tall = tall // (2 * vocab_section)
    same = wide == tall
    as_row = jnp.sum(jnp.where(same & row_first, 1, 0), axis=0, keepdims=True)
    as_column = jnp.sum(jnp.where(same & column_first, 1.0, 0.0), axis=1, keepdims=True)
    return wide[:1], as_row, tall[:, :1], as_column.astype(jnp.int32)


def hand_kernel(section_ref, ids_ref, cotangent_ref, *refs, vocab_section):
    *hand_refs, expand_ref, combine_ref = refs
    token_slots, row_slots = expand_ref.shape
    section = section_ref[0]
    wide_chip, wide_rank, _, _ = chip_ranks(ids_ref[...], vocab_section)
    slot = lax.broadcasted_iota(jnp.int32, (token_slots, LANES), 0)
    cotangent = cotangent_ref[...]
    for k, hand_ref in enumerate(hand_refs):
        wanted = one_hot((slot == wide_rank) & (wide_chip == (section // 2) ^ k))
        hand_ref[...] = jnp.dot(
            wanted, cotangent, preferred_element_type=jnp.float32
        ).astype(jnp.bfloat16)

    wide, tall, row_first, column_first = both_ways(ids_ref[...])
    wide_in = wide // vocab_section == section
    tall_in = tall // vocab_section == section
    same = wide == tall
    wide_repeat = jnp.max(jnp.where(same & row_first, 1, 0), axis=0, keepdims=True)
    tall_repeat = jnp.max(jnp.where(same & column_first, 1.0, 0.0), axis=1, keepdims=True)
    wide_new = wide_in & (jnp.broadcast_to(wide_repeat, (LANES, LANES)) == 0)
    tall_new = tall_in & (jnp.broadcast_to(tall_repeat, (LANES, LANES)) == 0.0)
    own = one_hot((slot == wide_rank) & wide_in[:1])
    tall_place = jnp.sum(jnp.where(wide_new & column_first, 1.0, 0.0), axis=1, keepdims=True)
    place = jnp.sum(
        jnp.where(same & tall_new, jnp.broadcast_to(tall_place, (LANES, LANES)), 0.0), axis=0, keepdims=True
    ).astype(jnp.int32)
    place = jnp.where(wide_in[:1], place, -1)
    rows = one_hot(lax.broadcasted_iota(jnp.int32, (row_slots, LANES), 0) == place)
    over_tokens = (((1,), (1,)), ((), ()))
    expand_ref[...] = lax.dot_general(
        own, rows, over_tokens, preferred_element_type=jnp.float32
    ).astype(jnp.bfloat16)
    combine_ref[...] = lax.dot_general(
        rows, own, over_tokens, preferred_element_type=jnp.float32
    ).astype(jnp.bfloat16)


def stack_kernel(*refs):
    *part_refs, stack_ref = refs
    for k, part_ref in enumerate(part_refs):
        stack_ref[k] = part_ref[...]


def grad_kernel(section_ref, rows_ref, gain_ref, expand_ref, got_ref, *refs):
    *hand_refs, keep_ref, give_ref, embedded_ref = refs
    pieces, _, columns = rows_ref.shape
    chips, slots, features = got_ref.shape
    per = features // columns
    width = pieces * columns
    expand = expand_ref[...]
    section = section_ref[0]
    core = section % 2
    parts = []
    for k in range(chips):
        chip = (section // 2) ^ k
        parts.append((2 * chip + core, hand_refs[k], keep_ref.at[k]))
        parts.append((2 * chip + 1 - core, got_ref.at[k], give_ref.at[k]))

    squares = jnp.zeros((slots, columns), jnp.float32)
    inners = jnp.zeros((slots, columns), jnp.float32)
    for i, (s, cotangent_ref, _) in enumerate(parts):
        rows = jnp.concatenate([rows_ref[s * per + j] for j in range(per)], axis=1)
        embedded = jnp.dot(expand, rows, preferred_element_type=jnp.float32)
        embedded_ref[i] = embedded.astype(jnp.bfloat16)
        scaled = cotangent_ref[...].astype(jnp.float32) * gain_ref[pl.ds(s, 1), :]
        square = embedded * embedded
        inner = scaled * embedded
        for j in range(per):
            squares = squares + square[:, j * columns : (j + 1) * columns]
            inners = inners + inner[:, j * columns : (j + 1) * columns]
    square_mean = jnp.sum(squares, axis=1, keepdims=True) * (1.0 / width)
    inner = jnp.sum(inners, axis=1, keepdims=True) * (1.0 / width)
    own = jnp.sum(expand.astype(jnp.float32), axis=1, keepdims=True)
    inverse = jnp.where(own > 0.0, lax.rsqrt(square_mean + epsilon), 0.0)
    pull = inverse * inverse * inverse * inner

    for i, (s, cotangent_ref, out_ref) in enumerate(parts):
        scaled = cotangent_ref[...].astype(jnp.float32) * gain_ref[pl.ds(s, 1), :]
        out_ref[...] = (inverse * scaled - embedded_ref[i].astype(jnp.float32) * pull).astype(jnp.bfloat16)


def combine_kernel(section_ref, combine_ref, keep_ref, give_ref, by_column_ref):
    columns = by_column_ref.shape[2]
    chips, _, features = keep_ref.shape
    per = features // columns
    combine = combine_ref[...]
    section = section_ref[0]
    core = section % 2
    for k in range(chips):
        chip = (section // 2) ^ k
        for s, grad_ref in ((2 * chip + core, keep_ref), (2 * chip + 1 - core, give_ref)):
            added = jnp.dot(combine, grad_ref[k], preferred_element_type=jnp.float32).astype(jnp.bfloat16)
            for j in range(per):
                by_column_ref[s * per + j] = added[:, j * columns : (j + 1) * columns]


def merge_kernel(keep_ref, got_ref, *out_refs):
    for k, out_ref in enumerate(out_refs):
        out_ref[...] = (keep_ref[k].astype(jnp.float32) + got_ref[k].astype(jnp.float32)).astype(jnp.bfloat16)


def gather_kernel(section_ref, ids_ref, *refs, vocab_section):
    *home_refs, own_ref = refs
    slots = home_refs[0].shape[0]
    _, _, tall_chip, tall_rank = chip_ranks(ids_ref[...], vocab_section)
    along = lax.broadcasted_iota(jnp.int32, (LANES, slots), 1)
    total = jnp.zeros(own_ref.shape, jnp.float32)
    for k, home_ref in enumerate(home_refs):
        wanted = one_hot((along == tall_rank) & (tall_chip == (section_ref[0] // 2) ^ k))
        total = total + jnp.dot(wanted, home_ref[...], preferred_element_type=jnp.float32)
    own_ref[...] = total.astype(jnp.bfloat16)


def settle_kernel(fits_ref, fast_ref, slow_ref, out_ref, semaphore):
    @pl.when(fits_ref[0] == 0)
    def _():
        copy = pltpu.make_async_copy(slow_ref, out_ref, semaphore)
        copy.start()
        copy.wait()


def in_order(own, travelled):
    return [own[0]] + [travelled[FAR_FIRST.index(k)] for k in range(1, len(own))]


def on_device(token_ids, embed_table, norm_gain, cotangent):
    vocab_section, columns = embed_table.shape
    groups = lax.axis_size("dp")
    sections = lax.axis_size(SECTION)
    tokens, features = cotangent.shape
    V, S = pltpu.VMEM, pltpu.SMEM
    bf16 = functools.partial(jax.ShapeDtypeStruct, dtype=jnp.bfloat16)
    f32 = pltpu.VMEM
    i32 = functools.partial(jax.ShapeDtypeStruct, dtype=jnp.int32)
    section = lax.axis_index(SECTION).reshape(1)
    own_ids = token_ids.reshape(1, tokens)
    (marked,) = call(mark_kernel, (own_ids,), (V,), [i32((groups, 1, tokens))])
    marked = lax.all_to_all(marked, "dp", 0, 0, tiled=True)
    chips = sections // 2
    part = bf16((TOKEN_SLOTS, features))
    parts = bf16((chips, TOKEN_SLOTS, features))

    def to_chip(k, array):
        return lax.ppermute(array, CHIPS, [(i, i ^ k) for i in range(chips)])

    def to_sibling(array):
        return lax.ppermute(array, CORES, [(0, 1), (1, 0)])

    *hands, expand, combine = call(
        functools.partial(hand_kernel, vocab_section=vocab_section),
        (section, own_ids, cotangent), (S, V, V),
        [part] * chips + [bf16((TOKEN_SLOTS, ROW_SLOTS)), bf16((ROW_SLOTS, TOKEN_SLOTS))],
    )
    handed = [to_chip(k, hands[k]) for k in FAR_FIRST]
    marked, handed[:EARLY] = lax.optimization_barrier((marked, handed[:EARLY]))
    handed = in_order(hands, handed)
    marked = marked.reshape(groups, tokens)
    wide_shape = (vocab_section + CHUNK, columns)
    wide_slots = f32((ROW_SLOTS, columns), jnp.float32)
    plan_shape = (ROW_SLOTS + CHUNK, LANES)
    rows, plan, over = call(
        functools.partial(row_pick_kernel, vocab_section=vocab_section),
        (section, marked, embed_table), (S, V, pltpu.HBM),
        [bf16((groups, ROW_SLOTS, columns)), i32(plan_shape), i32((8, LANES))],
        [f32(embed_table.shape, jnp.bfloat16), f32(wide_shape, jnp.float32), wide_slots],
        [pltpu.SMEM(plan_shape, jnp.int32), pltpu.SemaphoreType.DMA((4,)), pltpu.SemaphoreType.DMA],
    )
    full_rows = lax.all_to_all(rows, "dp", 0, 0, tiled=True)
    (stack,) = call(stack_kernel, tuple(handed), (V,) * chips, [parts])
    got = to_sibling(stack)
    keep, give = call(
        grad_kernel,
        (section, full_rows, norm_gain.reshape(sections, features), expand, got, *handed),
        (S,) + (V,) * (4 + chips), [parts, parts],
        [f32((sections, TOKEN_SLOTS, features), jnp.bfloat16)],
    )
    (by_column,) = call(
        combine_kernel, (section, combine, keep, give), (S, V, V, V), [bf16(full_rows.shape)]
    )
    outs = call(merge_kernel, (keep, to_sibling(give)), (V, V), [part] * chips)
    by_column, outs = lax.optimization_barrier((by_column, list(outs)))
    home = [to_chip(k, outs[k]) for k in FAR_FIRST]
    back = lax.all_to_all(by_column, "dp", 0, 0, tiled=True)

    def fast(plan, back, *_):
        (grad_table,) = call(
            row_add_kernel, (plan, back), (S, V),
            [bf16((vocab_section, columns))], [f32(wide_shape, jnp.float32), wide_slots],
        )
        return grad_table, jnp.zeros((tokens, features), jnp.bfloat16)

    def slow(plan, back, section, marked, *operands):
        return passage(tokens, section, marked % REPEATED, *operands)

    fits = jnp.max(over[:1]) <= 0

    grad_table, slow_grad = lax.cond(
        fits, fast, slow, plan, back,
        section, marked, own_ids, embed_table, norm_gain, cotangent,
    )
    grad_table, slow_grad, home = lax.optimization_barrier((grad_table, slow_grad, home))
    (fast_grad,) = call(
        functools.partial(gather_kernel, vocab_section=vocab_section),
        (section, own_ids, *in_order(outs, home)), (S,) + (V,) * (1 + chips), [bf16((tokens, features))],
    )
    anywhere = pl.BlockSpec(memory_space=pl.ANY)
    own_grad = pl.pallas_call(
        settle_kernel,
        in_specs=[whole((1,), S), anywhere, anywhere],
        out_specs=anywhere,
        out_shape=bf16((tokens, features)),
        scratch_shapes=[pltpu.SemaphoreType.DMA],
        input_output_aliases={1: 0},
    )(fits.astype(jnp.int32).reshape(1), fast_grad, slow_grad)
    return grad_table, own_grad


def solution(mesh):
    split = Mesh(mesh.devices.reshape(-1, 2, mesh.shape["dp"]), (CHIPS, CORES, "dp"))
    return jax.shard_map(
        on_device,
        mesh=split,
        in_specs=(P("dp"), P(SECTION, "dp"), P(), P("dp", SECTION)),
        out_specs=(P(SECTION, "dp"), P("dp", SECTION)),
        check_vma=False,
    )
```

```python
import functools
import math

import jax
import jax.numpy as jnp
from jax import lax
from jax.experimental import pallas as pl
from jax.experimental.pallas import tpu as pltpu
from jax.sharding import Mesh
from jax.sharding import PartitionSpec as P

epsilon = 1e-05
TOKEN_SLOTS = 72
ROW_SLOTS = 32
CHUNK = 8
ALWAYS = 2
FAR_FIRST = (2, 1, 3)
EARLY = 2
REPEATED = 1 << 16
CHIPS = "section_0"
CORES = "section_1"
SECTION = (CHIPS, CORES)
LANES = 128


def whole(shape, space=pltpu.VMEM):
    if space == pltpu.HBM:
        return pl.BlockSpec(memory_space=space)
    return pl.BlockSpec(shape, lambda *_: (0,) * len(shape), memory_space=space)


def plan_kernel(section_ref, ids_ref, index_ref, count_ref, *, slots, vocab_section):
    ids = ids_ref[...].astype(jnp.float32)
    ids = jnp.concatenate([ids, ids], axis=0)
    ids = ids.T.astype(jnp.int32)
    local = ids - section_ref[0] * vocab_section
    inside = (local >= 0) & (local < vocab_section)
    before = (
        lax.broadcasted_iota(jnp.int32, (LANES, LANES), 1)
        < lax.broadcasted_iota(jnp.int32, (LANES, LANES), 0)
    )
    ones = jnp.where(inside, 1.0, 0.0)
    rank = jnp.dot(
        jnp.where(before, 1.0, 0.0).astype(jnp.bfloat16),
        ones.astype(jnp.bfloat16),
        preferred_element_type=jnp.float32,
    ).astype(jnp.int32)
    rank = jnp.where(inside, rank, -1)
    for c in range(slots):
        index_ref[pl.ds(c, 1), :] = jnp.sum(jnp.where(rank == c, local, 0), axis=0, keepdims=True)
    count_ref[...] = jnp.broadcast_to(
        jnp.sum(ones, axis=0, keepdims=True).astype(jnp.int32), count_ref.shape
    )


def pick_kernel(index_ref, table_ref, rows_ref, wide_ref, picked_ref, *, slots, groups):
    step = 256

    def widen(i, carry):
        wide_ref[pl.ds(i * step, step), :] = table_ref[pl.ds(i * step, step), :].astype(jnp.float32)
        return carry

    lax.fori_loop(0, table_ref.shape[0] // step, widen, 0)

    def group(g, carry):
        for c in range(slots):
            picked_ref[pl.ds(c, 1), :] = wide_ref[pl.ds(index_ref[c, g], 1), :]
        rows_ref[g] = picked_ref[...].astype(jnp.bfloat16)
        return carry

    lax.fori_loop(0, groups, group, 0)


def slot_of(ids_row, slots, vocab_section):
    wide = jnp.broadcast_to(ids_row // vocab_section, (LANES, LANES))
    tall = wide.astype(jnp.float32).T.astype(jnp.int32)
    first = lax.broadcasted_iota(jnp.int32, (LANES, LANES), 0)
    second = lax.broadcasted_iota(jnp.int32, (LANES, LANES), 1)
    same = wide == tall
    as_row = jnp.sum(jnp.where(same & (first < second), 1, 0), axis=0, keepdims=True)
    as_column = jnp.sum(jnp.where(same & (second < first), 1.0, 0.0), axis=1, keepdims=True)
    row_slot = jnp.where(as_row < slots, wide[:1] * slots + as_row, -1)
    as_column = as_column.astype(jnp.int32)
    column_slot = jnp.where(as_column < slots, tall[:, :1] * slots + as_column, -1)
    return row_slot, column_slot


def deal_kernel(ids_ref, cotangent_ref, dealt_ref, *, slots, sections, vocab_section):
    row_slot, _ = slot_of(ids_ref[...], slots, vocab_section)
    cotangent = cotangent_ref[...]
    for s in range(sections):
        wanted = lax.broadcasted_iota(jnp.int32, (slots, LANES), 0) + s * slots == row_slot
        dealt_ref[s] = jnp.dot(
            jnp.where(wanted, 1.0, 0.0).astype(jnp.bfloat16),
            cotangent,
            preferred_element_type=jnp.float32,
        ).astype(jnp.bfloat16)


def collect_kernel(ids_ref, dealt_ref, own_ref, *, slots, sections, vocab_section):
    _, column_slot = slot_of(ids_ref[...], slots, vocab_section)
    total = jnp.zeros(own_ref.shape, jnp.float32)
    for s in range(sections):
        wanted = lax.broadcasted_iota(jnp.int32, (LANES, slots), 1) + s * slots == column_slot
        total = total + jnp.dot(
            jnp.where(wanted, 1.0, 0.0).astype(jnp.bfloat16),
            dealt_ref[s],
            preferred_element_type=jnp.float32,
        )
    own_ref[...] = total.astype(jnp.bfloat16)


def norm_kernel(rows_ref, cotangent_ref, gain_ref, by_column_ref, by_feature_ref):
    pieces, slots, columns = rows_ref.shape
    per = cotangent_ref.shape[2] // columns
    width = pieces * columns

    def parts(k, j):
        embedded = rows_ref[k * per + j].astype(jnp.float32)
        own = cotangent_ref[k, :, j * columns : (j + 1) * columns].astype(jnp.float32)
        return embedded, own * gain_ref[pl.ds(k * per + j, 1), :]

    def sums(k, carry):
        squares, inners = carry
        for j in range(per):
            embedded, scaled = parts(k, j)
            squares = squares + embedded * embedded
            inners = inners + scaled * embedded
        return squares, inners

    zeros = jnp.zeros((slots, columns), jnp.float32)
    squares, inners = lax.fori_loop(0, pieces // per, sums, (zeros, zeros))
    square_mean = jnp.sum(squares, axis=1, keepdims=True) * (1.0 / width)
    inner = jnp.sum(inners, axis=1, keepdims=True) * (1.0 / width)
    inverse = lax.rsqrt(square_mean + epsilon)
    pull = inverse * inverse * inverse * inner

    def grads(k, carry):
        for j in range(per):
            embedded, scaled = parts(k, j)
            grad = (inverse * scaled - embedded * pull).astype(jnp.bfloat16)
            by_column_ref[k * per + j] = grad
            by_feature_ref[k, :, j * columns : (j + 1) * columns] = grad
        return carry

    lax.fori_loop(0, pieces // per, grads, 0)


def add_kernel(index_ref, count_ref, grads_ref, table_ref, total_ref, wide_ref, *, groups):
    step = 256
    slots = grads_ref.shape[1]

    def clear(i, carry):
        total_ref[pl.ds(i * step, step), :] = jnp.zeros((step, LANES), jnp.float32)
        return carry

    lax.fori_loop(0, total_ref.shape[0] // step, clear, 0)

    def group(g, carry):
        wide_ref[...] = grads_ref[g].astype(jnp.float32)

        def one(c, carry):
            row = pl.ds(index_ref[c, g], 1)
            total_ref[row, :] = total_ref[row, :] + wide_ref[pl.ds(c, 1), :]
            return carry

        lax.fori_loop(0, jnp.minimum(count_ref[0, g], slots), one, 0)
        return carry

    lax.fori_loop(0, groups, group, 0)

    def narrow(i, carry):
        table_ref[pl.ds(i * step, step), :] = total_ref[pl.ds(i * step, step), :].astype(jnp.bfloat16)
        return carry

    lax.fori_loop(0, total_ref.shape[0] // step, narrow, 0)


def call(kernel, operands, spaces, outs, scratch=(), semaphores=(), room=6):
    held = sum(math.prod(a.shape) * a.dtype.itemsize for a in (*operands, *outs, *scratch))
    return pl.pallas_call(
        kernel,
        in_specs=[whole(o.shape, s) for o, s in zip(operands, spaces)],
        out_specs=[whole(o.shape) for o in outs],
        out_shape=outs,
        scratch_shapes=[*scratch, *semaphores],
        compiler_params=pltpu.CompilerParams(vmem_limit_bytes=2 * held + (room << 20)),
    )(*operands)


def passage(slots, section, all_ids, own_ids, embed_table, norm_gain, cotangent):
    vocab_section, columns = embed_table.shape
    groups = all_ids.shape[0]
    tokens, features = cotangent.shape
    sections = lax.axis_size(SECTION)
    V, S = pltpu.VMEM, pltpu.SMEM
    bf16 = functools.partial(jax.ShapeDtypeStruct, dtype=jnp.bfloat16)
    i32 = functools.partial(jax.ShapeDtypeStruct, dtype=jnp.int32)
    (dealt,) = call(
        functools.partial(deal_kernel, slots=slots, sections=sections, vocab_section=vocab_section),
        (own_ids, cotangent), (V, V), [bf16((sections, slots, features))],
    )
    their_cotangent = lax.all_to_all(dealt, SECTION, 0, 0, tiled=True)
    index, count = call(
        functools.partial(plan_kernel, slots=slots, vocab_section=vocab_section),
        (section, all_ids), (S, V), [i32((slots, LANES)), i32((8, LANES))],
    )
    (rows,) = call(
        functools.partial(pick_kernel, slots=slots, groups=groups),
        (index, embed_table), (S, V), [bf16((groups, slots, columns))],
        [pltpu.VMEM((vocab_section, columns), jnp.float32), pltpu.VMEM((slots, columns), jnp.float32)],
    )
    full_rows = lax.all_to_all(rows, "dp", 0, 0, tiled=True)
    gain = norm_gain.reshape(groups, columns)
    by_column, by_feature = call(
        norm_kernel, (full_rows, their_cotangent, gain), (V, V, V),
        [bf16(full_rows.shape), bf16(their_cotangent.shape)],
    )
    back = lax.all_to_all(by_column, "dp", 0, 0, tiled=True)
    home = lax.all_to_all(by_feature, SECTION, 0, 0, tiled=True)
    (grad_table,) = call(
        functools.partial(add_kernel, groups=groups),
        (index, count, back), (S, S, V), [bf16((vocab_section, columns))],
        [pltpu.VMEM((vocab_section, columns), jnp.float32), pltpu.VMEM((slots, columns), jnp.float32)],
    )
    (own_grad,) = call(
        functools.partial(collect_kernel, slots=slots, sections=sections, vocab_section=vocab_section),
        (own_ids, home), (V, V), [bf16((tokens, features))],
    )
    return grad_table, own_grad


def row_plan(section, ids, plan_ref, over_ref, vocab_section):
    slots = plan_ref.shape[0] - CHUNK
    sections = 1 + (REPEATED - 1) // vocab_section
    ids = ids.astype(jnp.float32)
    ids = jnp.concatenate([ids, ids], axis=0)
    ids = ids.T.astype(jnp.int32)
    home = (ids % REPEATED) // vocab_section
    over = jnp.full((1, LANES), -1, jnp.int32)
    for s in range(sections):
        new = jnp.where((home == s) & (ids < REPEATED), 1, 0)
        over = jnp.maximum(over, jnp.sum(new, axis=0, keepdims=True) - slots)
    for s in range(0, sections, 2):
        here = jnp.where(home // 2 == s // 2, 1, 0)
        over = jnp.maximum(over, jnp.sum(here, axis=0, keepdims=True) - TOKEN_SLOTS)
    over_ref[...] = jnp.broadcast_to(over, over_ref.shape)
    local = ids - section * vocab_section
    inside = (local >= 0) & (local < vocab_section) & (ids < REPEATED)
    before = (
        lax.broadcasted_iota(jnp.int32, (LANES, LANES), 1)
        < lax.broadcasted_iota(jnp.int32, (LANES, LANES), 0)
    )
    ones = jnp.where(inside, 1.0, 0.0)
    rank = jnp.dot(
        jnp.where(before, 1.0, 0.0).astype(jnp.bfloat16),
        ones.astype(jnp.bfloat16),
        preferred_element_type=jnp.float32,
    ).astype(jnp.int32)
    rank = jnp.where(inside, rank, -1)
    short = local - vocab_section
    for c in range(slots):
        plan_ref[pl.ds(c, 1), :] = vocab_section + jnp.sum(
            jnp.where(rank == c, short, 0), axis=0, keepdims=True
        )
    count = jnp.minimum(jnp.sum(ones, axis=0, keepdims=True).astype(jnp.int32), slots)
    plan_ref[pl.ds(slots, CHUNK), :] = jnp.broadcast_to((count + (CHUNK - 1)) // CHUNK, (CHUNK, LANES))


def row_pick_kernel(
    section_ref, ids_ref, table_ref, rows_ref, plan_ref, over_ref,
    held_ref, wide_ref, picked_ref, steps_ref, arrived, planned, *, vocab_section
):
    groups, slots, columns = rows_ref.shape
    entries = table_ref.shape[0]
    pieces = arrived.shape[0]
    piece = entries // pieces
    copies = [
        pltpu.make_async_copy(
            table_ref.at[pl.ds(i * piece, piece)], held_ref.at[pl.ds(i * piece, piece)], arrived.at[i]
        )
        for i in range(pieces)
    ]
    for copy in copies:
        copy.start()
    row_plan(section_ref[0], ids_ref[...], plan_ref, over_ref, vocab_section)
    plan_copy = pltpu.make_async_copy(plan_ref, steps_ref, planned)
    plan_copy.start()
    picked_ref[...] = jnp.zeros(picked_ref.shape, jnp.float32)
    wide_ref[pl.ds(entries, CHUNK), :] = jnp.zeros((CHUNK, columns), jnp.float32)
    step = 512

    for i, copy in enumerate(copies):
        copy.wait()

        def widen(j, carry):
            at = pl.ds(pl.multiple_of(i * piece + j * step, step), step)
            wide_ref[at, :] = held_ref[at, :].astype(jnp.float32)
            return carry

        lax.fori_loop(0, piece // step, widen, 0)
    plan_copy.wait()

    def group(g, carry):
        def copy_row(c):
            picked_ref[pl.ds(c, 1), :] = wide_ref[pl.ds(steps_ref[c, g], 1), :]

        def chunk(i, carry):
            for j in range(CHUNK):
                copy_row(i * CHUNK + j)
            return carry

        for c in range(ALWAYS * CHUNK):
            copy_row(c)
        lax.fori_loop(ALWAYS, steps_ref[slots, g], chunk, 0)
        rows_ref[g] = picked_ref[...].astype(jnp.bfloat16)
        return carry

    lax.fori_loop(0, groups, group, 0)


def row_add_kernel(plan_ref, grads_ref, table_ref, total_ref, wide_ref):
    groups, slots, columns = grads_ref.shape
    entries = table_ref.shape[0]
    step = 512

    def clear(i, carry):
        total_ref[pl.ds(i * step, step), :] = jnp.zeros((step, columns), jnp.float32)
        return carry

    lax.fori_loop(0, entries // step, clear, 0)
    total_ref[pl.ds(entries, CHUNK), :] = jnp.zeros((CHUNK, columns), jnp.float32)

    def group(g, carry):
        wide_ref[...] = grads_ref[g].astype(jnp.float32)

        def add_rows(slots_here):
            rows = [pl.ds(plan_ref[c, g], 1) for c in slots_here]
            sums = [total_ref[row, :] + wide_ref[pl.ds(c, 1), :] for c, row in zip(slots_here, rows)]
            for row, value in zip(rows, sums):
                total_ref[row, :] = value

        def chunk(i, carry):
            add_rows([i * CHUNK + j for j in range(CHUNK)])
            return carry

        add_rows(list(range(ALWAYS * CHUNK)))
        lax.fori_loop(ALWAYS, plan_ref[slots, g], chunk, 0)
        return carry

    lax.fori_loop(0, groups, group, 0)

    def narrow(i, carry):
        table_ref[pl.ds(i * step, step), :] = total_ref[pl.ds(i * step, step), :].astype(jnp.bfloat16)
        return carry

    lax.fori_loop(0, entries // step, narrow, 0)


def both_ways(ids_row):
    wide = jnp.broadcast_to(ids_row, (LANES, LANES))
    tall = wide.astype(jnp.float32).T.astype(jnp.int32)
    down = lax.broadcasted_iota(jnp.int32, (LANES, LANES), 0)
    along = lax.broadcasted_iota(jnp.int32, (LANES, LANES), 1)
    return wide, tall, down < along, along < down


def mark_kernel(ids_ref, marked_ref):
    wide, tall, row_first, _ = both_ways(ids_ref[...])
    repeated = jnp.max(jnp.where((wide == tall) & row_first, REPEATED, 0), axis=0, keepdims=True)
    marked_ref[...] = jnp.broadcast_to((wide[:1] + repeated)[None], marked_ref.shape)


def one_hot(condition):
    return jnp.where(condition, 1.0, 0.0).astype(jnp.bfloat16)


def chip_ranks(ids_row, vocab_section):
    wide, tall, row_first, column_first = both_ways(ids_row)
    wide = wide // (2 * vocab_section)
    tall = tall // (2 * vocab_section)
    same = wide == tall
    as_row = jnp.sum(jnp.where(same & row_first, 1, 0), axis=0, keepdims=True)
    as_column = jnp.sum(jnp.where(same & column_first, 1.0, 0.0), axis=1, keepdims=True)
    return wide[:1], as_row, tall[:, :1], as_column.astype(jnp.int32)


def hand_kernel(section_ref, ids_ref, cotangent_ref, *refs, vocab_section):
    *hand_refs, expand_ref, combine_ref = refs
    token_slots, row_slots = expand_ref.shape
    section = section_ref[0]
    wide_chip, wide_rank, _, _ = chip_ranks(ids_ref[...], vocab_section)
    slot = lax.broadcasted_iota(jnp.int32, (token_slots, LANES), 0)
    cotangent = cotangent_ref[...]
    for k, hand_ref in enumerate(hand_refs):
        wanted = one_hot((slot == wide_rank) & (wide_chip == (section // 2) ^ k))
        hand_ref[...] = jnp.dot(
            wanted, cotangent, preferred_element_type=jnp.float32
        ).astype(jnp.bfloat16)

    wide, tall, row_first, column_first = both_ways(ids_ref[...])
    wide_in = wide // vocab_section == section
    tall_in = tall // vocab_section == section
    same = wide == tall
    wide_repeat = jnp.max(jnp.where(same & row_first, 1, 0), axis=0, keepdims=True)
    tall_repeat = jnp.max(jnp.where(same & column_first, 1.0, 0.0), axis=1, keepdims=True)
    wide_new = wide_in & (jnp.broadcast_to(wide_repeat, (LANES, LANES)) == 0)
    tall_new = tall_in & (jnp.broadcast_to(tall_repeat, (LANES, LANES)) == 0.0)
    own = one_hot((slot == wide_rank) & wide_in[:1])
    tall_place = jnp.sum(jnp.where(wide_new & column_first, 1.0, 0.0), axis=1, keepdims=True)
    place = jnp.sum(
        jnp.where(same & tall_new, jnp.broadcast_to(tall_place, (LANES, LANES)), 0.0), axis=0, keepdims=True
    ).astype(jnp.int32)
    place = jnp.where(wide_in[:1], place, -1)
    rows = one_hot(lax.broadcasted_iota(jnp.int32, (row_slots, LANES), 0) == place)
    over_tokens = (((1,), (1,)), ((), ()))
    expand_ref[...] = lax.dot_general(
        own, rows, over_tokens, preferred_element_type=jnp.float32
    ).astype(jnp.bfloat16)
    combine_ref[...] = lax.dot_general(
        rows, own, over_tokens, preferred_element_type=jnp.float32
    ).astype(jnp.bfloat16)


def stack_kernel(*refs):
    *part_refs, stack_ref = refs
    for k, part_ref in enumerate(part_refs):
        stack_ref[k] = part_ref[...]


def grad_kernel(section_ref, rows_ref, gain_ref, expand_ref, got_ref, *refs):
    *hand_refs, keep_ref, give_ref, embedded_ref = refs
    pieces, _, columns = rows_ref.shape
    chips, slots, features = got_ref.shape
    per = features // columns
    width = pieces * columns
    expand = expand_ref[...]
    section = section_ref[0]
    core = section % 2
    parts = []
    for k in range(chips):
        chip = (section // 2) ^ k
        parts.append((2 * chip + core, hand_refs[k], keep_ref.at[k]))
        parts.append((2 * chip + 1 - core, got_ref.at[k], give_ref.at[k]))

    squares = jnp.zeros((slots, columns), jnp.float32)
    inners = jnp.zeros((slots, columns), jnp.float32)
    for i, (s, cotangent_ref, _) in enumerate(parts):
        rows = jnp.concatenate([rows_ref[s * per + j] for j in range(per)], axis=1)
        embedded = jnp.dot(expand, rows, preferred_element_type=jnp.float32)
        embedded_ref[i] = embedded.astype(jnp.bfloat16)
        scaled = cotangent_ref[...].astype(jnp.float32) * gain_ref[pl.ds(s, 1), :]
        square = embedded * embedded
        inner = scaled * embedded
        for j in range(per):
            squares = squares + square[:, j * columns : (j + 1) * columns]
            inners = inners + inner[:, j * columns : (j + 1) * columns]
    square_mean = jnp.sum(squares, axis=1, keepdims=True) * (1.0 / width)
    inner = jnp.sum(inners, axis=1, keepdims=True) * (1.0 / width)
    own = jnp.sum(expand.astype(jnp.float32), axis=1, keepdims=True)
    inverse = jnp.where(own > 0.0, lax.rsqrt(square_mean + epsilon), 0.0)
    pull = inverse * inverse * inverse * inner

    for i, (s, cotangent_ref, out_ref) in enumerate(parts):
        scaled = cotangent_ref[...].astype(jnp.float32) * gain_ref[pl.ds(s, 1), :]
        out_ref[...] = (inverse * scaled - embedded_ref[i].astype(jnp.float32) * pull).astype(jnp.bfloat16)


def combine_kernel(section_ref, combine_ref, keep_ref, give_ref, by_column_ref):
    columns = by_column_ref.shape[2]
    chips, _, features = keep_ref.shape
    per = features // columns
    combine = combine_ref[...]
    section = section_ref[0]
    core = section % 2
    for k in range(chips):
        chip = (section // 2) ^ k
        for s, grad_ref in ((2 * chip + core, keep_ref), (2 * chip + 1 - core, give_ref)):
            added = jnp.dot(combine, grad_ref[k], preferred_element_type=jnp.float32).astype(jnp.bfloat16)
            for j in range(per):
                by_column_ref[s * per + j] = added[:, j * columns : (j + 1) * columns]


def merge_kernel(keep_ref, got_ref, *out_refs):
    for k, out_ref in enumerate(out_refs):
        out_ref[...] = (keep_ref[k].astype(jnp.float32) + got_ref[k].astype(jnp.float32)).astype(jnp.bfloat16)


def gather_kernel(section_ref, ids_ref, *refs, vocab_section):
    *home_refs, own_ref = refs
    slots = home_refs[0].shape[0]
    _, _, tall_chip, tall_rank = chip_ranks(ids_ref[...], vocab_section)
    along = lax.broadcasted_iota(jnp.int32, (LANES, slots), 1)
    total = jnp.zeros(own_ref.shape, jnp.float32)
    for k, home_ref in enumerate(home_refs):
        wanted = one_hot((along == tall_rank) & (tall_chip == (section_ref[0] // 2) ^ k))
        total = total + jnp.dot(wanted, home_ref[...], preferred_element_type=jnp.float32)
    own_ref[...] = total.astype(jnp.bfloat16)


def settle_kernel(fits_ref, fast_ref, slow_ref, out_ref, semaphore):
    @pl.when(fits_ref[0] == 0)
    def _():
        copy = pltpu.make_async_copy(slow_ref, out_ref, semaphore)
        copy.start()
        copy.wait()


def in_order(own, travelled):
    return [own[0]] + [travelled[FAR_FIRST.index(k)] for k in range(1, len(own))]


def on_device(token_ids, embed_table, norm_gain, cotangent):
    vocab_section, columns = embed_table.shape
    groups = lax.axis_size("dp")
    sections = lax.axis_size(SECTION)
    tokens, features = cotangent.shape
    V, S = pltpu.VMEM, pltpu.SMEM
    bf16 = functools.partial(jax.ShapeDtypeStruct, dtype=jnp.bfloat16)
    f32 = pltpu.VMEM
    i32 = functools.partial(jax.ShapeDtypeStruct, dtype=jnp.int32)
    section = lax.axis_index(SECTION).reshape(1)
    own_ids = token_ids.reshape(1, tokens)
    (marked,) = call(mark_kernel, (own_ids,), (V,), [i32((groups, 1, tokens))])
    marked = lax.all_to_all(marked, "dp", 0, 0, tiled=True)
    chips = sections // 2
    part = bf16((TOKEN_SLOTS, features))
    parts = bf16((chips, TOKEN_SLOTS, features))

    def to_chip(k, array):
        return lax.ppermute(array, CHIPS, [(i, i ^ k) for i in range(chips)])

    def to_sibling(array):
        return lax.ppermute(array, CORES, [(0, 1), (1, 0)])

    *hands, expand, combine = call(
        functools.partial(hand_kernel, vocab_section=vocab_section),
        (section, own_ids, cotangent), (S, V, V),
        [part] * chips + [bf16((TOKEN_SLOTS, ROW_SLOTS)), bf16((ROW_SLOTS, TOKEN_SLOTS))],
    )
    handed = [to_chip(k, hands[k]) for k in FAR_FIRST]
    marked, handed[:EARLY] = lax.optimization_barrier((marked, handed[:EARLY]))
    handed = in_order(hands, handed)
    marked = marked.reshape(groups, tokens)
    wide_shape = (vocab_section + CHUNK, columns)
    wide_slots = f32((ROW_SLOTS, columns), jnp.float32)
    plan_shape = (ROW_SLOTS + CHUNK, LANES)
    rows, plan, over = call(
        functools.partial(row_pick_kernel, vocab_section=vocab_section),
        (section, marked, embed_table), (S, V, pltpu.HBM),
        [bf16((groups, ROW_SLOTS, columns)), i32(plan_shape), i32((8, LANES))],
        [f32(embed_table.shape, jnp.bfloat16), f32(wide_shape, jnp.float32), wide_slots],
        [pltpu.SMEM(plan_shape, jnp.int32), pltpu.SemaphoreType.DMA((4,)), pltpu.SemaphoreType.DMA],
    )
    full_rows = lax.all_to_all(rows, "dp", 0, 0, tiled=True)
    (stack,) = call(stack_kernel, tuple(handed), (V,) * chips, [parts])
    got = to_sibling(stack)
    keep, give = call(
        grad_kernel,
        (section, full_rows, norm_gain.reshape(sections, features), expand, got, *handed),
        (S,) + (V,) * (4 + chips), [parts, parts],
        [f32((sections, TOKEN_SLOTS, features), jnp.bfloat16)],
    )
    (by_column,) = call(
        combine_kernel, (section, combine, keep, give), (S, V, V, V), [bf16(full_rows.shape)]
    )
    outs = call(merge_kernel, (keep, to_sibling(give)), (V, V), [part] * chips)
    by_column, outs = lax.optimization_barrier((by_column, list(outs)))
    home = [to_chip(k, outs[k]) for k in FAR_FIRST]
    back = lax.all_to_all(by_column, "dp", 0, 0, tiled=True)

    def fast(plan, back, *_):
        (grad_table,) = call(
            row_add_kernel, (plan, back), (S, V),
            [bf16((vocab_section, columns))], [f32(wide_shape, jnp.float32), wide_slots],
        )
        return grad_table, jnp.zeros((tokens, features), jnp.bfloat16)

    def slow(plan, back, section, marked, *operands):
        return passage(tokens, section, marked % REPEATED, *operands)

    fits = jnp.max(over[:1]) <= 0

    grad_table, slow_grad = lax.cond(
        fits, fast, slow, plan, back,
        section, marked, own_ids, embed_table, norm_gain, cotangent,
    )
    grad_table, slow_grad, home = lax.optimization_barrier((grad_table, slow_grad, home))
    (fast_grad,) = call(
        functools.partial(gather_kernel, vocab_section=vocab_section),
        (section, own_ids, *in_order(outs, home)), (S,) + (V,) * (1 + chips), [bf16((tokens, features))],
    )
    anywhere = pl.BlockSpec(memory_space=pl.ANY)
    own_grad = pl.pallas_call(
        settle_kernel,
        in_specs=[whole((1,), S), anywhere, anywhere],
        out_specs=anywhere,
        out_shape=bf16((tokens, features)),
        scratch_shapes=[pltpu.SemaphoreType.DMA],
        input_output_aliases={1: 0},
    )(fits.astype(jnp.int32).reshape(1), fast_grad, slow_grad)
    return grad_table, own_grad


def solution(mesh):
    split = Mesh(mesh.devices.reshape(-1, 2, mesh.shape["dp"]), (CHIPS, CORES, "dp"))
    return jax.shard_map(
        on_device,
        mesh=split,
        in_specs=(P("dp"), P(SECTION, "dp"), P(), P("dp", SECTION)),
        out_specs=(P(SECTION, "dp"), P("dp", SECTION)),
        check_vma=False,
    )
```
